32 devices in a mesh: tmpl: 4 (over x, core), row: 4 (over z), col: 2 (over y).
Axes of the slice: x: 2, y: 2, z: 4, core: 2. Of those that a mesh axis runs over, the one named last changes fastest.
Arguments:
- templ_pair: bfloat16 [4, 256, 256, 64], P('tmpl', 'row', 'col'), may hold values from -10 to 10
- main_pair: bfloat16 [256, 256, 128], P('row', 'col'), may hold values from -8 to 8
- coverage: int32 [4, 2], replicated, may hold values from 0 to 1
- pair_mask: int32 [2, 2], replicated, may hold values from 0 to 1
- tri_gain: float32 [64], replicated, may hold values from 0.1 to 1.9
- w_project: bfloat16 [64, 256], replicated, may hold values from -1 to 1
- w_bias: bfloat16 [64, 4], replicated, may hold values from -0.75 to 0.75
- w_tri_out: bfloat16 [64, 64], replicated, may hold values from -0.75 to 0.75
- merge_gain: float32 [64], replicated, may hold values from 0.1 to 1.9
- w_merge_q: bfloat16 [128, 64], replicated, may hold values from -1 to 1
- w_merge_kv: bfloat16 [64, 128], replicated, may hold values from -1 to 1
- w_merge_out: bfloat16 [64, 128], replicated, may hold values from -0.75 to 0.75
Outputs:
- templ_out: bfloat16 [4, 256, 256, 64], P('tmpl', 'row', 'col')
- embedding: bfloat16 [256, 256, 128], P('row', 'col')
The draws below stay inside these ranges and needn't reach their ends.
All inputs are finite; a program needn't handle non-finite values.
Results may differ from the reference program's by a relative error of at most 0.015.
Values may be sent and summed in bfloat16 or wider, within the bound.
No kernel may reach another device: no remote copies, remote signals or barrier semaphores. Data moves between devices by JAX's collectives and lax.ppermute only.
A program may use at most 64 MiB of HBM per device.

```python
import jax
import jax.numpy as jnp
from jax import lax

TOKENS = 256
BLOCK = 128
TEMPL_CH = 64
PAIR_CH = 128
HEADS = 4
HEAD_DIM = 16
TEMPLATES = 4
NBLK = 2


def scaled_normal(key, tag, shape, fan_in):
    raw = jnp.clip(jax.random.normal(jax.random.fold_in(key, tag), shape, jnp.float32), -6.0, 6.0)
    return raw * fan_in ** (-0.5)


def draw_templ_pair(key, part):
    base = jnp.clip(jax.random.normal(jax.random.fold_in(key, 1), (TEMPLATES, TOKENS, TOKENS, TEMPL_CH), jnp.float32), -6.0, 6.0)
    return base.astype(jnp.bfloat16)


def draw_main_pair(key, part):
    base = jnp.clip(jax.random.normal(jax.random.fold_in(key, 2), (TOKENS, TOKENS, PAIR_CH), jnp.float32), -6.0, 6.0)
    return base.astype(jnp.bfloat16)


def draw_w_project(key, part):
    base = scaled_normal(key, 3, (TEMPL_CH, 4 * HEADS * HEAD_DIM), TEMPL_CH)
    return jnp.clip(base, -1.0, 1.0).astype(jnp.bfloat16)


def draw_w_merge_q(key, part):
    base = scaled_normal(key, 4, (PAIR_CH, HEADS * HEAD_DIM), PAIR_CH)
    return jnp.clip(base, -1.0, 1.0).astype(jnp.bfloat16)


def draw_w_merge_kv(key, part):
    base = scaled_normal(key, 5, (TEMPL_CH, 2 * HEADS * HEAD_DIM), TEMPL_CH)
    return jnp.clip(base, -1.0, 1.0).astype(jnp.bfloat16)


def place_ends(entries, stream_key, least, top_value):
    extent = entries.shape
    index_at = [jax.random.randint(jax.random.fold_in(stream_key, axis), (), 0, extent[axis]) for axis in range(len(extent))]
    entries = entries.at[tuple(index_at)].set(least)
    longest = extent.index(max(extent))
    index_at[longest] = (index_at[longest] + 1) % extent[longest]
    return entries.at[tuple(index_at)].set(top_value)


def bell_draw(stream_key, shape, scale, most, held_as=jnp.bfloat16):
    entries = jax.random.normal(stream_key, shape, jnp.float32) * scale
    return jnp.minimum(jnp.maximum(entries, -most), most).astype(held_as)


def setup_inputs(seed: int = 0) -> dict:
    streams_of = jax.random.split(jax.random.key(seed), 13)
    templ_pair = draw_templ_pair(jax.random.fold_in(streams_of[12], 71), 0)
    main_pair = draw_main_pair(jax.random.fold_in(streams_of[12], 71), 0)
    coverage = place_ends(jax.random.randint(streams_of[2], (TEMPLATES, NBLK), 0, 2), jax.random.fold_in(streams_of[2], 1), 0, 1).astype(jnp.int32)
    pair_mask = place_ends(jax.random.randint(streams_of[3], (NBLK, NBLK), 0, 2), jax.random.fold_in(streams_of[3], 1), 0, 1).astype(jnp.int32)
    tri_gain = jnp.clip(1.0 + 0.18 * jax.random.normal(streams_of[4], (TEMPL_CH,), jnp.float32), 0.1, 1.9)
    w_project = draw_w_project(jax.random.fold_in(streams_of[12], 71), 0)
    w_bias = bell_draw(streams_of[6], (TEMPL_CH, HEADS), TEMPL_CH ** -0.5, 0.75)
    w_tri_out = bell_draw(streams_of[7], (HEADS * HEAD_DIM, TEMPL_CH), (HEADS * HEAD_DIM) ** -0.5, 0.75)
    merge_gain = jnp.clip(1.0 + 0.18 * jax.random.normal(streams_of[8], (TEMPL_CH,), jnp.float32), 0.1, 1.9)
    w_merge_q = draw_w_merge_q(jax.random.fold_in(streams_of[12], 71), 0)
    w_merge_kv = draw_w_merge_kv(jax.random.fold_in(streams_of[12], 71), 0)
    w_merge_out = bell_draw(streams_of[11], (HEADS * HEAD_DIM, PAIR_CH), (HEADS * HEAD_DIM) ** -0.5, 0.75)
    return {"templ_pair": templ_pair, "main_pair": main_pair, "coverage": coverage, "pair_mask": pair_mask, "tri_gain": tri_gain, "w_project": w_project, "w_bias": w_bias, "w_tri_out": w_tri_out, "merge_gain": merge_gain, "w_merge_q": w_merge_q, "w_merge_kv": w_merge_kv, "w_merge_out": w_merge_out}


MASK_SHIFT = 10000.0
EPSILON = 1e-05

def layer_norm(values, scale_gain):
    values = values.astype(jnp.float32)
    center = values - lax.optimization_barrier(jnp.mean(values, axis=-1, keepdims=True))
    spread = lax.optimization_barrier(jnp.mean(center * center, axis=-1, keepdims=True))
    return center * lax.rsqrt(spread + EPSILON) * scale_gain

def reference(templ_pair, main_pair, coverage, pair_mask, tri_gain, w_project, w_bias, w_tri_out, merge_gain, w_merge_q, w_merge_kv, w_merge_out):
    hidden = HEADS * HEAD_DIM
    score_scale = HEAD_DIM ** (-0.5)
    channels = templ_pair.shape[-1]
    cover_tok = jnp.repeat(coverage, BLOCK, axis=1)
    pair_tok = jnp.repeat(jnp.repeat(pair_mask, BLOCK, axis=0), BLOCK, axis=1)
    valid_mask = cover_tok[:, :, None] * cover_tok[:, None, :] * pair_tok[None]
    shift_bias = MASK_SHIFT * (valid_mask.astype(jnp.float32) - 1.0)
    updated = []
    merge_rows = []
    for template in range(TEMPLATES):
        pair_tile = templ_pair[template]
        normed = layer_norm(pair_tile, tri_gain).astype(jnp.bfloat16)
        flat_norm = normed.reshape(-1, channels)
        project = jnp.dot(flat_norm, w_project, preferred_element_type=jnp.float32).reshape(TOKENS, TOKENS, 4 * hidden)
        queries = (project[..., :hidden] * score_scale).astype(jnp.bfloat16).reshape(TOKENS, TOKENS, HEADS, HEAD_DIM)
        keys_all = project[..., hidden:2 * hidden].astype(jnp.bfloat16).reshape(TOKENS, TOKENS, HEADS, HEAD_DIM)
        values_all = project[..., 2 * hidden:3 * hidden].astype(jnp.bfloat16).reshape(TOKENS, TOKENS, HEADS, HEAD_DIM)
        gate_values = jax.nn.sigmoid(project[..., 3 * hidden:])
        pair_bias = jnp.dot(flat_norm, w_bias, preferred_element_type=jnp.float32).astype(jnp.bfloat16)
        bias_head = jnp.transpose(pair_bias.reshape(TOKENS, TOKENS, HEADS), (0, 2, 1)).astype(jnp.float32)

        def one_row(row_args):
            query_row, key_row, value_row, shift_row = row_args
            scores = jnp.einsum('jhd,khd->jhk', query_row.astype(jnp.float32), key_row.astype(jnp.float32))
            scores = scores + bias_head + shift_row[None, None, :]
            highest = lax.optimization_barrier(jnp.max(scores, axis=-1, keepdims=True))
            weights = jnp.exp(scores - highest)
            totals = lax.optimization_barrier(jnp.sum(weights, axis=-1))
            rounded = weights.astype(jnp.bfloat16).astype(jnp.float32)
            summed = jnp.einsum('jhk,khd->jhd', rounded, value_row.astype(jnp.float32))
            return summed / totals[..., None]
        attended = lax.map(one_row, (queries, keys_all, values_all, shift_bias[template]))
        gated = (attended.reshape(TOKENS, TOKENS, hidden) * gate_values).astype(jnp.bfloat16)
        projected = jnp.dot(gated.reshape(-1, hidden), w_tri_out, preferred_element_type=jnp.float32).reshape(TOKENS, TOKENS, channels)
        new_pair = (pair_tile.astype(jnp.float32) + projected).astype(jnp.bfloat16)
        updated.append(new_pair)
        merge_norm = layer_norm(new_pair, merge_gain).astype(jnp.bfloat16)
        key_value = jnp.dot(merge_norm.reshape(-1, channels), w_merge_kv, preferred_element_type=jnp.float32).astype(jnp.bfloat16)
        merge_rows.append(key_value.reshape(TOKENS, TOKENS, 2 * hidden))
    merge_kv = jnp.stack(merge_rows)
    pair_ch = main_pair.shape[-1]
    main_query = (jnp.dot(main_pair.reshape(-1, pair_ch), w_merge_q, preferred_element_type=jnp.float32) * score_scale).reshape(TOKENS, TOKENS, HEADS, HEAD_DIM)
    merge_keys = merge_kv[..., :hidden].astype(jnp.float32).reshape(TEMPLATES, TOKENS, TOKENS, HEADS, HEAD_DIM)
    merge_values = merge_kv[..., hidden:].astype(jnp.float32).reshape(TEMPLATES, TOKENS, TOKENS, HEADS, HEAD_DIM)
    merge_scores = jnp.einsum('ijhd,tijhd->tijh', main_query, merge_keys) + shift_bias[..., None]
    highest = lax.optimization_barrier(jnp.max(merge_scores, axis=0, keepdims=True))
    weights = jnp.exp(merge_scores - highest)
    totals = lax.optimization_barrier(jnp.sum(weights, axis=0))
    merged = jnp.einsum('tijh,tijhd->ijhd', weights, merge_values) / totals[..., None]
    merged = merged.reshape(-1, hidden).astype(jnp.bfloat16)
    embedding = jnp.dot(merged, w_merge_out, preferred_element_type=jnp.float32).astype(jnp.bfloat16).reshape(TOKENS, TOKENS, pair_ch)
    return (jnp.stack(updated), embedding)
```

```python
import functools

import jax
import jax.numpy as jnp
from jax import lax
from jax.experimental import pallas as pl
from jax.experimental.pallas import tpu as pltpu
from jax.sharding import PartitionSpec as P

BLOCK = 128


MASK_SHIFT = 10000.0
EPSILON = 1e-05
NEG_START = -1e30


def combined_all(part, axis, combine):
    gathered = jax.tree.map(lambda a: lax.all_gather(a, axis), part)

    def take(source):
        return jax.tree.map(lambda a: lax.dynamic_index_in_dim(a, source, 0, False), gathered)

    return lax.fori_loop(
        1, lax.axis_size(axis), lambda source, state: combine(state, take(source)), take(0)
    )


def layer_norm(values, scale_gain):
    values = values.astype(jnp.float32)
    center = values - jnp.mean(values, axis=-1, keepdims=True)
    spread = jnp.mean(center * center, axis=-1, keepdims=True)
    return center * lax.rsqrt(spread + EPSILON) * scale_gain


def row_group(rows_dev, cols_dev):
    chosen = 1
    for candidate in range(1, rows_dev + 1):
        if rows_dev % candidate == 0 and candidate * cols_dev <= 2048:
            chosen = candidate
    return chosen


def plain_on_device(
    templ_pair,
    main_pair,
    coverage,
    pair_mask,
    tri_gain,
    w_project,
    w_bias,
    w_tri_out,
    merge_gain,
    w_merge_q,
    w_merge_kv,
    w_merge_out,
):
    pair_tile = templ_pair[0]
    rows_dev, cols_dev, channels = pair_tile.shape
    hidden = w_tri_out.shape[0]
    head_count = w_bias.shape[1]
    head_dim = hidden // head_count
    score_scale = head_dim ** (-0.5)
    row_start = lax.axis_index("row") * rows_dev
    col_start = lax.axis_index("col") * cols_dev
    templ_index = lax.axis_index("tmpl")
    cover_tok = jnp.repeat(coverage, BLOCK, axis=1)
    own_cover = lax.dynamic_index_in_dim(cover_tok, templ_index, 0, keepdims=False)
    mask_full = jnp.repeat(jnp.repeat(pair_mask, BLOCK, axis=0), BLOCK, axis=1)
    mask_rows = lax.dynamic_slice_in_dim(mask_full, row_start, rows_dev, 0)
    cover_rows = lax.dynamic_slice_in_dim(own_cover, row_start, rows_dev, 0)
    normed = layer_norm(pair_tile, tri_gain).astype(jnp.bfloat16)
    flat_norm = normed.reshape(-1, channels)
    w_query_gate = jnp.concatenate([w_project[:, :hidden], w_project[:, 3 * hidden :]], axis=1)
    query_gate = jnp.dot(flat_norm, w_query_gate, preferred_element_type=jnp.float32).reshape(
        rows_dev, cols_dev, 2 * hidden
    )
    queries = (
        (query_gate[..., :hidden] * score_scale)
        .astype(jnp.bfloat16)
        .reshape(rows_dev, cols_dev, head_count, head_dim)
    )
    gate_values = jax.nn.sigmoid(query_gate[..., hidden:])
    bias_tile = jnp.dot(flat_norm, w_bias, preferred_element_type=jnp.float32).astype(jnp.bfloat16)
    bias_tile = jnp.transpose(bias_tile.reshape(rows_dev, cols_dev, head_count), (2, 0, 1))
    bias_column = lax.all_gather(bias_tile, "row", axis=1, tiled=True)
    bias_slab = lax.all_to_all(bias_column, "col", split_axis=1, concat_axis=2, tiled=True)
    bias_rows = jnp.transpose(bias_slab, (1, 0, 2)).astype(jnp.float32)
    key_shift = MASK_SHIFT * (
        (cover_rows[:, None] * own_cover[None, :] * mask_rows).astype(jnp.float32) - 1.0
    )
    w_key_value = w_project[:, hidden : 3 * hidden]
    group = row_group(rows_dev, cols_dev)
    splits = rows_dev // group

    def grouped(array):
        return array.reshape((splits, group) + array.shape[1:])

    start_state = (
        jnp.full((rows_dev, cols_dev, head_count), NEG_START, jnp.float32),
        jnp.zeros((rows_dev, cols_dev, head_count), jnp.float32),
        jnp.zeros((rows_dev, cols_dev, head_count, head_dim), jnp.float32),
    )
    norm_piece = lax.all_gather(normed, "col", axis=1, tiled=True)
    piece_width = norm_piece.shape[1]

    def one_group(group_args):
        query_part, norm_part, shift_part, maxima, totals, weighted = group_args
        key_value = jnp.dot(
            norm_part.reshape(-1, channels), w_key_value, preferred_element_type=jnp.float32
        ).astype(jnp.bfloat16)
        key_value = key_value.reshape(group, piece_width, 2 * hidden)
        key_part = key_value[..., :hidden].reshape(group, piece_width, head_count, head_dim)
        value_part = key_value[..., hidden:].reshape(group, piece_width, head_count, head_dim)
        scores = jnp.einsum(
            "ijhd,ikhd->ijhk", query_part, key_part, preferred_element_type=jnp.float32
        )
        scores = scores + bias_rows[None] + shift_part[:, None, None, :]
        highest = jnp.maximum(maxima, jnp.max(scores, axis=-1))
        rescale = jnp.exp(maxima - highest)
        weights = jnp.exp(scores - highest[..., None])
        totals = totals * rescale + jnp.sum(weights, axis=-1)
        summed = jnp.einsum(
            "ijhk,ikhd->ijhd",
            weights.astype(jnp.bfloat16),
            value_part,
            preferred_element_type=jnp.float32,
        )
        weighted = weighted * rescale[..., None] + summed
        return (highest, totals, weighted)

    outcome = lax.map(
        one_group,
        (
            grouped(queries),
            grouped(norm_piece),
            grouped(key_shift),
            grouped(start_state[0]),
            grouped(start_state[1]),
            grouped(start_state[2]),
        ),
    )
    result = tuple((member.reshape((rows_dev,) + member.shape[2:]) for member in outcome))
    attended = result[2] / result[1][..., None]
    gated = (attended.reshape(rows_dev, cols_dev, hidden) * gate_values).astype(jnp.bfloat16)
    projected = jnp.dot(
        gated.reshape(-1, hidden), w_tri_out, preferred_element_type=jnp.float32
    ).reshape(rows_dev, cols_dev, channels)
    new_pair = (pair_tile.astype(jnp.float32) + projected).astype(jnp.bfloat16)
    merge_norm = layer_norm(new_pair, merge_gain).astype(jnp.bfloat16)
    merge_kv = jnp.dot(
        merge_norm.reshape(-1, channels), w_merge_kv, preferred_element_type=jnp.float32
    ).astype(jnp.bfloat16)
    merge_kv = merge_kv.reshape(rows_dev, cols_dev, 2 * hidden)
    pair_ch = main_pair.shape[-1]
    main_query = (
        jnp.dot(main_pair.reshape(-1, pair_ch), w_merge_q, preferred_element_type=jnp.float32)
        * score_scale
    )
    main_query = main_query.reshape(rows_dev, cols_dev, head_count, head_dim)
    mask_tile = lax.dynamic_slice_in_dim(mask_rows, col_start, cols_dev, 1)
    own_cols = lax.dynamic_slice_in_dim(own_cover, col_start, cols_dev, 0)
    own_valid = cover_rows[:, None] * own_cols[None, :] * mask_tile
    shift_bias = MASK_SHIFT * (own_valid.astype(jnp.float32) - 1.0)
    keys_own = (
        merge_kv[..., :hidden].astype(jnp.float32).reshape(rows_dev, cols_dev, head_count, head_dim)
    )
    values_own = (
        merge_kv[..., hidden:].astype(jnp.float32).reshape(rows_dev, cols_dev, head_count, head_dim)
    )
    scores = jnp.sum(main_query * keys_own, axis=-1) + shift_bias[..., None]

    def combine(earlier, later):
        highest = jnp.maximum(earlier[0], later[0])
        early_scale = jnp.exp(earlier[0] - highest)
        late_scale = jnp.exp(later[0] - highest)
        return (
            highest,
            earlier[1] * early_scale + later[1] * late_scale,
            earlier[2] * early_scale[..., None] + later[2] * late_scale[..., None],
        )

    merged_state = combined_all((scores, jnp.ones_like(scores), values_own), "tmpl", combine)
    merged = merged_state[2] / merged_state[1][..., None]
    merged = merged.reshape(-1, hidden).astype(jnp.bfloat16)
    embedding = jnp.dot(merged, w_merge_out, preferred_element_type=jnp.float32).astype(
        jnp.bfloat16
    )
    return (new_pair[None], embedding.reshape(rows_dev, cols_dev, pair_ch))


LOG2E = 1.4426950408889634


def normed_rows(values, gain):
    center = values - jnp.mean(values, axis=0, keepdims=True)
    spread = jnp.mean(center * center, axis=0, keepdims=True)
    return (center * lax.rsqrt(spread + EPSILON) * gain).astype(jnp.bfloat16)


def piece_block(idx_ref, piece, pieces):
    half = idx_ref[0]
    side = half if piece % 2 else 1 - half
    return side * (pieces // 2) + piece // 2


def mask_shift(cover_ref, mask_ref, templ, row_block, col_block):
    valid = (
        cover_ref[templ, row_block] * cover_ref[templ, col_block] * mask_ref[row_block, col_block]
    )
    return MASK_SHIFT * (valid.astype(jnp.float32) - 1.0)


def matmul(lhs, rhs, lhs_dim=1, rhs_dim=0):
    return lax.dot_general(
        lhs, rhs, (((lhs_dim,), (rhs_dim,)), ((), ())), preferred_element_type=jnp.float32
    )


def norm_kernel(
    heads, idx_ref, x_ref, gain_ref, bias_w_ref, *refs
):
    piece = pl.program_id(0)
    *norm_refs, bias_ref, held = refs
    for chunk, norm_ref in enumerate(norm_refs):

        @pl.when(piece // 2 == chunk)
        def _():
            for i in range(x_ref.shape[0]):
                normed = normed_rows(x_ref[i].astype(jnp.float32), gain_ref[...])
                norm_ref[i] = normed
                row_bias = matmul(bias_w_ref[...], normed)
                for head in range(heads):
                    held[head, i : i + 1, :] = row_bias[head : head + 1, :]

    bias_ref[...] = held[...].astype(jnp.bfloat16)


def weight_kernel(heads, project_ref, tri_out_ref, kv_ref, pack_ref):
    channels = project_ref.shape[0]
    hidden = tri_out_ref.shape[0]
    dim = hidden // heads
    scale = dim ** (-0.5) * LOG2E
    project = project_ref[...]
    for head in range(heads):
        query = project[:, head * dim : (head + 1) * dim]
        key = project[:, hidden + head * dim : hidden + (head + 1) * dim]
        pack_ref[head * channels : (head + 1) * channels, :] = (
            matmul(key, query, 1, 1) * scale
        ).astype(jnp.bfloat16)
    row = heads * channels
    rest = (
        project[:, 3 * hidden :],
        project[:, 2 * hidden : 3 * hidden],
        tri_out_ref[...],
        kv_ref[...],
    )
    for part in rest:
        flipped = part.astype(jnp.float32).T.astype(jnp.bfloat16)
        pack_ref[row : row + flipped.shape[0], :] = flipped
        row += flipped.shape[0]


def bias_kernel(tiles_per_col, row_devs, idx_ref, cover_ref, mask_ref, *refs):
    *tile_refs, out_ref = refs
    heads, tile_rows, cols = tile_refs[0].shape
    templ, row_dev, col_dev, row_block = idx_ref[1], idx_ref[2], idx_ref[3], idx_ref[4]
    col_devs = row_devs // tiles_per_col
    best = jnp.float32(-MASK_SHIFT)
    for block in range(col_devs):
        best = jnp.maximum(best, mask_shift(cover_ref, mask_ref, templ, row_block, block))
    for turn, tile_ref in enumerate(tile_refs):
        source = lax.rem(row_dev - turn + row_devs, row_devs)
        for place in range(row_devs):
            part, block = place // col_devs, place % col_devs

            @pl.when(source == place)
            def _():
                slot = lax.rem(block - col_dev + col_devs, col_devs)
                shift = mask_shift(cover_ref, mask_ref, templ, row_block, block) - best
                for head in range(heads):
                    flipped = tile_ref[head].astype(jnp.float32).T
                    out_ref[
                        head,
                        pl.ds(slot * cols, cols),
                        part * tile_rows : (part + 1) * tile_rows,
                    ] = (flipped + shift) * LOG2E


def attend_kernel(
    heads, idx_ref, x_ref, own_ref, far_ref, main_ref, bias_ref, pack_ref, query_ref, gain_ref, *refs
):
    out_ref, state_ref = refs[-2:]
    channels = x_ref.shape[1]
    cols = x_ref.shape[2]
    hidden = query_ref.shape[0]
    dim = hidden // heads
    row = heads * channels + hidden
    first_w = pack_ref[:row, :]
    value_w = pack_ref[row : row + hidden, :]
    tri_w = pack_ref[row + hidden : row + hidden + channels, :]
    kv_w = pack_ref[row + hidden + channels :, :]
    ones = jnp.ones((dim, 2 * cols), jnp.bfloat16)
    for i in range(x_ref.shape[0]):
        own = own_ref[i]
        both = jnp.concatenate([own, far_ref[i]], axis=1)
        first = matmul(first_w, own)
        gates = jax.nn.sigmoid(first[heads * channels :, :])
        probe = first.astype(jnp.bfloat16)
        probe = jnp.concatenate(
            [probe[h * channels : (h + 1) * channels, :] for h in range(heads)], axis=1
        )
        scores = matmul(both, probe, 0, 0)
        values = matmul(value_w, both).astype(jnp.bfloat16)
        gated = []
        for pair in range(heads // 2):
            weights = []
            for head in (2 * pair, 2 * pair + 1):
                part = scores[:, head * cols : (head + 1) * cols] + bias_ref[head]
                highest = jnp.max(part, axis=0, keepdims=True)
                weights.append(jnp.exp2(part - highest).astype(jnp.bfloat16))
            summed = matmul(
                jnp.concatenate([values[2 * pair * dim : 2 * (pair + 1) * dim, :], ones], axis=0),
                jnp.concatenate(weights, axis=1),
            )
            for side in range(2):
                head = 2 * pair + side
                lanes = slice(side * cols, (side + 1) * cols)
                total = summed[2 * dim : 2 * dim + 1, lanes]
                gated.append(
                    summed[side * dim : (side + 1) * dim, lanes]
                    * (1.0 / total)
                    * gates[head * dim : (head + 1) * dim, :]
                )
        gated = jnp.concatenate(gated, axis=0).astype(jnp.bfloat16)
        fresh = (x_ref[i].astype(jnp.float32) + matmul(tri_w, gated)).astype(jnp.bfloat16)
        out_ref[i] = fresh
        merge_norm = normed_rows(fresh.astype(jnp.float32), gain_ref[...])
        merge_kv = matmul(kv_w, merge_norm).astype(jnp.bfloat16)
        main_query = matmul(query_ref[...], main_ref[i], 1, 1) * dim ** (-0.5)
        product = main_query * merge_kv[:hidden, :].astype(jnp.float32)
        score = jnp.concatenate(
            [
                jnp.sum(product[h * dim : (h + 1) * dim, :], axis=0, keepdims=True)
                for h in range(heads)
            ],
            axis=0,
        )
        store_state(state_ref, i, merge_kv[hidden:, :], score)


def store_state(state_ref, i, values, score):
    hidden = values.shape[0]
    high = score.astype(jnp.bfloat16)
    low = (score - high.astype(jnp.float32)).astype(jnp.bfloat16)
    state_ref[i, :hidden, :] = values
    state_ref[i, hidden:, :] = jnp.concatenate([high, low], axis=0)


def spread_heads(per_head, dim):
    heads, cols = per_head.shape
    return jnp.concatenate(
        [jnp.broadcast_to(per_head[h : h + 1, :], (dim, cols)) for h in range(heads)], axis=0
    )


def joined(heads, first_ref, second_ref, i, first_shift, second_shift):
    hidden = first_ref.shape[1] - 2 * heads

    def parts(ref, shift):
        extra = ref[i, hidden:, :].astype(jnp.float32)
        return ref[i, :hidden, :].astype(jnp.float32), extra[:heads] + extra[heads:] + shift

    first_values, first_score = parts(first_ref, first_shift)
    second_values, second_score = parts(second_ref, second_shift)
    highest = jnp.maximum(first_score, second_score)
    first_weight = jnp.exp(first_score - highest)
    second_weight = jnp.exp(second_score - highest)
    total = first_weight + second_weight
    inverse = 1.0 / total
    dim = hidden // heads
    values = first_values * spread_heads(first_weight * inverse, dim)
    values = values + second_values * spread_heads(second_weight * inverse, dim)
    return values, highest + jnp.log(total)


def pair_shifts(idx_ref, cover_ref, mask_ref):
    templ, col_dev, row_block = idx_ref[1], idx_ref[3], idx_ref[4]
    even = templ - lax.rem(templ, 2)
    own = mask_shift(cover_ref, mask_ref, templ, row_block, col_dev)
    other = mask_shift(cover_ref, mask_ref, 2 * even + 1 - templ, row_block, col_dev)
    far = 2 - even
    far_best = jnp.maximum(
        mask_shift(cover_ref, mask_ref, far, row_block, col_dev),
        mask_shift(cover_ref, mask_ref, far + 1, row_block, col_dev),
    )
    best = jnp.maximum(own, other)
    return own - best, other - best, best, far_best


def core_join_kernel(heads, idx_ref, cover_ref, mask_ref, own_ref, other_ref, state_ref):
    own_shift, other_shift, _, _ = pair_shifts(idx_ref, cover_ref, mask_ref)
    for i in range(own_ref.shape[0]):
        values, score = joined(heads, own_ref, other_ref, i, own_shift, other_shift)
        store_state(state_ref, i, values.astype(jnp.bfloat16), score)


def chip_join_kernel(
    heads, idx_ref, cover_ref, mask_ref, own_ref, other_ref, w_ref, *refs
):
    merged_ref, out_ref = refs[-2:]
    _, _, best, far_best = pair_shifts(idx_ref, cover_ref, mask_ref)
    top = jnp.maximum(best, far_best)
    for i in range(own_ref.shape[0]):
        values, _ = joined(heads, own_ref, other_ref, i, best - top, far_best - top)
        merged = values.astype(jnp.bfloat16)
        merged_ref[i] = merged
        out_ref[i] = matmul(merged, w_ref[...], 0, 0).astype(jnp.bfloat16)


def embed_kernel(idx_ref, merged_ref, w_ref, prior_ref, out_ref):
    for i in range(merged_ref.shape[0]):
        out_ref[i] = matmul(merged_ref[i], w_ref[...], 0, 0).astype(jnp.bfloat16)


def fused_on_device(
    templ_pair, main_pair, coverage, pair_mask, tri_gain, w_project, w_bias, w_tri_out,
    merge_gain, w_merge_q, w_merge_kv, w_merge_out,
):
    rows, cols, channels = templ_pair.shape[1:]
    hidden = w_tri_out.shape[0]
    heads = w_bias.shape[1]
    pair_ch = main_pair.shape[-1]
    row_devs, col_devs = lax.axis_size("row"), lax.axis_size("col")
    tiles_per_col = row_devs // col_devs
    templ, row_dev, col_dev = (lax.axis_index(a) for a in ("tmpl", "row", "col"))
    idx = jnp.stack([templ % 2, templ, row_dev, col_dev, (row_dev * rows) // BLOCK]).astype(jnp.int32)
    pieces = PIECES
    piece_rows = rows // pieces
    step_rows = STEP_ROWS
    steps = piece_rows // step_rows
    stored = jnp.swapaxes(templ_pair[0], 1, 2)
    bf16, f32 = jnp.bfloat16, jnp.float32
    tri_gain_wide = jnp.broadcast_to(tri_gain[:, None], (channels, cols))
    merge_gain_wide = jnp.broadcast_to(merge_gain[:, None], (channels, cols))

    def whole(array):
        return pl.BlockSpec(array.shape, lambda *_: (0,) * array.ndim)

    smem = pl.BlockSpec(memory_space=pltpu.SMEM)

    def call(kernel, grid, in_specs, out_specs, out_shape, scratch=(), aliases=None, cost=1e6):
        return pl.pallas_call(
            kernel,
            grid_spec=pltpu.PrefetchScalarGridSpec(
                num_scalar_prefetch=1, grid=grid, in_specs=in_specs, out_specs=out_specs,
                scratch_shapes=list(scratch),
            ),
            out_shape=out_shape,
            input_output_aliases=aliases or {},
            cost_estimate=pl.CostEstimate(
                flops=int(cost), bytes_accessed=1 << 20, transcendentals=0
            ),
        )

    chunks = pieces // 2

    def piece_of(p, idx_ref):
        half = idx_ref[0]
        side = jnp.where(p % 2 == 1, half, 1 - half)
        return side * (pieces // 2) + p // 2

    norm_specs = [
        pl.BlockSpec(
            (piece_rows, channels, cols),
            functools.partial(lambda c, p, s: (jnp.clip(p - 2 * c, 0, 1), 0, 0), chunk),
        )
        for chunk in range(chunks)
    ]
    *norms, bias_tile = call(
        functools.partial(norm_kernel, heads),
        (pieces,),
        [
            pl.BlockSpec((piece_rows, channels, cols), lambda p, s: (piece_of(p, s), 0, 0)),
            whole(tri_gain_wide),
            pl.BlockSpec((heads, channels), lambda *_: (0, 0)),
        ],
        norm_specs + [pl.BlockSpec((heads, piece_rows, cols), lambda p, s: (0, piece_of(p, s), 0))],
        [jax.ShapeDtypeStruct((2 * piece_rows, channels, cols), bf16)] * chunks
        + [jax.ShapeDtypeStruct((heads, rows, cols), bf16)],
        [pltpu.VMEM((heads, piece_rows, cols), f32)],
    )(idx, stored, tri_gain_wide, w_bias.T)

    tiles = []
    for turn in range(row_devs):
        perm = []
        for source_row in range(row_devs):
            for source_col in range(col_devs):
                place = (source_row % tiles_per_col) * col_devs + source_col
                target = ((place + turn) % row_devs) * col_devs + source_row // tiles_per_col
                perm.append((source_row * col_devs + source_col, target))
        tiles.append(lax.ppermute(bias_tile, ("row", "col"), perm))
    swap = [(c, col_devs - 1 - c) for c in range(col_devs)]
    fars = [lax.ppermute(norm, "col", swap) for norm in norms]

    pack_shape = ((heads + 1) * channels * 0 + heads * channels + 2 * hidden + channels + 2 * hidden, channels)
    pack = pl.pallas_call(
        functools.partial(weight_kernel, heads),
        out_shape=jax.ShapeDtypeStruct(pack_shape, bf16),
    )(w_project, w_tri_out, w_merge_kv)
    bias = call(
        functools.partial(bias_kernel, tiles_per_col, row_devs),
        (1,),
        [smem, smem] + [whole(t) for t in tiles],
        pl.BlockSpec((heads, col_devs * cols, cols), lambda *_: (0, 0, 0)),
        jax.ShapeDtypeStruct((heads, col_devs * cols, cols), f32),
    )(idx, coverage, pair_mask, *tiles)

    query_w = w_merge_q.T
    out = None
    states = []
    for piece in range(pieces):
        chunk, side = piece // 2, piece % 2

        def at_rows(g, s, piece=piece):
            return (piece_block(s, piece, pieces) * steps + g, 0, 0)

        def at_norm(g, s, side=side):
            return (side * steps + g, 0, 0)

        prior = [] if out is None else [out]
        operands = [
            stored, norms[chunk], fars[chunk], main_pair, bias, pack, query_w, merge_gain_wide
        ] + prior
        specs = [
            pl.BlockSpec((step_rows, channels, cols), at_rows),
            pl.BlockSpec((step_rows, channels, cols), at_norm),
            pl.BlockSpec((step_rows, channels, cols), at_norm),
            pl.BlockSpec((step_rows, cols, pair_ch), at_rows),
            whole(bias), whole(pack), whole(query_w), whole(merge_gain_wide),
        ] + [pl.BlockSpec(memory_space=pl.ANY)] * len(prior)
        out, state = call(
            functools.partial(attend_kernel, heads),
            (steps,),
            specs,
            [
                pl.BlockSpec((step_rows, channels, cols), at_rows),
                pl.BlockSpec((step_rows, hidden + 2 * heads, cols), lambda g, s: (g, 0, 0)),
            ],
            [
                jax.ShapeDtypeStruct(stored.shape, bf16),
                jax.ShapeDtypeStruct((piece_rows, hidden + 2 * heads, cols), bf16),
            ],
            aliases={len(operands): 0} if prior else None,
            cost=6e9,
        )(idx, *operands)
        states.append(state)

    cores = [(t, t + 1 - 2 * (t % 2)) for t in range(lax.axis_size("tmpl"))]
    chips = [(t, (t + 2) % 4) for t in range(lax.axis_size("tmpl"))]
    emb = None
    emb_shape = jax.ShapeDtypeStruct(main_pair.shape, bf16)
    for chunk in range(chunks):
        sent, kept = states[2 * chunk], states[2 * chunk + 1]
        other = lax.ppermute(sent, "tmpl", cores)
        pair_state = call(
            functools.partial(core_join_kernel, heads),
            (1,),
            [smem, smem, whole(kept), whole(other)],
            whole(kept),
            jax.ShapeDtypeStruct(kept.shape, bf16),
        )(idx, coverage, pair_mask, kept, other)
        far_state = lax.ppermute(pair_state, "tmpl", chips)

        def at_own(g, s, piece=2 * chunk + 1):
            return (piece_block(s, piece, pieces), 0, 0)

        def at_other(g, s, piece=2 * chunk):
            return (piece_block(s, piece, pieces), 0, 0)

        prior = [] if emb is None else [emb]
        operands = [coverage, pair_mask, pair_state, far_state, w_merge_out] + prior
        merged, emb = call(
            functools.partial(chip_join_kernel, heads),
            (1,),
            [smem, smem, whole(pair_state), whole(far_state), whole(w_merge_out)]
            + [pl.BlockSpec(memory_space=pl.ANY)] * len(prior),
            [
                pl.BlockSpec((piece_rows, hidden, cols), lambda *_: (0, 0, 0)),
                pl.BlockSpec((piece_rows, cols, pair_ch), at_own),
            ],
            [jax.ShapeDtypeStruct((piece_rows, hidden, cols), bf16), emb_shape],
            aliases={len(operands): 1} if prior else None,
        )(idx, *operands)
        merged_other = lax.ppermute(merged, "tmpl", cores)
        emb = call(
            embed_kernel,
            (1,),
            [whole(merged_other), whole(w_merge_out), pl.BlockSpec(memory_space=pl.ANY)],
            pl.BlockSpec((piece_rows, cols, pair_ch), at_other),
            emb_shape,
            aliases={3: 0},
        )(idx, merged_other, w_merge_out, emb)
    return (jnp.swapaxes(out, 1, 2)[None], emb)


PIECES = 4
STEP_ROWS = 4


def takes_fused(templ_pair, main_pair):
    rows, cols = templ_pair.shape[1:3]
    row_devs, col_devs = lax.axis_size("row"), lax.axis_size("col")
    return (
        lax.axis_size("tmpl") == 4
        and col_devs == 2
        and cols == BLOCK
        and BLOCK % rows == 0
        and row_devs % col_devs == 0
        and rows * (row_devs // col_devs) == cols
        and rows % (PIECES * STEP_ROWS) == 0
    )


def on_device(*operands):
    if takes_fused(*operands[:2]):
        return fused_on_device(*operands)
    return plain_on_device(*operands)


def solution(mesh):
    in_specs = (
        P("tmpl", "row", "col", None),
        P("row", "col", None),
        P(),
        P(),
        P(),
        P(),
        P(),
        P(),
        P(),
        P(),
        P(),
        P(),
    )
    out_specs = (P("tmpl", "row", "col", None), P("row", "col", None))
    return jax.shard_map(
        on_device, mesh=mesh, in_specs=in_specs, out_specs=out_specs, check_vma=False
    )
```

```python
import functools

import jax
import jax.numpy as jnp
from jax import lax
from jax.experimental import pallas as pl
from jax.experimental.pallas import tpu as pltpu
from jax.sharding import PartitionSpec as P

BLOCK = 128


MASK_SHIFT = 10000.0
EPSILON = 1e-05
NEG_START = -1e30


def combined_all(part, axis, combine):
    gathered = jax.tree.map(lambda a: lax.all_gather(a, axis), part)

    def take(source):
        return jax.tree.map(lambda a: lax.dynamic_index_in_dim(a, source, 0, False), gathered)

    return lax.fori_loop(
        1, lax.axis_size(axis), lambda source, state: combine(state, take(source)), take(0)
    )


def layer_norm(values, scale_gain):
    values = values.astype(jnp.float32)
    center = values - jnp.mean(values, axis=-1, keepdims=True)
    spread = jnp.mean(center * center, axis=-1, keepdims=True)
    return center * lax.rsqrt(spread + EPSILON) * scale_gain


def row_group(rows_dev, cols_dev):
    chosen = 1
    for candidate in range(1, rows_dev + 1):
        if rows_dev % candidate == 0 and candidate * cols_dev <= 2048:
            chosen = candidate
    return chosen


def plain_on_device(
    templ_pair,
    main_pair,
    coverage,
    pair_mask,
    tri_gain,
    w_project,
    w_bias,
    w_tri_out,
    merge_gain,
    w_merge_q,
    w_merge_kv,
    w_merge_out,
):
    pair_tile = templ_pair[0]
    rows_dev, cols_dev, channels = pair_tile.shape
    hidden = w_tri_out.shape[0]
    head_count = w_bias.shape[1]
    head_dim = hidden // head_count
    score_scale = head_dim ** (-0.5)
    row_start = lax.axis_index("row") * rows_dev
    col_start = lax.axis_index("col") * cols_dev
    templ_index = lax.axis_index("tmpl")
    cover_tok = jnp.repeat(coverage, BLOCK, axis=1)
    own_cover = lax.dynamic_index_in_dim(cover_tok, templ_index, 0, keepdims=False)
    mask_full = jnp.repeat(jnp.repeat(pair_mask, BLOCK, axis=0), BLOCK, axis=1)
    mask_rows = lax.dynamic_slice_in_dim(mask_full, row_start, rows_dev, 0)
    cover_rows = lax.dynamic_slice_in_dim(own_cover, row_start, rows_dev, 0)
    normed = layer_norm(pair_tile, tri_gain).astype(jnp.bfloat16)
    flat_norm = normed.reshape(-1, channels)
    w_query_gate = jnp.concatenate([w_project[:, :hidden], w_project[:, 3 * hidden :]], axis=1)
    query_gate = jnp.dot(flat_norm, w_query_gate, preferred_element_type=jnp.float32).reshape(
        rows_dev, cols_dev, 2 * hidden
    )
    queries = (
        (query_gate[..., :hidden] * score_scale)
        .astype(jnp.bfloat16)
        .reshape(rows_dev, cols_dev, head_count, head_dim)
    )
    gate_values = jax.nn.sigmoid(query_gate[..., hidden:])
    bias_tile = jnp.dot(flat_norm, w_bias, preferred_element_type=jnp.float32).astype(jnp.bfloat16)
    bias_tile = jnp.transpose(bias_tile.reshape(rows_dev, cols_dev, head_count), (2, 0, 1))
    bias_column = lax.all_gather(bias_tile, "row", axis=1, tiled=True)
    bias_slab = lax.all_to_all(bias_column, "col", split_axis=1, concat_axis=2, tiled=True)
    bias_rows = jnp.transpose(bias_slab, (1, 0, 2)).astype(jnp.float32)
    key_shift = MASK_SHIFT * (
        (cover_rows[:, None] * own_cover[None, :] * mask_rows).astype(jnp.float32) - 1.0
    )
    w_key_value = w_project[:, hidden : 3 * hidden]
    group = row_group(rows_dev, cols_dev)
    splits = rows_dev // group

    def grouped(array):
        return array.reshape((splits, group) + array.shape[1:])

    start_state = (
        jnp.full((rows_dev, cols_dev, head_count), NEG_START, jnp.float32),
        jnp.zeros((rows_dev, cols_dev, head_count), jnp.float32),
        jnp.zeros((rows_dev, cols_dev, head_count, head_dim), jnp.float32),
    )
    norm_piece = lax.all_gather(normed, "col", axis=1, tiled=True)
    piece_width = norm_piece.shape[1]

    def one_group(group_args):
        query_part, norm_part, shift_part, maxima, totals, weighted = group_args
        key_value = jnp.dot(
            norm_part.reshape(-1, channels), w_key_value, preferred_element_type=jnp.float32
        ).astype(jnp.bfloat16)
        key_value = key_value.reshape(group, piece_width, 2 * hidden)
        key_part = key_value[..., :hidden].reshape(group, piece_width, head_count, head_dim)
        value_part = key_value[..., hidden:].reshape(group, piece_width, head_count, head_dim)
        scores = jnp.einsum(
            "ijhd,ikhd->ijhk", query_part, key_part, preferred_element_type=jnp.float32
        )
        scores = scores + bias_rows[None] + shift_part[:, None, None, :]
        highest = jnp.maximum(maxima, jnp.max(scores, axis=-1))
        rescale = jnp.exp(maxima - highest)
        weights = jnp.exp(scores - highest[..., None])
        totals = totals * rescale + jnp.sum(weights, axis=-1)
        summed = jnp.einsum(
            "ijhk,ikhd->ijhd",
            weights.astype(jnp.bfloat16),
            value_part,
            preferred_element_type=jnp.float32,
        )
        weighted = weighted * rescale[..., None] + summed
        return (highest, totals, weighted)

    outcome = lax.map(
        one_group,
        (
            grouped(queries),
            grouped(norm_piece),
            grouped(key_shift),
            grouped(start_state[0]),
            grouped(start_state[1]),
            grouped(start_state[2]),
        ),
    )
    result = tuple((member.reshape((rows_dev,) + member.shape[2:]) for member in outcome))
    attended = result[2] / result[1][..., None]
    gated = (attended.reshape(rows_dev, cols_dev, hidden) * gate_values).astype(jnp.bfloat16)
    projected = jnp.dot(
        gated.reshape(-1, hidden), w_tri_out, preferred_element_type=jnp.float32
    ).reshape(rows_dev, cols_dev, channels)
    new_pair = (pair_tile.astype(jnp.float32) + projected).astype(jnp.bfloat16)
    merge_norm = layer_norm(new_pair, merge_gain).astype(jnp.bfloat16)
    merge_kv = jnp.dot(
        merge_norm.reshape(-1, channels), w_merge_kv, preferred_element_type=jnp.float32
    ).astype(jnp.bfloat16)
    merge_kv = merge_kv.reshape(rows_dev, cols_dev, 2 * hidden)
    pair_ch = main_pair.shape[-1]
    main_query = (
        jnp.dot(main_pair.reshape(-1, pair_ch), w_merge_q, preferred_element_type=jnp.float32)
        * score_scale
    )
    main_query = main_query.reshape(rows_dev, cols_dev, head_count, head_dim)
    mask_tile = lax.dynamic_slice_in_dim(mask_rows, col_start, cols_dev, 1)
    own_cols = lax.dynamic_slice_in_dim(own_cover, col_start, cols_dev, 0)
    own_valid = cover_rows[:, None] * own_cols[None, :] * mask_tile
    shift_bias = MASK_SHIFT * (own_valid.astype(jnp.float32) - 1.0)
    keys_own = (
        merge_kv[..., :hidden].astype(jnp.float32).reshape(rows_dev, cols_dev, head_count, head_dim)
    )
    values_own = (
        merge_kv[..., hidden:].astype(jnp.float32).reshape(rows_dev, cols_dev, head_count, head_dim)
    )
    scores = jnp.sum(main_query * keys_own, axis=-1) + shift_bias[..., None]

    def combine(earlier, later):
        highest = jnp.maximum(earlier[0], later[0])
        early_scale = jnp.exp(earlier[0] - highest)
        late_scale = jnp.exp(later[0] - highest)
        return (
            highest,
            earlier[1] * early_scale + later[1] * late_scale,
            earlier[2] * early_scale[..., None] + later[2] * late_scale[..., None],
        )

    merged_state = combined_all((scores, jnp.ones_like(scores), values_own), "tmpl", combine)
    merged = merged_state[2] / merged_state[1][..., None]
    merged = merged.reshape(-1, hidden).astype(jnp.bfloat16)
    embedding = jnp.dot(merged, w_merge_out, preferred_element_type=jnp.float32).astype(
        jnp.bfloat16
    )
    return (new_pair[None], embedding.reshape(rows_dev, cols_dev, pair_ch))


LOG2E = 1.4426950408889634


def normed_rows(values, gain):
    center = values - jnp.mean(values, axis=0, keepdims=True)
    spread = jnp.mean(center * center, axis=0, keepdims=True)
    return (center * lax.rsqrt(spread + EPSILON) * gain).astype(jnp.bfloat16)


def piece_block(idx_ref, piece, pieces):
    half = idx_ref[0]
    side = half if piece % 2 else 1 - half
    return side * (pieces // 2) + piece // 2


def mask_shift(cover_ref, mask_ref, templ, row_block, col_block):
    valid = (
        cover_ref[templ, row_block] * cover_ref[templ, col_block] * mask_ref[row_block, col_block]
    )
    return MASK_SHIFT * (valid.astype(jnp.float32) - 1.0)


def matmul(lhs, rhs, lhs_dim=1, rhs_dim=0):
    return lax.dot_general(
        lhs, rhs, (((lhs_dim,), (rhs_dim,)), ((), ())), preferred_element_type=jnp.float32
    )


def norm_kernel(
    heads, idx_ref, x_ref, gain_ref, bias_w_ref, *refs
):
    piece = pl.program_id(0)
    *norm_refs, bias_ref, held = refs
    for chunk, norm_ref in enumerate(norm_refs):

        @pl.when(piece // 2 == chunk)
        def _():
            for i in range(x_ref.shape[0]):
                normed = normed_rows(x_ref[i].astype(jnp.float32), gain_ref[...])
                norm_ref[i] = normed
                row_bias = matmul(bias_w_ref[...], normed)
                for head in range(heads):
                    held[head, i : i + 1, :] = row_bias[head : head + 1, :]

    bias_ref[...] = held[...].astype(jnp.bfloat16)


def weight_kernel(heads, project_ref, tri_out_ref, kv_ref, pack_ref):
    channels = project_ref.shape[0]
    hidden = tri_out_ref.shape[0]
    dim = hidden // heads
    scale = dim ** (-0.5) * LOG2E
    project = project_ref[...]
    for head in range(heads):
        query = project[:, head * dim : (head + 1) * dim]
        key = project[:, hidden + head * dim : hidden + (head + 1) * dim]
        pack_ref[head * channels : (head + 1) * channels, :] = (
            matmul(key, query, 1, 1) * scale
        ).astype(jnp.bfloat16)
    row = heads * channels
    rest = (
        project[:, 3 * hidden :],
        project[:, 2 * hidden : 3 * hidden],
        tri_out_ref[...],
        kv_ref[...],
    )
    for part in rest:
        flipped = part.astype(jnp.float32).T.astype(jnp.bfloat16)
        pack_ref[row : row + flipped.shape[0], :] = flipped
        row += flipped.shape[0]


def bias_kernel(tiles_per_col, row_devs, idx_ref, cover_ref, mask_ref, *refs):
    *tile_refs, out_ref = refs
    heads, tile_rows, cols = tile_refs[0].shape
    templ, row_dev, col_dev, row_block = idx_ref[1], idx_ref[2], idx_ref[3], idx_ref[4]
    col_devs = row_devs // tiles_per_col
    best = jnp.float32(-MASK_SHIFT)
    for block in range(col_devs):
        best = jnp.maximum(best, mask_shift(cover_ref, mask_ref, templ, row_block, block))
    for turn, tile_ref in enumerate(tile_refs):
        source = lax.rem(row_dev - turn + row_devs, row_devs)
        for place in range(row_devs):
            part, block = place // col_devs, place % col_devs

            @pl.when(source == place)
            def _():
                slot = lax.rem(block - col_dev + col_devs, col_devs)
                shift = mask_shift(cover_ref, mask_ref, templ, row_block, block) - best
                for head in range(heads):
                    flipped = tile_ref[head].astype(jnp.float32).T
                    out_ref[
                        head,
                        pl.ds(slot * cols, cols),
                        part * tile_rows : (part + 1) * tile_rows,
                    ] = (flipped + shift) * LOG2E


def attend_kernel(
    heads, idx_ref, x_ref, own_ref, far_ref, main_ref, bias_ref, pack_ref, query_ref, gain_ref, *refs
):
    out_ref, state_ref, turned, probes, gates, mixers, held, tops, gated = refs[-9:]
    step_rows, channels, cols = x_ref.shape
    hidden = query_ref.shape[0]
    dim = hidden // heads
    row = heads * channels + hidden
    first_w = pack_ref[:row, :]
    value_w = pack_ref[row : row + hidden, :]
    tri_w = pack_ref[row + hidden : row + hidden + channels, :]
    kv_w = pack_ref[row + hidden + channels :, :]
    for i in range(step_rows):
        own = own_ref[i]
        both = jnp.concatenate([own, far_ref[i]], axis=1)
        first = matmul(first_w, own)
        for h in range(heads):
            probes[i, h] = first[h * channels : (h + 1) * channels, :].astype(jnp.bfloat16)
        gates[i] = jax.nn.sigmoid(first[heads * channels :, :])
        values = matmul(value_w, both).astype(jnp.bfloat16)
        for h in range(heads):
            mixers[i, h, :dim, :] = values[h * dim : (h + 1) * dim, :]
            mixers[i, h, dim:, :] = jnp.ones((mixers.shape[2] - dim, both.shape[1]), jnp.bfloat16)
        turned[i] = both.T

    slots = held.shape[0]

    def score_row(i):
        for h in range(heads):
            scores = matmul(turned[i], probes[i, h]) + bias_ref[h]
            held[i % slots, h] = scores
            tops[i % slots, h] = jnp.broadcast_to(
                jnp.max(scores, axis=0, keepdims=True), tops.shape[2:]
            )

    def mix_row(i):
        for h in range(heads):
            weights = jnp.exp2(held[i % slots, h] - tops[i % slots, h][:1])
            mixed = matmul(mixers[i, h], weights.astype(jnp.bfloat16))
            span = slice(h * dim, (h + 1) * dim)
            gated[i, span, :] = (
                mixed[:dim] * (1.0 / mixed[dim : dim + 1]) * gates[i, span, :]
            ).astype(jnp.bfloat16)

    score_row(0)
    for i in range(step_rows):
        if i + 1 < step_rows:
            score_row(i + 1)
        mix_row(i)
    for i in range(step_rows):
        fresh = x_ref[i].astype(jnp.float32) + matmul(tri_w, gated[i])
        out_ref[i] = fresh.astype(jnp.bfloat16)
    for i in range(step_rows):
        merge_norm = normed_rows(out_ref[i].astype(jnp.float32), gain_ref[...])
        merge_kv = matmul(kv_w, merge_norm).astype(jnp.bfloat16)
        main_query = matmul(query_ref[...], main_ref[i], 1, 1) * dim ** (-0.5)
        product = main_query * merge_kv[:hidden, :].astype(jnp.float32)
        score = jnp.concatenate(
            [
                jnp.sum(product[h * dim : (h + 1) * dim, :], axis=0, keepdims=True)
                for h in range(heads)
            ],
            axis=0,
        )
        store_state(state_ref, i, merge_kv[hidden:, :], score)


def store_state(state_ref, i, values, score):
    hidden = values.shape[0]
    high = score.astype(jnp.bfloat16)
    low = (score - high.astype(jnp.float32)).astype(jnp.bfloat16)
    state_ref[i, :hidden, :] = values
    state_ref[i, hidden:, :] = jnp.concatenate([high, low], axis=0)


def spread_heads(per_head, dim):
    heads, cols = per_head.shape
    return jnp.concatenate(
        [jnp.broadcast_to(per_head[h : h + 1, :], (dim, cols)) for h in range(heads)], axis=0
    )


def joined(heads, first_ref, second_ref, i, first_shift, second_shift):
    hidden = first_ref.shape[1] - 2 * heads

    def parts(ref, shift):
        extra = ref[i, hidden:, :].astype(jnp.float32)
        return ref[i, :hidden, :].astype(jnp.float32), extra[:heads] + extra[heads:] + shift

    first_values, first_score = parts(first_ref, first_shift)
    second_values, second_score = parts(second_ref, second_shift)
    highest = jnp.maximum(first_score, second_score)
    first_weight = jnp.exp(first_score - highest)
    second_weight = jnp.exp(second_score - highest)
    total = first_weight + second_weight
    inverse = 1.0 / total
    dim = hidden // heads
    values = first_values * spread_heads(first_weight * inverse, dim)
    values = values + second_values * spread_heads(second_weight * inverse, dim)
    return values, highest + jnp.log(total)


def pair_shifts(idx_ref, cover_ref, mask_ref):
    templ, col_dev, row_block = idx_ref[1], idx_ref[3], idx_ref[4]
    even = templ - lax.rem(templ, 2)
    own = mask_shift(cover_ref, mask_ref, templ, row_block, col_dev)
    other = mask_shift(cover_ref, mask_ref, 2 * even + 1 - templ, row_block, col_dev)
    far = 2 - even
    far_best = jnp.maximum(
        mask_shift(cover_ref, mask_ref, far, row_block, col_dev),
        mask_shift(cover_ref, mask_ref, far + 1, row_block, col_dev),
    )
    best = jnp.maximum(own, other)
    return own - best, other - best, best, far_best


def core_join_kernel(heads, idx_ref, cover_ref, mask_ref, own_ref, other_ref, state_ref):
    own_shift, other_shift, _, _ = pair_shifts(idx_ref, cover_ref, mask_ref)
    for i in range(own_ref.shape[0]):
        values, score = joined(heads, own_ref, other_ref, i, own_shift, other_shift)
        store_state(state_ref, i, values.astype(jnp.bfloat16), score)


def chip_join_kernel(
    heads, idx_ref, cover_ref, mask_ref, own_ref, other_ref, w_ref, *refs
):
    merged_ref, out_ref = refs[-2:]
    _, _, best, far_best = pair_shifts(idx_ref, cover_ref, mask_ref)
    top = jnp.maximum(best, far_best)
    for i in range(own_ref.shape[0]):
        values, _ = joined(heads, own_ref, other_ref, i, best - top, far_best - top)
        merged = values.astype(jnp.bfloat16)
        merged_ref[i] = merged
        out_ref[i] = matmul(merged, w_ref[...], 0, 0).astype(jnp.bfloat16)


def embed_kernel(idx_ref, merged_ref, w_ref, prior_ref, out_ref):
    for i in range(merged_ref.shape[0]):
        out_ref[i] = matmul(merged_ref[i], w_ref[...], 0, 0).astype(jnp.bfloat16)


def fused_on_device(
    templ_pair, main_pair, coverage, pair_mask, tri_gain, w_project, w_bias, w_tri_out,
    merge_gain, w_merge_q, w_merge_kv, w_merge_out,
):
    rows, cols, channels = templ_pair.shape[1:]
    hidden = w_tri_out.shape[0]
    heads = w_bias.shape[1]
    dim = hidden // heads
    pair_ch = main_pair.shape[-1]
    row_devs, col_devs = lax.axis_size("row"), lax.axis_size("col")
    tiles_per_col = row_devs // col_devs
    templ, row_dev, col_dev = (lax.axis_index(a) for a in ("tmpl", "row", "col"))
    idx = jnp.stack([templ % 2, templ, row_dev, col_dev, (row_dev * rows) // BLOCK]).astype(jnp.int32)
    pieces = PIECES
    piece_rows = rows // pieces
    step_rows = STEP_ROWS
    steps = piece_rows // step_rows
    stored = jnp.swapaxes(templ_pair[0], 1, 2)
    bf16, f32 = jnp.bfloat16, jnp.float32
    tri_gain_wide = jnp.broadcast_to(tri_gain[:, None], (channels, cols))
    merge_gain_wide = jnp.broadcast_to(merge_gain[:, None], (channels, cols))

    def whole(array):
        return pl.BlockSpec(array.shape, lambda *_: (0,) * array.ndim)

    smem = pl.BlockSpec(memory_space=pltpu.SMEM)

    def call(kernel, grid, in_specs, out_specs, out_shape, scratch=(), aliases=None, cost=1e6):
        return pl.pallas_call(
            kernel,
            grid_spec=pltpu.PrefetchScalarGridSpec(
                num_scalar_prefetch=1, grid=grid, in_specs=in_specs, out_specs=out_specs,
                scratch_shapes=list(scratch),
            ),
            out_shape=out_shape,
            input_output_aliases=aliases or {},
            cost_estimate=pl.CostEstimate(
                flops=int(cost), bytes_accessed=1 << 20, transcendentals=0
            ),
        )

    chunks = pieces // 2

    def piece_of(p, idx_ref):
        half = idx_ref[0]
        side = jnp.where(p % 2 == 1, half, 1 - half)
        return side * (pieces // 2) + p // 2

    norm_specs = [
        pl.BlockSpec(
            (piece_rows, channels, cols),
            functools.partial(lambda c, p, s: (jnp.clip(p - 2 * c, 0, 1), 0, 0), chunk),
        )
        for chunk in range(chunks)
    ]
    *norms, bias_tile = call(
        functools.partial(norm_kernel, heads),
        (pieces,),
        [
            pl.BlockSpec((piece_rows, channels, cols), lambda p, s: (piece_of(p, s), 0, 0)),
            whole(tri_gain_wide),
            pl.BlockSpec((heads, channels), lambda *_: (0, 0)),
        ],
        norm_specs + [pl.BlockSpec((heads, piece_rows, cols), lambda p, s: (0, piece_of(p, s), 0))],
        [jax.ShapeDtypeStruct((2 * piece_rows, channels, cols), bf16)] * chunks
        + [jax.ShapeDtypeStruct((heads, rows, cols), bf16)],
        [pltpu.VMEM((heads, piece_rows, cols), f32)],
    )(idx, stored, tri_gain_wide, w_bias.T)

    tiles = []
    for turn in range(row_devs):
        perm = []
        for source_row in range(row_devs):
            for source_col in range(col_devs):
                place = (source_row % tiles_per_col) * col_devs + source_col
                target = ((place + turn) % row_devs) * col_devs + source_row // tiles_per_col
                perm.append((source_row * col_devs + source_col, target))
        tiles.append(lax.ppermute(bias_tile, ("row", "col"), perm))
    swap = [(c, col_devs - 1 - c) for c in range(col_devs)]
    fars = [lax.ppermute(norm, "col", swap) for norm in norms]

    pack_shape = (heads * channels + 2 * hidden + channels + 2 * hidden, channels)
    pack = pl.pallas_call(
        functools.partial(weight_kernel, heads),
        out_shape=jax.ShapeDtypeStruct(pack_shape, bf16),
    )(w_project, w_tri_out, w_merge_kv)
    bias = call(
        functools.partial(bias_kernel, tiles_per_col, row_devs),
        (1,),
        [smem, smem] + [whole(t) for t in tiles],
        pl.BlockSpec((heads, col_devs * cols, cols), lambda *_: (0, 0, 0)),
        jax.ShapeDtypeStruct((heads, col_devs * cols, cols), f32),
    )(idx, coverage, pair_mask, *tiles)

    query_w = w_merge_q.T
    out = None
    states = []
    for piece in range(pieces):
        chunk, side = piece // 2, piece % 2

        def at_rows(g, s, piece=piece):
            return (piece_block(s, piece, pieces) * steps + g, 0, 0)

        def at_norm(g, s, side=side):
            return (side * steps + g, 0, 0)

        prior = [] if out is None else [out]
        operands = [
            stored, norms[chunk], fars[chunk], main_pair, bias, pack, query_w, merge_gain_wide
        ] + prior
        specs = [
            pl.BlockSpec((step_rows, channels, cols), at_rows),
            pl.BlockSpec((step_rows, channels, cols), at_norm),
            pl.BlockSpec((step_rows, channels, cols), at_norm),
            pl.BlockSpec((step_rows, cols, pair_ch), at_rows),
            whole(bias), whole(pack), whole(query_w), whole(merge_gain_wide),
        ] + [pl.BlockSpec(memory_space=pl.ANY)] * len(prior)
        out, state = call(
            functools.partial(attend_kernel, heads),
            (steps,),
            specs,
            [
                pl.BlockSpec((step_rows, channels, cols), at_rows),
                pl.BlockSpec((step_rows, hidden + 2 * heads, cols), lambda g, s: (g, 0, 0)),
            ],
            [
                jax.ShapeDtypeStruct(stored.shape, bf16),
                jax.ShapeDtypeStruct((piece_rows, hidden + 2 * heads, cols), bf16),
            ],
            [
                pltpu.VMEM((step_rows, col_devs * cols, channels), bf16),
                pltpu.VMEM((step_rows, heads, channels, cols), bf16),
                pltpu.VMEM((step_rows, hidden, cols), f32),
                pltpu.VMEM((step_rows, heads, 2 * dim, col_devs * cols), bf16),
                pltpu.VMEM((2, heads, col_devs * cols, cols), f32),
                pltpu.VMEM((2, heads, 8, cols), f32),
                pltpu.VMEM((step_rows, hidden, cols), bf16),
            ],
            aliases={len(operands): 0} if prior else None,
            cost=6e9,
        )(idx, *operands)
        states.append(state)

    cores = [(t, t + 1 - 2 * (t % 2)) for t in range(lax.axis_size("tmpl"))]
    chips = [(t, (t + 2) % 4) for t in range(lax.axis_size("tmpl"))]
    emb = None
    emb_shape = jax.ShapeDtypeStruct(main_pair.shape, bf16)
    for chunk in range(chunks):
        sent, kept = states[2 * chunk], states[2 * chunk + 1]
        other = lax.ppermute(sent, "tmpl", cores)
        pair_state = call(
            functools.partial(core_join_kernel, heads),
            (1,),
            [smem, smem, whole(kept), whole(other)],
            whole(kept),
            jax.ShapeDtypeStruct(kept.shape, bf16),
        )(idx, coverage, pair_mask, kept, other)
        far_state = lax.ppermute(pair_state, "tmpl", chips)

        def at_own(g, s, piece=2 * chunk + 1):
            return (piece_block(s, piece, pieces), 0, 0)

        def at_other(g, s, piece=2 * chunk):
            return (piece_block(s, piece, pieces), 0, 0)

        prior = [] if emb is None else [emb]
        operands = [coverage, pair_mask, pair_state, far_state, w_merge_out] + prior
        merged, emb = call(
            functools.partial(chip_join_kernel, heads),
            (1,),
            [smem, smem, whole(pair_state), whole(far_state), whole(w_merge_out)]
            + [pl.BlockSpec(memory_space=pl.ANY)] * len(prior),
            [
                pl.BlockSpec((piece_rows, hidden, cols), lambda *_: (0, 0, 0)),
                pl.BlockSpec((piece_rows, cols, pair_ch), at_own),
            ],
            [jax.ShapeDtypeStruct((piece_rows, hidden, cols), bf16), emb_shape],
            aliases={len(operands): 1} if prior else None,
        )(idx, *operands)
        merged_other = lax.ppermute(merged, "tmpl", cores)
        emb = call(
            embed_kernel,
            (1,),
            [whole(merged_other), whole(w_merge_out), pl.BlockSpec(memory_space=pl.ANY)],
            pl.BlockSpec((piece_rows, cols, pair_ch), at_other),
            emb_shape,
            aliases={3: 0},
        )(idx, merged_other, w_merge_out, emb)
    return (jnp.swapaxes(out, 1, 2)[None], emb)


PIECES = 4
STEP_ROWS = 8


def takes_fused(templ_pair, main_pair):
    rows, cols = templ_pair.shape[1:3]
    row_devs, col_devs = lax.axis_size("row"), lax.axis_size("col")
    return (
        lax.axis_size("tmpl") == 4
        and col_devs == 2
        and cols == BLOCK
        and BLOCK % rows == 0
        and row_devs % col_devs == 0
        and rows * (row_devs // col_devs) == cols
        and rows % (PIECES * STEP_ROWS) == 0
    )


def on_device(*operands):
    if takes_fused(*operands[:2]):
        return fused_on_device(*operands)
    return plain_on_device(*operands)


def solution(mesh):
    in_specs = (
        P("tmpl", "row", "col", None),
        P("row", "col", None),
        P(),
        P(),
        P(),
        P(),
        P(),
        P(),
        P(),
        P(),
        P(),
        P(),
    )
    out_specs = (P("tmpl", "row", "col", None), P("row", "col", None))
    return jax.shard_map(
        on_device, mesh=mesh, in_specs=in_specs, out_specs=out_specs, check_vma=False
    )
```

```python
import functools

import jax
import jax.numpy as jnp
from jax import lax
from jax.experimental import pallas as pl
from jax.experimental.pallas import tpu as pltpu
from jax.sharding import PartitionSpec as P

BLOCK = 128


MASK_SHIFT = 10000.0
EPSILON = 1e-05
NEG_START = -1e30


def combined_all(part, axis, combine):
    gathered = jax.tree.map(lambda a: lax.all_gather(a, axis), part)

    def take(source):
        return jax.tree.map(lambda a: lax.dynamic_index_in_dim(a, source, 0, False), gathered)

    return lax.fori_loop(
        1, lax.axis_size(axis), lambda source, state: combine(state, take(source)), take(0)
    )


def layer_norm(values, scale_gain):
    values = values.astype(jnp.float32)
    center = values - jnp.mean(values, axis=-1, keepdims=True)
    spread = jnp.mean(center * center, axis=-1, keepdims=True)
    return center * lax.rsqrt(spread + EPSILON) * scale_gain


def row_group(rows_dev, cols_dev):
    chosen = 1
    for candidate in range(1, rows_dev + 1):
        if rows_dev % candidate == 0 and candidate * cols_dev <= 2048:
            chosen = candidate
    return chosen


def plain_on_device(
    templ_pair,
    main_pair,
    coverage,
    pair_mask,
    tri_gain,
    w_project,
    w_bias,
    w_tri_out,
    merge_gain,
    w_merge_q,
    w_merge_kv,
    w_merge_out,
):
    pair_tile = templ_pair[0]
    rows_dev, cols_dev, channels = pair_tile.shape
    hidden = w_tri_out.shape[0]
    head_count = w_bias.shape[1]
    head_dim = hidden // head_count
    score_scale = head_dim ** (-0.5)
    row_start = lax.axis_index("row") * rows_dev
    col_start = lax.axis_index("col") * cols_dev
    templ_index = lax.axis_index("tmpl")
    cover_tok = jnp.repeat(coverage, BLOCK, axis=1)
    own_cover = lax.dynamic_index_in_dim(cover_tok, templ_index, 0, keepdims=False)
    mask_full = jnp.repeat(jnp.repeat(pair_mask, BLOCK, axis=0), BLOCK, axis=1)
    mask_rows = lax.dynamic_slice_in_dim(mask_full, row_start, rows_dev, 0)
    cover_rows = lax.dynamic_slice_in_dim(own_cover, row_start, rows_dev, 0)
    normed = layer_norm(pair_tile, tri_gain).astype(jnp.bfloat16)
    flat_norm = normed.reshape(-1, channels)
    w_query_gate = jnp.concatenate([w_project[:, :hidden], w_project[:, 3 * hidden :]], axis=1)
    query_gate = jnp.dot(flat_norm, w_query_gate, preferred_element_type=jnp.float32).reshape(
        rows_dev, cols_dev, 2 * hidden
    )
    queries = (
        (query_gate[..., :hidden] * score_scale)
        .astype(jnp.bfloat16)
        .reshape(rows_dev, cols_dev, head_count, head_dim)
    )
    gate_values = jax.nn.sigmoid(query_gate[..., hidden:])
    bias_tile = jnp.dot(flat_norm, w_bias, preferred_element_type=jnp.float32).astype(jnp.bfloat16)
    bias_tile = jnp.transpose(bias_tile.reshape(rows_dev, cols_dev, head_count), (2, 0, 1))
    bias_column = lax.all_gather(bias_tile, "row", axis=1, tiled=True)
    bias_slab = lax.all_to_all(bias_column, "col", split_axis=1, concat_axis=2, tiled=True)
    bias_rows = jnp.transpose(bias_slab, (1, 0, 2)).astype(jnp.float32)
    key_shift = MASK_SHIFT * (
        (cover_rows[:, None] * own_cover[None, :] * mask_rows).astype(jnp.float32) - 1.0
    )
    w_key_value = w_project[:, hidden : 3 * hidden]
    group = row_group(rows_dev, cols_dev)
    splits = rows_dev // group

    def grouped(array):
        return array.reshape((splits, group) + array.shape[1:])

    start_state = (
        jnp.full((rows_dev, cols_dev, head_count), NEG_START, jnp.float32),
        jnp.zeros((rows_dev, cols_dev, head_count), jnp.float32),
        jnp.zeros((rows_dev, cols_dev, head_count, head_dim), jnp.float32),
    )
    norm_piece = lax.all_gather(normed, "col", axis=1, tiled=True)
    piece_width = norm_piece.shape[1]

    def one_group(group_args):
        query_part, norm_part, shift_part, maxima, totals, weighted = group_args
        key_value = jnp.dot(
            norm_part.reshape(-1, channels), w_key_value, preferred_element_type=jnp.float32
        ).astype(jnp.bfloat16)
        key_value = key_value.reshape(group, piece_width, 2 * hidden)
        key_part = key_value[..., :hidden].reshape(group, piece_width, head_count, head_dim)
        value_part = key_value[..., hidden:].reshape(group, piece_width, head_count, head_dim)
        scores = jnp.einsum(
            "ijhd,ikhd->ijhk", query_part, key_part, preferred_element_type=jnp.float32
        )
        scores = scores + bias_rows[None] + shift_part[:, None, None, :]
        highest = jnp.maximum(maxima, jnp.max(scores, axis=-1))
        rescale = jnp.exp(maxima - highest)
        weights = jnp.exp(scores - highest[..., None])
        totals = totals * rescale + jnp.sum(weights, axis=-1)
        summed = jnp.einsum(
            "ijhk,ikhd->ijhd",
            weights.astype(jnp.bfloat16),
            value_part,
            preferred_element_type=jnp.float32,
        )
        weighted = weighted * rescale[..., None] + summed
        return (highest, totals, weighted)

    outcome = lax.map(
        one_group,
        (
            grouped(queries),
            grouped(norm_piece),
            grouped(key_shift),
            grouped(start_state[0]),
            grouped(start_state[1]),
            grouped(start_state[2]),
        ),
    )
    result = tuple((member.reshape((rows_dev,) + member.shape[2:]) for member in outcome))
    attended = result[2] / result[1][..., None]
    gated = (attended.reshape(rows_dev, cols_dev, hidden) * gate_values).astype(jnp.bfloat16)
    projected = jnp.dot(
        gated.reshape(-1, hidden), w_tri_out, preferred_element_type=jnp.float32
    ).reshape(rows_dev, cols_dev, channels)
    new_pair = (pair_tile.astype(jnp.float32) + projected).astype(jnp.bfloat16)
    merge_norm = layer_norm(new_pair, merge_gain).astype(jnp.bfloat16)
    merge_kv = jnp.dot(
        merge_norm.reshape(-1, channels), w_merge_kv, preferred_element_type=jnp.float32
    ).astype(jnp.bfloat16)
    merge_kv = merge_kv.reshape(rows_dev, cols_dev, 2 * hidden)
    pair_ch = main_pair.shape[-1]
    main_query = (
        jnp.dot(main_pair.reshape(-1, pair_ch), w_merge_q, preferred_element_type=jnp.float32)
        * score_scale
    )
    main_query = main_query.reshape(rows_dev, cols_dev, head_count, head_dim)
    mask_tile = lax.dynamic_slice_in_dim(mask_rows, col_start, cols_dev, 1)
    own_cols = lax.dynamic_slice_in_dim(own_cover, col_start, cols_dev, 0)
    own_valid = cover_rows[:, None] * own_cols[None, :] * mask_tile
    shift_bias = MASK_SHIFT * (own_valid.astype(jnp.float32) - 1.0)
    keys_own = (
        merge_kv[..., :hidden].astype(jnp.float32).reshape(rows_dev, cols_dev, head_count, head_dim)
    )
    values_own = (
        merge_kv[..., hidden:].astype(jnp.float32).reshape(rows_dev, cols_dev, head_count, head_dim)
    )
    scores = jnp.sum(main_query * keys_own, axis=-1) + shift_bias[..., None]

    def combine(earlier, later):
        highest = jnp.maximum(earlier[0], later[0])
        early_scale = jnp.exp(earlier[0] - highest)
        late_scale = jnp.exp(later[0] - highest)
        return (
            highest,
            earlier[1] * early_scale + later[1] * late_scale,
            earlier[2] * early_scale[..., None] + later[2] * late_scale[..., None],
        )

    merged_state = combined_all((scores, jnp.ones_like(scores), values_own), "tmpl", combine)
    merged = merged_state[2] / merged_state[1][..., None]
    merged = merged.reshape(-1, hidden).astype(jnp.bfloat16)
    embedding = jnp.dot(merged, w_merge_out, preferred_element_type=jnp.float32).astype(
        jnp.bfloat16
    )
    return (new_pair[None], embedding.reshape(rows_dev, cols_dev, pair_ch))


LOG2E = 1.4426950408889634


def normed_rows(values, gain):
    center = values - jnp.mean(values, axis=0, keepdims=True)
    spread = jnp.mean(center * center, axis=0, keepdims=True)
    return (center * lax.rsqrt(spread + EPSILON) * gain).astype(jnp.bfloat16)


def piece_of(piece, idx_ref, pieces):
    half = idx_ref[0]
    odd = lax.rem(piece, 2)
    side = odd * half + (1 - odd) * (1 - half)
    return side * (pieces // 2) + piece // 2


def mask_shift(cover_ref, mask_ref, templ, row_block, col_block):
    valid = (
        cover_ref[row_block, templ] * cover_ref[col_block, templ] * mask_ref[row_block, col_block]
    )
    return MASK_SHIFT * (valid.astype(jnp.float32) - 1.0)


def matmul(lhs, rhs, lhs_dim=1, rhs_dim=0):
    return lax.dot_general(
        lhs, rhs, (((lhs_dim,), (rhs_dim,)), ((), ())), preferred_element_type=jnp.float32
    )


def widened(row_ref, cols):
    return jnp.broadcast_to(row_ref[...], (cols, row_ref.shape[1])).T


def norm_kernel(heads, idx_ref, x_ref, gain_ref, bias_w_ref, *refs):
    piece = pl.program_id(0)
    *kept_refs, bias_ref, held, wide = refs
    norm_refs, raw_refs = kept_refs[::2], kept_refs[1::2]

    @pl.when(piece == 0)
    def _():
        wide[...] = widened(gain_ref, wide.shape[1])

    step_rows = x_ref.shape[0]
    for chunk, (norm_ref, raw_ref) in enumerate(zip(norm_refs, raw_refs)):

        @pl.when(piece // 2 == chunk)
        def _():
            base = (piece - 2 * chunk) * step_rows
            for i in range(step_rows):
                raw_ref[base + i] = x_ref[i]
                norm_ref[base + i] = normed_rows(x_ref[i].astype(jnp.float32), wide[...])
            cols = x_ref.shape[2]
            wide_norm = jnp.concatenate([norm_ref[base + i] for i in range(step_rows)], axis=1)
            wide_bias = matmul(bias_w_ref[...], wide_norm)
            for i in range(step_rows):
                for head in range(heads):
                    held[head, i : i + 1, :] = wide_bias[head : head + 1, i * cols : (i + 1) * cols]

    first = pl.multiple_of(piece_of(piece, idx_ref, pl.num_programs(0)) * step_rows, step_rows)
    bias_ref[:, pl.ds(first, step_rows), :] = held[...].astype(jnp.bfloat16)


def weight_kernel(heads, idx_ref, project_ref, tri_out_ref, kv_ref, gain_ref, pack_ref, wide_ref):
    wide_ref[...] = widened(gain_ref, wide_ref.shape[1])
    channels = project_ref.shape[0]
    hidden = tri_out_ref.shape[0]
    dim = hidden // heads
    scale = dim ** (-0.5) * LOG2E
    project = project_ref[...]
    for head in range(heads):
        query = project[:, head * dim : (head + 1) * dim]
        key = project[:, hidden + head * dim : hidden + (head + 1) * dim]
        pack_ref[head * channels : (head + 1) * channels, :] = (
            matmul(key, query, 1, 1) * scale
        ).astype(jnp.bfloat16)
    row = heads * channels
    rest = (
        project[:, 3 * hidden :],
        project[:, 2 * hidden : 3 * hidden],
        tri_out_ref[...],
        kv_ref[...],
    )
    for part in rest:
        flipped = part.astype(jnp.float32).T.astype(jnp.bfloat16)
        pack_ref[row : row + flipped.shape[0], :] = flipped
        row += flipped.shape[0]


def when_held(idx_ref, column, part, tile_refs, tiles_per_col, act):
    wanted = idx_ref[2] ^ (tiles_per_col * column + part)
    for turn, tile_ref in enumerate(tile_refs):

        @pl.when(wanted == turn)
        def _():
            act(tile_ref)


def pick_kernel(idx_ref, *refs):
    *tile_refs, _, _, out_ref = refs
    for part in range(out_ref.shape[0]):

        def act(tile_ref, part=part):
            out_ref[part] = tile_ref[...]

        when_held(idx_ref, 1 - idx_ref[3], part, tile_refs, out_ref.shape[0], act)


def relative_shift(idx_ref, cover_ref, mask_ref, block):
    shifts = [mask_shift(cover_ref, mask_ref, idx_ref[1], idx_ref[4], b) for b in (block, 1 - block)]
    return shifts[0] - jnp.maximum(*shifts)


def place_bias(out_ref, part, tile, shift):
    heads, tile_rows, _ = tile.shape
    for head in range(heads):
        flipped = tile[head].astype(jnp.float32).T
        out_ref[head, :, part * tile_rows : (part + 1) * tile_rows] = (flipped + shift) * LOG2E


def own_bias_kernel(idx_ref, cover_ref, mask_ref, *refs):
    *tile_refs, out_ref = refs
    tiles_per_col = out_ref.shape[2] // tile_refs[0].shape[1]
    shift = relative_shift(idx_ref, cover_ref, mask_ref, idx_ref[3])
    for part in range(tiles_per_col):

        def act(tile_ref, part=part):
            place_bias(out_ref, part, tile_ref[...], shift)

        when_held(idx_ref, idx_ref[3], part, tile_refs, tiles_per_col, act)


def far_bias_kernel(idx_ref, cover_ref, mask_ref, tiles_ref, out_ref):
    shift = relative_shift(idx_ref, cover_ref, mask_ref, 1 - idx_ref[3])
    for part in range(tiles_ref.shape[0]):
        place_bias(out_ref, part, tiles_ref[part], shift)


def query_kernel(scale, idx_ref, main_ref, w_ref, out_ref):
    step_rows, cols, pair_ch = main_ref.shape
    base = pl.program_id(0) * step_rows
    wide = matmul(w_ref[...], main_ref[...].reshape(step_rows * cols, pair_ch), 1, 1) * scale
    for i in range(step_rows):
        out_ref[base + i] = wide[:, i * cols : (i + 1) * cols]


def attend_kernel(
    heads,
    skip,
    query_skip,
    x_ref,
    own_ref,
    far_ref,
    main_query,
    own_bias_ref,
    far_bias_ref,
    pack_ref,
    gain_ref,
    after_ref,
    out_ref,
    state_ref,
    turned,
    probes,
    gates,
    mixers,
    held,
    tops,
    gated,
):
    step_rows, channels, cols = out_ref.shape
    hidden = main_query.shape[1]
    dim = hidden // heads
    row = heads * channels + hidden
    first_w = pack_ref[:row, :]
    value_w = pack_ref[row : row + hidden, :]
    tri_w = pack_ref[row + hidden : row + hidden + channels, :]
    kv_w = pack_ref[row + hidden + channels :, :]
    for i in range(step_rows):
        own = own_ref[skip + i]
        both = jnp.concatenate([own, far_ref[skip + i]], axis=1)
        first = matmul(first_w, own)
        for h in range(heads):
            probes[i, h] = first[h * channels : (h + 1) * channels, :].astype(jnp.bfloat16)
        gates[i] = jax.nn.sigmoid(first[heads * channels :, :])
        values = matmul(value_w, both).astype(jnp.bfloat16)
        for h in range(heads):
            mixers[i, h, :dim, :] = values[h * dim : (h + 1) * dim, :]
            mixers[i, h, dim:, :] = jnp.ones((mixers.shape[2] - dim, both.shape[1]), jnp.bfloat16)
        turned[i] = both.T

    slots = held.shape[0]

    def score_row(i):
        for h in range(heads):
            scores = matmul(turned[i], probes[i, h])
            near = scores[:cols] + own_bias_ref[h]
            other = scores[cols:] + far_bias_ref[h]
            held[i % slots, h, :cols] = near
            held[i % slots, h, cols:] = other
            highest = jnp.max(jnp.maximum(near, other), axis=0, keepdims=True)
            tops[i % slots, h] = jnp.broadcast_to(highest, tops.shape[2:])

    def mix_row(i):
        for h in range(heads):
            weights = jnp.exp2(held[i % slots, h] - tops[i % slots, h][:1])
            mixed = matmul(mixers[i, h], weights.astype(jnp.bfloat16))
            span = slice(h * dim, (h + 1) * dim)
            gated[i, span, :] = (
                mixed[:dim] * (1.0 / mixed[dim : dim + 1]) * gates[i, span, :]
            ).astype(jnp.bfloat16)

    score_row(0)
    for i in range(step_rows):
        if i + 1 < step_rows:
            score_row(i + 1)
        mix_row(i)
    for i in range(step_rows):
        fresh = x_ref[skip + i].astype(jnp.float32) + matmul(tri_w, gated[i])
        out_ref[i] = fresh.astype(jnp.bfloat16)
    for i in range(step_rows):
        merge_norm = normed_rows(out_ref[i].astype(jnp.float32), gain_ref[...])
        merge_kv = matmul(kv_w, merge_norm).astype(jnp.bfloat16)
        product = main_query[query_skip + i] * merge_kv[:hidden, :].astype(jnp.float32)
        score = jnp.concatenate(
            [
                jnp.sum(product[h * dim : (h + 1) * dim, :], axis=0, keepdims=True)
                for h in range(heads)
            ],
            axis=0,
        )
        store_state(state_ref, i, merge_kv[hidden:, :], score)


def store_state(state_ref, i, values, score):
    hidden = values.shape[0]
    high = score.astype(jnp.bfloat16)
    low = (score - high.astype(jnp.float32)).astype(jnp.bfloat16)
    state_ref[i, :hidden, :] = values
    state_ref[i, hidden:, :] = jnp.concatenate([high, low], axis=0)


def spread_heads(per_head, dim):
    heads, cols = per_head.shape
    return jnp.concatenate(
        [jnp.broadcast_to(per_head[h : h + 1, :], (dim, cols)) for h in range(heads)], axis=0
    )


def joined(heads, first_ref, second_ref, i, first_shift, second_shift):
    hidden = first_ref.shape[1] - 2 * heads

    def parts(ref, shift):
        extra = ref[i, hidden:, :].astype(jnp.float32)
        return ref[i, :hidden, :].astype(jnp.float32), extra[:heads] + extra[heads:] + shift

    first_values, first_score = parts(first_ref, first_shift)
    second_values, second_score = parts(second_ref, second_shift)
    highest = jnp.maximum(first_score, second_score)
    first_weight = jnp.exp(first_score - highest)
    second_weight = jnp.exp(second_score - highest)
    total = first_weight + second_weight
    inverse = 1.0 / total
    dim = hidden // heads
    values = first_values * spread_heads(first_weight * inverse, dim)
    values = values + second_values * spread_heads(second_weight * inverse, dim)
    return values, highest + jnp.log(total)


def pair_shifts(idx_ref, cover_ref, mask_ref):
    templ, col_dev, row_block = idx_ref[1], idx_ref[3], idx_ref[4]
    even = templ - lax.rem(templ, 2)
    own = mask_shift(cover_ref, mask_ref, templ, row_block, col_dev)
    other = mask_shift(cover_ref, mask_ref, 2 * even + 1 - templ, row_block, col_dev)
    far = 2 - even
    far_best = jnp.maximum(
        mask_shift(cover_ref, mask_ref, far, row_block, col_dev),
        mask_shift(cover_ref, mask_ref, far + 1, row_block, col_dev),
    )
    best = jnp.maximum(own, other)
    return own - best, other - best, best, far_best


def core_join_kernel(heads, idx_ref, cover_ref, mask_ref, own_ref, other_ref, state_ref):
    own_shift, other_shift, _, _ = pair_shifts(idx_ref, cover_ref, mask_ref)
    for i in range(own_ref.shape[0]):
        values, score = joined(heads, own_ref, other_ref, i, own_shift, other_shift)
        store_state(state_ref, i, values.astype(jnp.bfloat16), score)


def chip_join_kernel(heads, idx_ref, cover_ref, mask_ref, own_ref, other_ref, _, merged_ref):
    _, _, best, far_best = pair_shifts(idx_ref, cover_ref, mask_ref)
    top = jnp.maximum(best, far_best)
    for i in range(own_ref.shape[0]):
        values, _ = joined(heads, own_ref, other_ref, i, best - top, far_best - top)
        merged_ref[i] = values.astype(jnp.bfloat16)


def embed_rows(merged_ref, w_ref, out_ref):
    for i in range(merged_ref.shape[0]):
        out_ref[i] = matmul(merged_ref[i], w_ref[...], 0, 0).astype(jnp.bfloat16)


def embed_kernel(idx_ref, merged_ref, w_ref, prior_ref, out_ref):
    embed_rows(merged_ref, w_ref, out_ref)


def finish_kernel(idx_ref, *refs):
    *row_refs, other_ref, own_ref, w_ref, fresh_ref, out_ref, token_ref = refs
    token_ref[...] = jnp.zeros_like(token_ref)
    for piece, row_ref in enumerate(row_refs):

        @pl.when(pl.program_id(0) == piece)
        def _():
            fresh_ref[...] = row_ref[...]
            if piece < 2:
                embed_rows((other_ref, own_ref)[piece], w_ref, out_ref)


def fused_on_device(
    templ_pair, main_pair, coverage, pair_mask, tri_gain, w_project, w_bias, w_tri_out,
    merge_gain, w_merge_q, w_merge_kv, w_merge_out,
):
    rows, cols, channels = templ_pair.shape[1:]
    hidden = w_tri_out.shape[0]
    heads = w_bias.shape[1]
    dim = hidden // heads
    pair_ch = main_pair.shape[-1]
    row_devs, col_devs = lax.axis_size("row"), lax.axis_size("col")
    tiles_per_col = row_devs // col_devs
    templ, row_dev, col_dev = (lax.axis_index(a) for a in ("tmpl", "row", "col"))
    idx = jnp.stack([templ % 2, templ, row_dev, col_dev, (row_dev * rows) // BLOCK]).astype(jnp.int32)
    pieces = PIECES
    piece_rows = rows // pieces
    step_rows = STEP_ROWS
    steps = piece_rows // step_rows
    stored = jnp.swapaxes(templ_pair[0], 1, 2)
    bf16, f32 = jnp.bfloat16, jnp.float32
    def in_hbm(array):
        return pltpu.with_memory_space_constraint(array, pltpu.HBM)

    gain_row = in_hbm(tri_gain[None, :])
    cover = coverage.T
    stored, main_pair = in_hbm(stored), in_hbm(main_pair)

    def whole(array):
        return pl.BlockSpec(array.shape, lambda *_: (0,) * array.ndim)

    smem = pl.BlockSpec(memory_space=pltpu.SMEM)
    vmem = pl.BlockSpec(memory_space=pltpu.VMEM)
    anywhere = pl.BlockSpec(memory_space=pl.ANY)

    def call(kernel, grid, in_specs, out_specs, out_shape, scratch=(), aliases=None, cost=1e6):
        return pl.pallas_call(
            kernel,
            grid_spec=pltpu.PrefetchScalarGridSpec(
                num_scalar_prefetch=1, grid=grid, in_specs=in_specs, out_specs=out_specs,
                scratch_shapes=list(scratch),
            ),
            out_shape=out_shape,
            input_output_aliases=aliases or {},
            cost_estimate=pl.CostEstimate(
                flops=int(cost), bytes_accessed=1 << 20, transcendentals=0
            ),
            compiler_params=pltpu.CompilerParams(vmem_limit_bytes=VMEM_GRANT),
        )

    chunks = pieces // 2

    *kept_rows, bias_tile = call(
        functools.partial(norm_kernel, heads),
        (pieces,),
        [
            pl.BlockSpec((piece_rows, channels, cols), lambda p, s: (piece_of(p, s, pieces), 0, 0)),
            whole(gain_row),
            pl.BlockSpec((heads, channels), lambda *_: (0, 0)),
        ],
        [vmem] * (2 * chunks + 1),
        [jax.ShapeDtypeStruct((2 * piece_rows, channels, cols), bf16)] * (2 * chunks)
        + [jax.ShapeDtypeStruct((heads, rows, cols), bf16)],
        [pltpu.VMEM((heads, piece_rows, cols), f32), pltpu.VMEM((channels, cols), f32)],
    )(idx, stored, gain_row, in_hbm(w_bias.T))
    norms, raws = kept_rows[::2], kept_rows[1::2]


    def plain_call(kernel, in_specs, out_shape, scratch=(), cost=1e6):
        return pl.pallas_call(
            kernel,
            in_specs=in_specs,
            out_specs=jax.tree.map(lambda _: vmem, out_shape),
            out_shape=out_shape,
            scratch_shapes=list(scratch),
            cost_estimate=pl.CostEstimate(
                flops=int(cost), bytes_accessed=1 << 20, transcendentals=0
            ),
            compiler_params=pltpu.CompilerParams(vmem_limit_bytes=VMEM_GRANT),
        )

    tiles = [bias_tile]
    for turn in range(1, row_devs):
        perm = [(z, z ^ turn) for z in range(row_devs)]
        tiles.append(lax.ppermute(bias_tile, "row", perm))
    swap = [(c, col_devs - 1 - c) for c in range(col_devs)]
    fars = [lax.ppermute(norms[0], "col", swap)]
    pack_shape = (heads * channels + 2 * hidden + channels + 2 * hidden, channels)
    raw_weights = [in_hbm(w) for w in (w_project, w_tri_out, w_merge_kv, merge_gain[None, :])]
    packed_shapes = [
        jax.ShapeDtypeStruct(pack_shape, bf16),
        jax.ShapeDtypeStruct((channels, cols), f32),
    ]
    with jax.named_scope("pack"):
        pack, merge_gain_wide = call(
            functools.partial(weight_kernel, heads),
            (1,),
            [whole(w) for w in raw_weights],
            [vmem] * len(packed_shapes),
            packed_shapes,
        )(idx, *raw_weights)
    query_w = in_hbm(w_merge_q.T)
    query_w = in_hbm(w_merge_q.T)
    with jax.named_scope("query"):
        main_query = call(
            functools.partial(query_kernel, dim ** (-0.5)),
            (pieces,),
            [
                pl.BlockSpec(
                    (piece_rows, cols, pair_ch),
                    lambda g, s: (piece_of(g, s, pieces), 0, 0),
                ),
                whole(query_w),
            ],
            vmem,
            jax.ShapeDtypeStruct((rows, hidden, cols), f32),
        )(idx, main_pair, query_w)
    picked = plain_call(
        pick_kernel,
        [smem] + [vmem] * row_devs + [anywhere] * 2,
        jax.ShapeDtypeStruct((tiles_per_col,) + bias_tile.shape, bf16),
    )(idx, *tiles, pack, main_query)
    far_tiles = lax.ppermute(picked, "col", swap)
    half_shape = jax.ShapeDtypeStruct((heads, cols, cols), f32)
    own_bias = plain_call(own_bias_kernel, [smem] * 3 + [vmem] * row_devs, half_shape)(
        idx, cover, pair_mask, *tiles
    )
    far_bias = plain_call(far_bias_kernel, [smem] * 3 + [vmem], half_shape)(
        idx, cover, pair_mask, far_tiles
    )
    fars += [lax.ppermute(norm, "col", swap) for norm in norms[1:]]

    fresh, states, pair_states = [], [], []
    after = far_bias
    cores = [(t, t + 1 - 2 * (t % 2)) for t in range(lax.axis_size("tmpl"))]
    chips = [(t, (t + 2) % 4) for t in range(lax.axis_size("tmpl"))]
    state_shape = jax.ShapeDtypeStruct((piece_rows, hidden + 2 * heads, cols), bf16)
    for piece in range(pieces):
        chunk, side = piece // 2, piece % 2
        with jax.named_scope("attend%d" % piece):
            rows_out, state = plain_call(
                functools.partial(attend_kernel, heads, side * piece_rows, piece * piece_rows),
                [vmem] * 8 + [anywhere],
                [jax.ShapeDtypeStruct((piece_rows, channels, cols), bf16), state_shape],
                [
                    pltpu.VMEM((piece_rows, col_devs * cols, channels), bf16),
                    pltpu.VMEM((piece_rows, heads, channels, cols), bf16),
                    pltpu.VMEM((piece_rows, hidden, cols), f32),
                    pltpu.VMEM((piece_rows, heads, 2 * dim, col_devs * cols), bf16),
                    pltpu.VMEM((2, heads, col_devs * cols, cols), f32),
                    pltpu.VMEM((2, heads, 8, cols), f32),
                    pltpu.VMEM((piece_rows, hidden, cols), bf16),
                ],
                6e9,
            )(
                raws[chunk], norms[chunk], fars[chunk], main_query, own_bias, far_bias, pack,
                merge_gain_wide, after,
            )
        fresh.append(rows_out)
        states.append(state)
        after = state
        if side:
            with jax.named_scope("corejoin%d" % chunk):
                after = plain_call(
                    functools.partial(core_join_kernel, heads),
                    [smem] * 3 + [vmem] * 2,
                    state_shape,
                )(idx, cover, pair_mask, state, swapped)
            pair_states.append(after)
        else:
            with jax.named_scope("coreswap%d" % chunk):
                swapped = lax.ppermute(state, "tmpl", cores)

    emb_shape = jax.ShapeDtypeStruct(main_pair.shape, bf16)
    token = pair_states[-1]
    token_shape = jax.ShapeDtypeStruct((8, cols), f32)
    merged_shape = jax.ShapeDtypeStruct((piece_rows, hidden, cols), bf16)
    for chunk in range(chunks):
        pair_state = pair_states[chunk]
        with jax.named_scope("chipswap%d" % chunk):
            far_state = lax.ppermute(pair_state, "tmpl", chips)
        with jax.named_scope("chipjoin%d" % chunk):
            merged = plain_call(
                functools.partial(chip_join_kernel, heads),
                [smem] * 3 + [vmem] * 2 + [anywhere],
                merged_shape,
            )(idx, cover, pair_mask, pair_state, far_state, token)
        with jax.named_scope("lastswap%d" % chunk):
            merged_other = lax.ppermute(merged, "tmpl", cores)

        def at_piece(piece):
            return lambda g, s: (piece_of(piece, s, pieces), 0, 0)

        if chunk == 0:
            with jax.named_scope("finish"):
                out, emb, token = call(
                    finish_kernel,
                    (pieces,),
                    [vmem] * (pieces + 3),
                    [
                        pl.BlockSpec(
                            (piece_rows, channels, cols),
                            lambda g, s: (piece_of(g, s, pieces), 0, 0),
                        ),
                        pl.BlockSpec(
                            (piece_rows, cols, pair_ch),
                            lambda g, s: (piece_of(jnp.minimum(g, 1), s, pieces), 0, 0),
                        ),
                        vmem,
                    ],
                    [jax.ShapeDtypeStruct(stored.shape, bf16), emb_shape, token_shape],
                )(idx, *fresh, merged_other, merged, w_merge_out)
        else:
            for piece, part in ((2 * chunk + 1, merged), (2 * chunk, merged_other)):
                with jax.named_scope("embed%d" % piece):
                    emb = call(
                        embed_kernel,
                        (1,),
                        [vmem, vmem, anywhere],
                        pl.BlockSpec((piece_rows, cols, pair_ch), at_piece(piece)),
                        emb_shape,
                        aliases={3: 0},
                    )(idx, part, w_merge_out, emb)
    return (jnp.swapaxes(out, 1, 2)[None], emb)


PIECES = 4
VMEM_GRANT = 16 << 20
STEP_ROWS = 8


def takes_fused(templ_pair, main_pair):
    rows, cols = templ_pair.shape[1:3]
    row_devs, col_devs = lax.axis_size("row"), lax.axis_size("col")
    return (
        lax.axis_size("tmpl") == 4
        and col_devs == 2
        and cols == BLOCK
        and BLOCK % rows == 0
        and row_devs & (row_devs - 1) == 0
        and row_devs % col_devs == 0
        and rows * (row_devs // col_devs) == cols
        and rows % (PIECES * STEP_ROWS) == 0
    )


def on_device(*operands):
    if takes_fused(*operands[:2]):
        return fused_on_device(*operands)
    return plain_on_device(*operands)


def solution(mesh):
    in_specs = (
        P("tmpl", "row", "col", None),
        P("row", "col", None),
        P(),
        P(),
        P(),
        P(),
        P(),
        P(),
        P(),
        P(),
        P(),
        P(),
    )
    out_specs = (P("tmpl", "row", "col", None), P("row", "col", None))
    return jax.shard_map(
        on_device, mesh=mesh, in_specs=in_specs, out_specs=out_specs, check_vma=False
    )
```

```python
import functools

import jax
import jax.numpy as jnp
from jax import lax
from jax.experimental import pallas as pl
from jax.experimental.pallas import tpu as pltpu
from jax.sharding import PartitionSpec as P

BLOCK = 128


MASK_SHIFT = 10000.0
EPSILON = 1e-05
NEG_START = -1e30


def combined_all(part, axis, combine):
    gathered = jax.tree.map(lambda a: lax.all_gather(a, axis), part)

    def take(source):
        return jax.tree.map(lambda a: lax.dynamic_index_in_dim(a, source, 0, False), gathered)

    return lax.fori_loop(
        1, lax.axis_size(axis), lambda source, state: combine(state, take(source)), take(0)
    )


def layer_norm(values, scale_gain):
    values = values.astype(jnp.float32)
    center = values - jnp.mean(values, axis=-1, keepdims=True)
    spread = jnp.mean(center * center, axis=-1, keepdims=True)
    return center * lax.rsqrt(spread + EPSILON) * scale_gain


def row_group(rows_dev, cols_dev):
    chosen = 1
    for candidate in range(1, rows_dev + 1):
        if rows_dev % candidate == 0 and candidate * cols_dev <= 2048:
            chosen = candidate
    return chosen


def plain_on_device(
    templ_pair,
    main_pair,
    coverage,
    pair_mask,
    tri_gain,
    w_project,
    w_bias,
    w_tri_out,
    merge_gain,
    w_merge_q,
    w_merge_kv,
    w_merge_out,
):
    pair_tile = templ_pair[0]
    rows_dev, cols_dev, channels = pair_tile.shape
    hidden = w_tri_out.shape[0]
    head_count = w_bias.shape[1]
    head_dim = hidden // head_count
    score_scale = head_dim ** (-0.5)
    row_start = lax.axis_index("row") * rows_dev
    col_start = lax.axis_index("col") * cols_dev
    templ_index = lax.axis_index("tmpl")
    cover_tok = jnp.repeat(coverage, BLOCK, axis=1)
    own_cover = lax.dynamic_index_in_dim(cover_tok, templ_index, 0, keepdims=False)
    mask_full = jnp.repeat(jnp.repeat(pair_mask, BLOCK, axis=0), BLOCK, axis=1)
    mask_rows = lax.dynamic_slice_in_dim(mask_full, row_start, rows_dev, 0)
    cover_rows = lax.dynamic_slice_in_dim(own_cover, row_start, rows_dev, 0)
    normed = layer_norm(pair_tile, tri_gain).astype(jnp.bfloat16)
    flat_norm = normed.reshape(-1, channels)
    w_query_gate = jnp.concatenate([w_project[:, :hidden], w_project[:, 3 * hidden :]], axis=1)
    query_gate = jnp.dot(flat_norm, w_query_gate, preferred_element_type=jnp.float32).reshape(
        rows_dev, cols_dev, 2 * hidden
    )
    queries = (
        (query_gate[..., :hidden] * score_scale)
        .astype(jnp.bfloat16)
        .reshape(rows_dev, cols_dev, head_count, head_dim)
    )
    gate_values = jax.nn.sigmoid(query_gate[..., hidden:])
    bias_tile = jnp.dot(flat_norm, w_bias, preferred_element_type=jnp.float32).astype(jnp.bfloat16)
    bias_tile = jnp.transpose(bias_tile.reshape(rows_dev, cols_dev, head_count), (2, 0, 1))
    bias_column = lax.all_gather(bias_tile, "row", axis=1, tiled=True)
    bias_slab = lax.all_to_all(bias_column, "col", split_axis=1, concat_axis=2, tiled=True)
    bias_rows = jnp.transpose(bias_slab, (1, 0, 2)).astype(jnp.float32)
    key_shift = MASK_SHIFT * (
        (cover_rows[:, None] * own_cover[None, :] * mask_rows).astype(jnp.float32) - 1.0
    )
    w_key_value = w_project[:, hidden : 3 * hidden]
    group = row_group(rows_dev, cols_dev)
    splits = rows_dev // group

    def grouped(array):
        return array.reshape((splits, group) + array.shape[1:])

    start_state = (
        jnp.full((rows_dev, cols_dev, head_count), NEG_START, jnp.float32),
        jnp.zeros((rows_dev, cols_dev, head_count), jnp.float32),
        jnp.zeros((rows_dev, cols_dev, head_count, head_dim), jnp.float32),
    )
    norm_piece = lax.all_gather(normed, "col", axis=1, tiled=True)
    piece_width = norm_piece.shape[1]

    def one_group(group_args):
        query_part, norm_part, shift_part, maxima, totals, weighted = group_args
        key_value = jnp.dot(
            norm_part.reshape(-1, channels), w_key_value, preferred_element_type=jnp.float32
        ).astype(jnp.bfloat16)
        key_value = key_value.reshape(group, piece_width, 2 * hidden)
        key_part = key_value[..., :hidden].reshape(group, piece_width, head_count, head_dim)
        value_part = key_value[..., hidden:].reshape(group, piece_width, head_count, head_dim)
        scores = jnp.einsum(
            "ijhd,ikhd->ijhk", query_part, key_part, preferred_element_type=jnp.float32
        )
        scores = scores + bias_rows[None] + shift_part[:, None, None, :]
        highest = jnp.maximum(maxima, jnp.max(scores, axis=-1))
        rescale = jnp.exp(maxima - highest)
        weights = jnp.exp(scores - highest[..., None])
        totals = totals * rescale + jnp.sum(weights, axis=-1)
        summed = jnp.einsum(
            "ijhk,ikhd->ijhd",
            weights.astype(jnp.bfloat16),
            value_part,
            preferred_element_type=jnp.float32,
        )
        weighted = weighted * rescale[..., None] + summed
        return (highest, totals, weighted)

    outcome = lax.map(
        one_group,
        (
            grouped(queries),
            grouped(norm_piece),
            grouped(key_shift),
            grouped(start_state[0]),
            grouped(start_state[1]),
            grouped(start_state[2]),
        ),
    )
    result = tuple((member.reshape((rows_dev,) + member.shape[2:]) for member in outcome))
    attended = result[2] / result[1][..., None]
    gated = (attended.reshape(rows_dev, cols_dev, hidden) * gate_values).astype(jnp.bfloat16)
    projected = jnp.dot(
        gated.reshape(-1, hidden), w_tri_out, preferred_element_type=jnp.float32
    ).reshape(rows_dev, cols_dev, channels)
    new_pair = (pair_tile.astype(jnp.float32) + projected).astype(jnp.bfloat16)
    merge_norm = layer_norm(new_pair, merge_gain).astype(jnp.bfloat16)
    merge_kv = jnp.dot(
        merge_norm.reshape(-1, channels), w_merge_kv, preferred_element_type=jnp.float32
    ).astype(jnp.bfloat16)
    merge_kv = merge_kv.reshape(rows_dev, cols_dev, 2 * hidden)
    pair_ch = main_pair.shape[-1]
    main_query = (
        jnp.dot(main_pair.reshape(-1, pair_ch), w_merge_q, preferred_element_type=jnp.float32)
        * score_scale
    )
    main_query = main_query.reshape(rows_dev, cols_dev, head_count, head_dim)
    mask_tile = lax.dynamic_slice_in_dim(mask_rows, col_start, cols_dev, 1)
    own_cols = lax.dynamic_slice_in_dim(own_cover, col_start, cols_dev, 0)
    own_valid = cover_rows[:, None] * own_cols[None, :] * mask_tile
    shift_bias = MASK_SHIFT * (own_valid.astype(jnp.float32) - 1.0)
    keys_own = (
        merge_kv[..., :hidden].astype(jnp.float32).reshape(rows_dev, cols_dev, head_count, head_dim)
    )
    values_own = (
        merge_kv[..., hidden:].astype(jnp.float32).reshape(rows_dev, cols_dev, head_count, head_dim)
    )
    scores = jnp.sum(main_query * keys_own, axis=-1) + shift_bias[..., None]

    def combine(earlier, later):
        highest = jnp.maximum(earlier[0], later[0])
        early_scale = jnp.exp(earlier[0] - highest)
        late_scale = jnp.exp(later[0] - highest)
        return (
            highest,
            earlier[1] * early_scale + later[1] * late_scale,
            earlier[2] * early_scale[..., None] + later[2] * late_scale[..., None],
        )

    merged_state = combined_all((scores, jnp.ones_like(scores), values_own), "tmpl", combine)
    merged = merged_state[2] / merged_state[1][..., None]
    merged = merged.reshape(-1, hidden).astype(jnp.bfloat16)
    embedding = jnp.dot(merged, w_merge_out, preferred_element_type=jnp.float32).astype(
        jnp.bfloat16
    )
    return (new_pair[None], embedding.reshape(rows_dev, cols_dev, pair_ch))


LOG2E = 1.4426950408889634


def normed_rows(values, gain):
    center = values - jnp.mean(values, axis=0, keepdims=True)
    spread = jnp.mean(center * center, axis=0, keepdims=True)
    return (center * lax.rsqrt(spread + EPSILON) * gain).astype(jnp.bfloat16)


def places(rows):
    templ, row_dev, col_dev = (lax.axis_index(axis) for axis in ("tmpl", "row", "col"))
    return lax.rem(templ, 2), templ, row_dev, col_dev, row_dev * rows // BLOCK


def piece_of(piece, idx_ref, pieces):
    half = idx_ref[0]
    odd = lax.rem(piece, 2)
    side = odd * half + (1 - odd) * (1 - half)
    return side * (pieces // 2) + piece // 2


def mask_shift(cover_ref, mask_ref, templ, row_block, col_block):
    valid = (
        cover_ref[row_block, templ] * cover_ref[col_block, templ] * mask_ref[row_block, col_block]
    )
    return MASK_SHIFT * (valid.astype(jnp.float32) - 1.0)


def matmul(lhs, rhs, lhs_dim=1, rhs_dim=0):
    return lax.dot_general(
        lhs, rhs, (((lhs_dim,), (rhs_dim,)), ((), ())), preferred_element_type=jnp.float32
    )


def widened(row_ref, cols):
    return jnp.broadcast_to(row_ref[...], (cols, row_ref.shape[1])).T


def norm_kernel(heads, x_hbm, gain_hbm, bias_w_hbm, *refs):
    *kept_refs, bias_ref, held, wide, x_ref, gain_ref, bias_w_ref, done = refs
    norm_refs, raw_refs = kept_refs[::2], kept_refs[1::2]
    pieces, step_rows, _, cols = x_ref.shape
    idx_ref = places(pieces * step_rows)
    small = [
        pltpu.make_async_copy(gain_hbm, gain_ref, done.at[pieces]),
        pltpu.make_async_copy(bias_w_hbm, bias_w_ref, done.at[pieces + 1]),
    ]
    firsts = [
        pl.multiple_of(piece_of(piece, idx_ref, pieces) * step_rows, step_rows)
        for piece in range(pieces)
    ]
    copies = [
        pltpu.make_async_copy(x_hbm.at[pl.ds(first, step_rows)], x_ref.at[piece], done.at[piece])
        for piece, first in enumerate(firsts)
    ]
    for copy in small + copies:
        copy.start()
    for copy in small:
        copy.wait()
    wide[...] = widened(gain_ref, cols)
    for piece in range(pieces):
        copies[piece].wait()
        base = piece % 2 * step_rows
        norm_ref, raw_ref = norm_refs[piece // 2], raw_refs[piece // 2]
        for i in range(step_rows):
            raw_ref[base + i] = x_ref[piece, i]
            norm_ref[base + i] = normed_rows(x_ref[piece, i].astype(jnp.float32), wide[...])
        wide_norm = jnp.concatenate([norm_ref[base + i] for i in range(step_rows)], axis=1)
        wide_bias = matmul(bias_w_ref[...], wide_norm)
        for i in range(step_rows):
            for head in range(heads):
                held[piece, head, i : i + 1, :] = wide_bias[
                    head : head + 1, i * cols : (i + 1) * cols
                ]
        bias_ref[:, pl.ds(firsts[piece], step_rows), :] = held[piece].astype(jnp.bfloat16)


def weight_kernel(
    heads, idx_ref, project_ref, tri_out_ref, kv_ref, gain_ref, cover_ref, mask_ref, pack_ref, wide_ref, table_ref
):
    for line, shift in enumerate(all_shifts(idx_ref, cover_ref, mask_ref)):
        table_ref[line : line + 1, :] = jnp.full((1, table_ref.shape[1]), shift, jnp.float32)
    wide_ref[...] = widened(gain_ref, wide_ref.shape[1])
    channels = project_ref.shape[0]
    hidden = tri_out_ref.shape[0]
    dim = hidden // heads
    scale = dim ** (-0.5) * LOG2E
    project = project_ref[...]
    for head in range(heads):
        query = project[:, head * dim : (head + 1) * dim]
        key = project[:, hidden + head * dim : hidden + (head + 1) * dim]
        pack_ref[head * channels : (head + 1) * channels, :] = (
            matmul(key, query, 1, 1) * scale
        ).astype(jnp.bfloat16)
    row = heads * channels
    rest = (
        project[:, 3 * hidden :],
        project[:, 2 * hidden : 3 * hidden],
        tri_out_ref[...],
        kv_ref[...],
    )
    for part in rest:
        flipped = part.astype(jnp.float32).T.astype(jnp.bfloat16)
        pack_ref[row : row + flipped.shape[0], :] = flipped
        row += flipped.shape[0]


def when_held(idx_ref, column, part, tile_refs, tiles_per_col, act):
    wanted = idx_ref[2] ^ (tiles_per_col * column + part)
    for turn, tile_ref in enumerate(tile_refs):

        @pl.when(wanted == turn)
        def _():
            act(tile_ref)


def pick_kernel(*refs):
    *tile_refs, _, _, out_ref = refs
    idx_ref = places(tile_refs[0].shape[1])
    for part in range(out_ref.shape[0]):

        def act(tile_ref, part=part):
            out_ref[part] = tile_ref[...]

        when_held(idx_ref, 1 - idx_ref[3], part, tile_refs, out_ref.shape[0], act)


def relative_shift(idx_ref, cover_ref, mask_ref, block):
    shifts = [mask_shift(cover_ref, mask_ref, idx_ref[1], idx_ref[4], b) for b in (block, 1 - block)]
    return shifts[0] - jnp.maximum(*shifts)


def all_shifts(idx_ref, cover_ref, mask_ref):
    own, other, best, far_best = pair_shifts(idx_ref, cover_ref, mask_ref)
    top = jnp.maximum(best, far_best)
    blocks = (idx_ref[3], 1 - idx_ref[3])
    return [relative_shift(idx_ref, cover_ref, mask_ref, block) for block in blocks] + [
        own,
        other,
        best - top,
        far_best - top,
    ]


def place_bias(out_ref, part, tile, shift):
    heads, tile_rows, _ = tile.shape
    for head in range(heads):
        flipped = tile[head].astype(jnp.float32).T
        out_ref[head, :, part * tile_rows : (part + 1) * tile_rows] = (flipped + shift) * LOG2E


def own_bias_kernel(table_ref, *refs):
    *tile_refs, out_ref = refs
    idx_ref = places(tile_refs[0].shape[1])
    tiles_per_col = out_ref.shape[2] // tile_refs[0].shape[1]
    shift = table_ref[0:1, : tile_refs[0].shape[1]]
    for part in range(tiles_per_col):

        def act(tile_ref, part=part):
            place_bias(out_ref, part, tile_ref[...], shift)

        when_held(idx_ref, idx_ref[3], part, tile_refs, tiles_per_col, act)


def far_bias_kernel(table_ref, tiles_ref, _, out_ref):
    shift = table_ref[1:2, : tiles_ref.shape[2]]
    for part in range(tiles_ref.shape[0]):
        place_bias(out_ref, part, tiles_ref[part], shift)


def query_kernel(scale, idx_ref, main_ref, w_ref, out_ref):
    step_rows, cols, pair_ch = main_ref.shape
    base = pl.program_id(0) * step_rows
    wide = matmul(w_ref[...], main_ref[...].reshape(step_rows * cols, pair_ch), 1, 1) * scale
    for i in range(step_rows):
        out_ref[base + i] = wide[:, i * cols : (i + 1) * cols]


def split_pack(pack_ref, heads, hidden):
    channels = pack_ref.shape[1]
    ends = [heads * channels]
    for size in (hidden, hidden, channels):
        ends.append(ends[-1] + size)
    return ends


def near_kernel(
    heads, skip, own_ref, own_bias_ref, pack_ref, after_ref, probes, gates, own_mix, near, near_tops, turned
):
    step_rows, _, channels, cols = probes.shape
    ends = split_pack(pack_ref, heads, gates.shape[1])
    for i in range(step_rows):
        own = own_ref[skip + i]
        first = matmul(pack_ref[: ends[2], :], own)
        for h in range(heads):
            probes[i, h] = first[h * channels : (h + 1) * channels, :].astype(jnp.bfloat16)
        gates[i] = jax.nn.sigmoid(first[ends[0] : ends[1], :])
        own_mix[i] = first[ends[1] :, :].astype(jnp.bfloat16)
        turned[i] = own.T
    for i in range(step_rows):
        for h in range(heads):
            scores = matmul(turned[i], probes[i, h]) + own_bias_ref[h]
            near[i, h] = scores
            near_tops[i, h] = jnp.broadcast_to(
                jnp.max(scores, axis=0, keepdims=True), near_tops.shape[2:]
            )


def late_kernel(
    heads,
    skip,
    query_skip,
    x_ref,
    far_ref,
    main_query,
    far_bias_ref,
    pack_ref,
    gain_ref,
    probes,
    gates,
    own_mix,
    near,
    near_tops,
    after_ref,
    out_ref,
    state_ref,
    turned,
    mixers,
    held,
    tops,
    gated,
):
    step_rows, channels, cols = out_ref.shape
    hidden = main_query.shape[1]
    dim = hidden // heads
    ends = split_pack(pack_ref, heads, hidden)
    value_w = pack_ref[ends[1] : ends[2], :]
    for i in range(step_rows):
        far = far_ref[skip + i]
        values = matmul(value_w, far).astype(jnp.bfloat16)
        for h in range(heads):
            span = slice(h * dim, (h + 1) * dim)
            mixers[i, h, :dim, :cols] = own_mix[i, span, :]
            mixers[i, h, :dim, cols:] = values[span, :]
            mixers[i, h, dim:, :] = jnp.ones((mixers.shape[2] - dim, 2 * cols), jnp.bfloat16)
        turned[i] = far.T

    slots = held.shape[0]

    def score_row(i):
        for h in range(heads):
            scores = matmul(turned[i], probes[i, h]) + far_bias_ref[h]
            held[i % slots, h] = scores
            highest = jnp.max(scores, axis=0, keepdims=True)
            tops[i % slots, h] = jnp.maximum(near_tops[i, h], highest)

    def mix_row(i):
        for h in range(heads):
            top = tops[i % slots, h][:1]
            weights = jnp.concatenate(
                [
                    jnp.exp2(part - top).astype(jnp.bfloat16)
                    for part in (near[i, h], held[i % slots, h])
                ],
                axis=0,
            )
            mixed = matmul(mixers[i, h], weights)
            span = slice(h * dim, (h + 1) * dim)
            gated[i, span, :] = (
                mixed[:dim] * (1.0 / mixed[dim : dim + 1]) * gates[i, span, :]
            ).astype(jnp.bfloat16)

    score_row(0)
    for i in range(step_rows):
        if i + 1 < step_rows:
            score_row(i + 1)
        mix_row(i)
    write_rows(
        heads, skip, query_skip, x_ref, main_query, pack_ref, gain_ref, gated, out_ref, state_ref
    )


def attend_kernel(
    heads,
    skip,
    query_skip,
    x_ref,
    own_ref,
    far_ref,
    main_query,
    own_bias_ref,
    far_bias_ref,
    pack_ref,
    gain_ref,
    after_ref,
    out_ref,
    state_ref,
    turned,
    probes,
    gates,
    mixers,
    held,
    tops,
    gated,
):
    step_rows, channels, cols = out_ref.shape
    hidden = main_query.shape[1]
    dim = hidden // heads
    row = heads * channels + hidden
    first_w = pack_ref[:row, :]
    value_w = pack_ref[row : row + hidden, :]
    for i in range(step_rows):
        own = own_ref[skip + i]
        both = jnp.concatenate([own, far_ref[skip + i]], axis=1)
        first = matmul(first_w, own)
        for h in range(heads):
            probes[i, h] = first[h * channels : (h + 1) * channels, :].astype(jnp.bfloat16)
        gates[i] = jax.nn.sigmoid(first[heads * channels :, :])
        values = matmul(value_w, both).astype(jnp.bfloat16)
        for h in range(heads):
            mixers[i, h, :dim, :] = values[h * dim : (h + 1) * dim, :]
            mixers[i, h, dim:, :] = jnp.ones((mixers.shape[2] - dim, both.shape[1]), jnp.bfloat16)
        turned[i] = both.T

    slots = held.shape[0]

    def score_row(i):
        for h in range(heads):
            scores = matmul(turned[i], probes[i, h])
            near = scores[:cols] + own_bias_ref[h]
            other = scores[cols:] + far_bias_ref[h]
            held[i % slots, h, :cols] = near
            held[i % slots, h, cols:] = other
            highest = jnp.max(jnp.maximum(near, other), axis=0, keepdims=True)
            tops[i % slots, h] = jnp.broadcast_to(highest, tops.shape[2:])

    def mix_row(i):
        for h in range(heads):
            weights = jnp.exp2(held[i % slots, h] - tops[i % slots, h][:1])
            mixed = matmul(mixers[i, h], weights.astype(jnp.bfloat16))
            span = slice(h * dim, (h + 1) * dim)
            gated[i, span, :] = (
                mixed[:dim] * (1.0 / mixed[dim : dim + 1]) * gates[i, span, :]
            ).astype(jnp.bfloat16)

    score_row(0)
    for i in range(step_rows):
        if i + 1 < step_rows:
            score_row(i + 1)
        mix_row(i)
    write_rows(
        heads, skip, query_skip, x_ref, main_query, pack_ref, gain_ref, gated, out_ref, state_ref
    )


def write_rows(
    heads, skip, query_skip, x_ref, main_query, pack_ref, gain_ref, gated, out_ref, state_ref
):
    step_rows = out_ref.shape[0]
    hidden = gated.shape[1]
    dim = hidden // heads
    ends = split_pack(pack_ref, heads, hidden)
    tri_w = pack_ref[ends[2] : ends[3], :]
    kv_w = pack_ref[ends[3] :, :]
    for i in range(step_rows):
        fresh = x_ref[skip + i].astype(jnp.float32) + matmul(tri_w, gated[i])
        out_ref[i] = fresh.astype(jnp.bfloat16)
    for i in range(step_rows):
        merge_norm = normed_rows(out_ref[i].astype(jnp.float32), gain_ref[...])
        merge_kv = matmul(kv_w, merge_norm).astype(jnp.bfloat16)
        product = main_query[query_skip + i] * merge_kv[:hidden, :].astype(jnp.float32)
        score = jnp.concatenate(
            [
                jnp.sum(product[h * dim : (h + 1) * dim, :], axis=0, keepdims=True)
                for h in range(heads)
            ],
            axis=0,
        )
        store_state(state_ref, i, merge_kv[hidden:, :], score)


def store_state(state_ref, i, values, score):
    hidden = values.shape[0]
    high = score.astype(jnp.bfloat16)
    low = (score - high.astype(jnp.float32)).astype(jnp.bfloat16)
    state_ref[i, :hidden, :] = values
    state_ref[i, hidden:, :] = jnp.concatenate([high, low], axis=0)


def spread_heads(per_head, dim):
    heads, cols = per_head.shape
    return jnp.concatenate(
        [jnp.broadcast_to(per_head[h : h + 1, :], (dim, cols)) for h in range(heads)], axis=0
    )


def joined(heads, first_ref, second_ref, i, first_shift, second_shift):
    hidden = first_ref.shape[1] - 2 * heads

    def parts(ref, shift):
        extra = ref[i, hidden:, :].astype(jnp.float32)
        return ref[i, :hidden, :].astype(jnp.float32), extra[:heads] + extra[heads:] + shift

    first_values, first_score = parts(first_ref, first_shift)
    second_values, second_score = parts(second_ref, second_shift)
    highest = jnp.maximum(first_score, second_score)
    first_weight = jnp.exp(first_score - highest)
    second_weight = jnp.exp(second_score - highest)
    total = first_weight + second_weight
    inverse = 1.0 / total
    dim = hidden // heads
    values = first_values * spread_heads(first_weight * inverse, dim)
    values = values + second_values * spread_heads(second_weight * inverse, dim)
    return values, highest + jnp.log(total)


def pair_shifts(idx_ref, cover_ref, mask_ref):
    templ, col_dev, row_block = idx_ref[1], idx_ref[3], idx_ref[4]
    even = templ - lax.rem(templ, 2)
    own = mask_shift(cover_ref, mask_ref, templ, row_block, col_dev)
    other = mask_shift(cover_ref, mask_ref, 2 * even + 1 - templ, row_block, col_dev)
    far = 2 - even
    far_best = jnp.maximum(
        mask_shift(cover_ref, mask_ref, far, row_block, col_dev),
        mask_shift(cover_ref, mask_ref, far + 1, row_block, col_dev),
    )
    best = jnp.maximum(own, other)
    return own - best, other - best, best, far_best


def core_join_kernel(heads, table_ref, own_ref, other_ref, state_ref):
    own_shift, other_shift = table_ref[2:3, :], table_ref[3:4, :]
    for i in range(own_ref.shape[0]):
        values, score = joined(heads, own_ref, other_ref, i, own_shift, other_shift)
        store_state(state_ref, i, values.astype(jnp.bfloat16), score)


def chip_join_kernel(heads, table_ref, own_ref, other_ref, _, merged_ref):
    own_shift, other_shift = table_ref[4:5, :], table_ref[5:6, :]
    for i in range(own_ref.shape[0]):
        values, _ = joined(heads, own_ref, other_ref, i, own_shift, other_shift)
        merged_ref[i] = values.astype(jnp.bfloat16)


def embed_rows(merged_ref, w_ref, out_ref):
    for i in range(merged_ref.shape[0]):
        out_ref[i] = matmul(merged_ref[i], w_ref[...], 0, 0).astype(jnp.bfloat16)


def embed_kernel(idx_ref, merged_ref, w_ref, prior_ref, out_ref):
    embed_rows(merged_ref, w_ref, out_ref)


def finish_kernel(idx_ref, *refs):
    *row_refs, other_ref, own_ref, w_ref, fresh_ref, out_ref, token_ref = refs
    token_ref[...] = jnp.zeros_like(token_ref)
    for piece, row_ref in enumerate(row_refs):

        @pl.when(pl.program_id(0) == piece)
        def _():
            fresh_ref[...] = row_ref[...]
            if piece < 2:
                embed_rows((other_ref, own_ref)[piece], w_ref, out_ref)


def fused_on_device(
    templ_pair, main_pair, coverage, pair_mask, tri_gain, w_project, w_bias, w_tri_out,
    merge_gain, w_merge_q, w_merge_kv, w_merge_out,
):
    rows, cols, channels = templ_pair.shape[1:]
    hidden = w_tri_out.shape[0]
    heads = w_bias.shape[1]
    dim = hidden // heads
    pair_ch = main_pair.shape[-1]
    row_devs, col_devs = lax.axis_size("row"), lax.axis_size("col")
    tiles_per_col = row_devs // col_devs
    templ, row_dev, col_dev = (lax.axis_index(a) for a in ("tmpl", "row", "col"))
    idx = jnp.stack([templ % 2, templ, row_dev, col_dev, (row_dev * rows) // BLOCK]).astype(jnp.int32)
    pieces = PIECES
    piece_rows = rows // pieces
    step_rows = STEP_ROWS
    steps = piece_rows // step_rows
    stored = jnp.swapaxes(templ_pair[0], 1, 2)
    bf16, f32 = jnp.bfloat16, jnp.float32
    def in_hbm(array):
        return pltpu.with_memory_space_constraint(array, pltpu.HBM)

    gain_row = in_hbm(tri_gain[None, :])
    cover = coverage.T
    stored, main_pair = in_hbm(stored), in_hbm(main_pair)

    def whole(array):
        return pl.BlockSpec(array.shape, lambda *_: (0,) * array.ndim)

    smem = pl.BlockSpec(memory_space=pltpu.SMEM)
    vmem = pl.BlockSpec(memory_space=pltpu.VMEM)
    anywhere = pl.BlockSpec(memory_space=pl.ANY)

    def call(kernel, grid, in_specs, out_specs, out_shape, scratch=(), aliases=None, cost=1e6):
        return pl.pallas_call(
            kernel,
            grid_spec=pltpu.PrefetchScalarGridSpec(
                num_scalar_prefetch=1, grid=grid, in_specs=in_specs, out_specs=out_specs,
                scratch_shapes=list(scratch),
            ),
            out_shape=out_shape,
            input_output_aliases=aliases or {},
            cost_estimate=pl.CostEstimate(
                flops=int(cost), bytes_accessed=1 << 20, transcendentals=0
            ),
            compiler_params=pltpu.CompilerParams(vmem_limit_bytes=VMEM_GRANT),
        )

    chunks = pieces // 2

    def plain_call(kernel, in_specs, out_shape, scratch=(), cost=1e6):
        return pl.pallas_call(
            kernel,
            in_specs=in_specs,
            out_specs=jax.tree.map(lambda _: vmem, out_shape),
            out_shape=out_shape,
            scratch_shapes=list(scratch),
            cost_estimate=pl.CostEstimate(
                flops=int(cost), bytes_accessed=1 << 20, transcendentals=0
            ),
            compiler_params=pltpu.CompilerParams(vmem_limit_bytes=VMEM_GRANT),
        )

    hbm = pl.BlockSpec(memory_space=pltpu.HBM)
    flat_bias_w = in_hbm(w_bias.T)
    *kept_rows, bias_tile = plain_call(
        functools.partial(norm_kernel, heads),
        [hbm, hbm, hbm],
        [jax.ShapeDtypeStruct((2 * piece_rows, channels, cols), bf16)] * (2 * chunks)
        + [jax.ShapeDtypeStruct((heads, rows, cols), bf16)],
        [
            pltpu.VMEM((pieces, heads, piece_rows, cols), f32),
            pltpu.VMEM((channels, cols), f32),
            pltpu.VMEM((pieces, piece_rows, channels, cols), bf16),
            pltpu.VMEM((1, channels), f32),
            pltpu.VMEM(flat_bias_w.shape, bf16),
            pltpu.SemaphoreType.DMA((pieces + 2,)),
        ],
    )(stored, gain_row, flat_bias_w)
    norms, raws = kept_rows[::2], kept_rows[1::2]


    tiles = [bias_tile]
    for turn in range(1, row_devs):
        perm = [(z, z ^ turn) for z in range(row_devs)]
        tiles.append(lax.ppermute(bias_tile, "row", perm))
    swap = [(c, col_devs - 1 - c) for c in range(col_devs)]
    fars = [lax.ppermute(norms[0], "col", swap)]
    pack_shape = (heads * channels + 2 * hidden + channels + 2 * hidden, channels)
    raw_weights = [in_hbm(w) for w in (w_project, w_tri_out, w_merge_kv, merge_gain[None, :])]
    packed_shapes = [
        jax.ShapeDtypeStruct(pack_shape, bf16),
        jax.ShapeDtypeStruct((channels, cols), f32),
        jax.ShapeDtypeStruct((8, cols), f32),
    ]
    with jax.named_scope("pack"):
        pack, merge_gain_wide, table = call(
            functools.partial(weight_kernel, heads),
            (1,),
            [whole(w) for w in raw_weights] + [smem] * 2,
            [vmem] * len(packed_shapes),
            packed_shapes,
        )(idx, *raw_weights, cover, pair_mask)
    query_w = in_hbm(w_merge_q.T)
    query_w = in_hbm(w_merge_q.T)
    with jax.named_scope("query"):
        main_query = call(
            functools.partial(query_kernel, dim ** (-0.5)),
            (pieces,),
            [
                pl.BlockSpec(
                    (piece_rows, cols, pair_ch),
                    lambda g, s: (piece_of(g, s, pieces), 0, 0),
                ),
                whole(query_w),
            ],
            vmem,
            jax.ShapeDtypeStruct((rows, hidden, cols), f32),
        )(idx, main_pair, query_w)
    picked = plain_call(
        pick_kernel,
        [vmem] * row_devs + [anywhere] * 2,
        jax.ShapeDtypeStruct((tiles_per_col,) + bias_tile.shape, bf16),
    )(*tiles, pack, main_query)
    far_tiles = lax.ppermute(picked, "col", swap)
    half_shape = jax.ShapeDtypeStruct((heads, cols, cols), f32)
    own_bias = plain_call(own_bias_kernel, [vmem] * (row_devs + 1), half_shape)(
        table, *tiles
    )
    after = own_bias
    nears = []
    near_shapes = [
        jax.ShapeDtypeStruct((piece_rows,) + shape, dtype)
        for shape, dtype in (
            ((heads, channels, cols), bf16),
            ((hidden, cols), f32),
            ((hidden, cols), bf16),
            ((heads, cols, cols), f32),
            ((heads, 8, cols), f32),
        )
    ]
    for side in range(2):
        with jax.named_scope("near%d" % side):
            nears.append(
                plain_call(
                    functools.partial(near_kernel, heads, side * piece_rows),
                    [vmem] * 3 + [anywhere],
                    near_shapes,
                    [pltpu.VMEM((piece_rows, cols, channels), bf16)],
                    2e9,
                )(norms[0], own_bias, pack, after)
            )
        after = nears[-1][-1]
    far_bias = plain_call(far_bias_kernel, [vmem, vmem, anywhere], half_shape)(
        table, far_tiles, after
    )
    held_back = lax.optimization_barrier((norms[1:], picked))[0]
    fars += [lax.ppermute(norm, "col", swap) for norm in held_back]

    fresh, states, pair_states = [], [], []
    after = far_bias
    cores = [(t, t + 1 - 2 * (t % 2)) for t in range(lax.axis_size("tmpl"))]
    chips = [(t, (t + 2) % 4) for t in range(lax.axis_size("tmpl"))]
    state_shape = jax.ShapeDtypeStruct((piece_rows, hidden + 2 * heads, cols), bf16)
    for piece in range(pieces):
        chunk, side = piece // 2, piece % 2
        row_shapes = [jax.ShapeDtypeStruct((piece_rows, channels, cols), bf16), state_shape]
        if chunk == 0:
            with jax.named_scope("attend%d" % piece):
                rows_out, state = plain_call(
                    functools.partial(late_kernel, heads, side * piece_rows, piece * piece_rows),
                    [vmem] * 11 + [anywhere],
                    row_shapes,
                    [
                        pltpu.VMEM((piece_rows, cols, channels), bf16),
                        pltpu.VMEM((piece_rows, heads, 2 * dim, col_devs * cols), bf16),
                        pltpu.VMEM((2, heads, cols, cols), f32),
                        pltpu.VMEM((2, heads, 8, cols), f32),
                        pltpu.VMEM((piece_rows, hidden, cols), bf16),
                    ],
                    6e9,
                )(
                    raws[chunk], fars[chunk], main_query, far_bias, pack, merge_gain_wide,
                    *nears[side], after,
                )
        else:
            with jax.named_scope("attend%d" % piece):
                rows_out, state = plain_call(
                    functools.partial(attend_kernel, heads, side * piece_rows, piece * piece_rows),
                    [vmem] * 8 + [anywhere],
                    [jax.ShapeDtypeStruct((piece_rows, channels, cols), bf16), state_shape],
                    [
                        pltpu.VMEM((piece_rows, col_devs * cols, channels), bf16),
                        pltpu.VMEM((piece_rows, heads, channels, cols), bf16),
                        pltpu.VMEM((piece_rows, hidden, cols), f32),
                        pltpu.VMEM((piece_rows, heads, 2 * dim, col_devs * cols), bf16),
                        pltpu.VMEM((2, heads, col_devs * cols, cols), f32),
                        pltpu.VMEM((2, heads, 8, cols), f32),
                        pltpu.VMEM((piece_rows, hidden, cols), bf16),
                    ],
                    6e9,
                )(
                    raws[chunk], norms[chunk], fars[chunk], main_query, own_bias, far_bias, pack,
                    merge_gain_wide, after,
                )
        fresh.append(rows_out)
        states.append(state)
        after = state
        if side:
            with jax.named_scope("corejoin%d" % chunk):
                after = plain_call(
                    functools.partial(core_join_kernel, heads),
                    [vmem] * 3,
                    state_shape,
                )(table, state, swapped)
            pair_states.append(after)
        else:
            with jax.named_scope("coreswap%d" % chunk):
                swapped = lax.ppermute(state, "tmpl", cores)

    emb_shape = jax.ShapeDtypeStruct(main_pair.shape, bf16)
    token = pair_states[-1]
    token_shape = jax.ShapeDtypeStruct((8, cols), f32)
    merged_shape = jax.ShapeDtypeStruct((piece_rows, hidden, cols), bf16)
    for chunk in range(chunks):
        pair_state = pair_states[chunk]
        with jax.named_scope("chipswap%d" % chunk):
            far_state = lax.ppermute(pair_state, "tmpl", chips)
        with jax.named_scope("chipjoin%d" % chunk):
            merged = plain_call(
                functools.partial(chip_join_kernel, heads),
                [vmem] * 3 + [anywhere],
                merged_shape,
            )(table, pair_state, far_state, token)
        with jax.named_scope("lastswap%d" % chunk):
            merged_other = lax.ppermute(merged, "tmpl", cores)

        def at_piece(piece):
            return lambda g, s: (piece_of(piece, s, pieces), 0, 0)

        if chunk == 0:
            with jax.named_scope("finish"):
                out, emb, token = call(
                    finish_kernel,
                    (pieces,),
                    [vmem] * (pieces + 3),
                    [
                        pl.BlockSpec(
                            (piece_rows, channels, cols),
                            lambda g, s: (piece_of(g, s, pieces), 0, 0),
                        ),
                        pl.BlockSpec(
                            (piece_rows, cols, pair_ch),
                            lambda g, s: (piece_of(jnp.minimum(g, 1), s, pieces), 0, 0),
                        ),
                        vmem,
                    ],
                    [jax.ShapeDtypeStruct(stored.shape, bf16), emb_shape, token_shape],
                )(idx, *fresh, merged_other, merged, w_merge_out)
        else:
            for piece, part in ((2 * chunk + 1, merged), (2 * chunk, merged_other)):
                with jax.named_scope("embed%d" % piece):
                    emb = call(
                        embed_kernel,
                        (1,),
                        [vmem, vmem, anywhere],
                        pl.BlockSpec((piece_rows, cols, pair_ch), at_piece(piece)),
                        emb_shape,
                        aliases={3: 0},
                    )(idx, part, w_merge_out, emb)
    return (jnp.swapaxes(out, 1, 2)[None], emb)


PIECES = 4
VMEM_GRANT = 16 << 20
STEP_ROWS = 8


def takes_fused(templ_pair, main_pair):
    rows, cols = templ_pair.shape[1:3]
    row_devs, col_devs = lax.axis_size("row"), lax.axis_size("col")
    return (
        lax.axis_size("tmpl") == 4
        and col_devs == 2
        and cols == BLOCK
        and BLOCK % rows == 0
        and row_devs & (row_devs - 1) == 0
        and row_devs % col_devs == 0
        and rows * (row_devs // col_devs) == cols
        and rows % (PIECES * STEP_ROWS) == 0
    )


def on_device(*operands):
    if takes_fused(*operands[:2]):
        return fused_on_device(*operands)
    return plain_on_device(*operands)


def solution(mesh):
    in_specs = (
        P("tmpl", "row", "col", None),
        P("row", "col", None),
        P(),
        P(),
        P(),
        P(),
        P(),
        P(),
        P(),
        P(),
        P(),
        P(),
    )
    out_specs = (P("tmpl", "row", "col", None), P("row", "col", None))
    return jax.shard_map(
        on_device, mesh=mesh, in_specs=in_specs, out_specs=out_specs, check_vma=False
    )
```

```python
import functools

import jax
import jax.numpy as jnp
from jax import lax
from jax.experimental import pallas as pl
from jax.experimental.pallas import tpu as pltpu
from jax.sharding import PartitionSpec as P

BLOCK = 128


MASK_SHIFT = 10000.0
EPSILON = 1e-05
NEG_START = -1e30


def combined_all(part, axis, combine):
    gathered = jax.tree.map(lambda a: lax.all_gather(a, axis), part)

    def take(source):
        return jax.tree.map(lambda a: lax.dynamic_index_in_dim(a, source, 0, False), gathered)

    return lax.fori_loop(
        1, lax.axis_size(axis), lambda source, state: combine(state, take(source)), take(0)
    )


def layer_norm(values, scale_gain):
    values = values.astype(jnp.float32)
    center = values - jnp.mean(values, axis=-1, keepdims=True)
    spread = jnp.mean(center * center, axis=-1, keepdims=True)
    return center * lax.rsqrt(spread + EPSILON) * scale_gain


def row_group(rows_dev, cols_dev):
    chosen = 1
    for candidate in range(1, rows_dev + 1):
        if rows_dev % candidate == 0 and candidate * cols_dev <= 2048:
            chosen = candidate
    return chosen


def plain_on_device(
    templ_pair,
    main_pair,
    coverage,
    pair_mask,
    tri_gain,
    w_project,
    w_bias,
    w_tri_out,
    merge_gain,
    w_merge_q,
    w_merge_kv,
    w_merge_out,
):
    pair_tile = templ_pair[0]
    rows_dev, cols_dev, channels = pair_tile.shape
    hidden = w_tri_out.shape[0]
    head_count = w_bias.shape[1]
    head_dim = hidden // head_count
    score_scale = head_dim ** (-0.5)
    row_start = lax.axis_index("row") * rows_dev
    col_start = lax.axis_index("col") * cols_dev
    templ_index = lax.axis_index("tmpl")
    cover_tok = jnp.repeat(coverage, BLOCK, axis=1)
    own_cover = lax.dynamic_index_in_dim(cover_tok, templ_index, 0, keepdims=False)
    mask_full = jnp.repeat(jnp.repeat(pair_mask, BLOCK, axis=0), BLOCK, axis=1)
    mask_rows = lax.dynamic_slice_in_dim(mask_full, row_start, rows_dev, 0)
    cover_rows = lax.dynamic_slice_in_dim(own_cover, row_start, rows_dev, 0)
    normed = layer_norm(pair_tile, tri_gain).astype(jnp.bfloat16)
    flat_norm = normed.reshape(-1, channels)
    w_query_gate = jnp.concatenate([w_project[:, :hidden], w_project[:, 3 * hidden :]], axis=1)
    query_gate = jnp.dot(flat_norm, w_query_gate, preferred_element_type=jnp.float32).reshape(
        rows_dev, cols_dev, 2 * hidden
    )
    queries = (
        (query_gate[..., :hidden] * score_scale)
        .astype(jnp.bfloat16)
        .reshape(rows_dev, cols_dev, head_count, head_dim)
    )
    gate_values = jax.nn.sigmoid(query_gate[..., hidden:])
    bias_tile = jnp.dot(flat_norm, w_bias, preferred_element_type=jnp.float32).astype(jnp.bfloat16)
    bias_tile = jnp.transpose(bias_tile.reshape(rows_dev, cols_dev, head_count), (2, 0, 1))
    bias_column = lax.all_gather(bias_tile, "row", axis=1, tiled=True)
    bias_slab = lax.all_to_all(bias_column, "col", split_axis=1, concat_axis=2, tiled=True)
    bias_rows = jnp.transpose(bias_slab, (1, 0, 2)).astype(jnp.float32)
    key_shift = MASK_SHIFT * (
        (cover_rows[:, None] * own_cover[None, :] * mask_rows).astype(jnp.float32) - 1.0
    )
    w_key_value = w_project[:, hidden : 3 * hidden]
    group = row_group(rows_dev, cols_dev)
    splits = rows_dev // group

    def grouped(array):
        return array.reshape((splits, group) + array.shape[1:])

    start_state = (
        jnp.full((rows_dev, cols_dev, head_count), NEG_START, jnp.float32),
        jnp.zeros((rows_dev, cols_dev, head_count), jnp.float32),
        jnp.zeros((rows_dev, cols_dev, head_count, head_dim), jnp.float32),
    )
    norm_piece = lax.all_gather(normed, "col", axis=1, tiled=True)
    piece_width = norm_piece.shape[1]

    def one_group(group_args):
        query_part, norm_part, shift_part, maxima, totals, weighted = group_args
        key_value = jnp.dot(
            norm_part.reshape(-1, channels), w_key_value, preferred_element_type=jnp.float32
        ).astype(jnp.bfloat16)
        key_value = key_value.reshape(group, piece_width, 2 * hidden)
        key_part = key_value[..., :hidden].reshape(group, piece_width, head_count, head_dim)
        value_part = key_value[..., hidden:].reshape(group, piece_width, head_count, head_dim)
        scores = jnp.einsum(
            "ijhd,ikhd->ijhk", query_part, key_part, preferred_element_type=jnp.float32
        )
        scores = scores + bias_rows[None] + shift_part[:, None, None, :]
        highest = jnp.maximum(maxima, jnp.max(scores, axis=-1))
        rescale = jnp.exp(maxima - highest)
        weights = jnp.exp(scores - highest[..., None])
        totals = totals * rescale + jnp.sum(weights, axis=-1)
        summed = jnp.einsum(
            "ijhk,ikhd->ijhd",
            weights.astype(jnp.bfloat16),
            value_part,
            preferred_element_type=jnp.float32,
        )
        weighted = weighted * rescale[..., None] + summed
        return (highest, totals, weighted)

    outcome = lax.map(
        one_group,
        (
            grouped(queries),
            grouped(norm_piece),
            grouped(key_shift),
            grouped(start_state[0]),
            grouped(start_state[1]),
            grouped(start_state[2]),
        ),
    )
    result = tuple((member.reshape((rows_dev,) + member.shape[2:]) for member in outcome))
    attended = result[2] / result[1][..., None]
    gated = (attended.reshape(rows_dev, cols_dev, hidden) * gate_values).astype(jnp.bfloat16)
    projected = jnp.dot(
        gated.reshape(-1, hidden), w_tri_out, preferred_element_type=jnp.float32
    ).reshape(rows_dev, cols_dev, channels)
    new_pair = (pair_tile.astype(jnp.float32) + projected).astype(jnp.bfloat16)
    merge_norm = layer_norm(new_pair, merge_gain).astype(jnp.bfloat16)
    merge_kv = jnp.dot(
        merge_norm.reshape(-1, channels), w_merge_kv, preferred_element_type=jnp.float32
    ).astype(jnp.bfloat16)
    merge_kv = merge_kv.reshape(rows_dev, cols_dev, 2 * hidden)
    pair_ch = main_pair.shape[-1]
    main_query = (
        jnp.dot(main_pair.reshape(-1, pair_ch), w_merge_q, preferred_element_type=jnp.float32)
        * score_scale
    )
    main_query = main_query.reshape(rows_dev, cols_dev, head_count, head_dim)
    mask_tile = lax.dynamic_slice_in_dim(mask_rows, col_start, cols_dev, 1)
    own_cols = lax.dynamic_slice_in_dim(own_cover, col_start, cols_dev, 0)
    own_valid = cover_rows[:, None] * own_cols[None, :] * mask_tile
    shift_bias = MASK_SHIFT * (own_valid.astype(jnp.float32) - 1.0)
    keys_own = (
        merge_kv[..., :hidden].astype(jnp.float32).reshape(rows_dev, cols_dev, head_count, head_dim)
    )
    values_own = (
        merge_kv[..., hidden:].astype(jnp.float32).reshape(rows_dev, cols_dev, head_count, head_dim)
    )
    scores = jnp.sum(main_query * keys_own, axis=-1) + shift_bias[..., None]

    def combine(earlier, later):
        highest = jnp.maximum(earlier[0], later[0])
        early_scale = jnp.exp(earlier[0] - highest)
        late_scale = jnp.exp(later[0] - highest)
        return (
            highest,
            earlier[1] * early_scale + later[1] * late_scale,
            earlier[2] * early_scale[..., None] + later[2] * late_scale[..., None],
        )

    merged_state = combined_all((scores, jnp.ones_like(scores), values_own), "tmpl", combine)
    merged = merged_state[2] / merged_state[1][..., None]
    merged = merged.reshape(-1, hidden).astype(jnp.bfloat16)
    embedding = jnp.dot(merged, w_merge_out, preferred_element_type=jnp.float32).astype(
        jnp.bfloat16
    )
    return (new_pair[None], embedding.reshape(rows_dev, cols_dev, pair_ch))


LOG2E = 1.4426950408889634


def normed_rows(values, gain):
    center = values - jnp.mean(values, axis=0, keepdims=True)
    spread = jnp.mean(center * center, axis=0, keepdims=True)
    return (center * lax.rsqrt(spread + EPSILON) * gain).astype(jnp.bfloat16)


def places(rows):
    templ, row_dev, col_dev = (lax.axis_index(axis) for axis in ("tmpl", "row", "col"))
    return lax.rem(templ, 2), templ, row_dev, col_dev, row_dev * rows // BLOCK


def piece_of(piece, idx_ref, pieces):
    half = idx_ref[0]
    odd = lax.rem(piece, 2)
    side = odd * half + (1 - odd) * (1 - half)
    return side * (pieces // 2) + piece // 2


def mask_shift(cover_ref, mask_ref, templ, row_block, col_block):
    valid = (
        cover_ref[row_block, templ] * cover_ref[col_block, templ] * mask_ref[row_block, col_block]
    )
    return MASK_SHIFT * (valid.astype(jnp.float32) - 1.0)


def matmul(lhs, rhs, lhs_dim=1, rhs_dim=0):
    return lax.dot_general(
        lhs, rhs, (((lhs_dim,), (rhs_dim,)), ((), ())), preferred_element_type=jnp.float32
    )


def widened(row_ref, cols):
    return jnp.broadcast_to(row_ref[...], (cols, row_ref.shape[1])).T


def norm_kernel(heads, x_hbm, gain_hbm, bias_w_hbm, *refs):
    *kept_refs, bias_ref, held, wide, x_ref, gain_ref, bias_w_ref, done = refs
    norm_refs, raw_refs = kept_refs[::2], kept_refs[1::2]
    pieces, step_rows, _, cols = x_ref.shape
    idx_ref = places(pieces * step_rows)
    small = [
        pltpu.make_async_copy(gain_hbm, gain_ref, done.at[pieces]),
        pltpu.make_async_copy(bias_w_hbm, bias_w_ref, done.at[pieces + 1]),
    ]
    firsts = [
        pl.multiple_of(piece_of(piece, idx_ref, pieces) * step_rows, step_rows)
        for piece in range(pieces)
    ]
    copies = [
        pltpu.make_async_copy(x_hbm.at[pl.ds(first, step_rows)], x_ref.at[piece], done.at[piece])
        for piece, first in enumerate(firsts)
    ]
    for copy in small + copies:
        copy.start()
    for copy in small:
        copy.wait()
    wide[...] = widened(gain_ref, cols)
    for piece in range(pieces):
        copies[piece].wait()
        base = piece % 2 * step_rows
        norm_ref, raw_ref = norm_refs[piece // 2], raw_refs[piece // 2]
        for i in range(step_rows):
            raw_ref[base + i] = x_ref[piece, i]
            norm_ref[base + i] = normed_rows(x_ref[piece, i].astype(jnp.float32), wide[...])
        wide_norm = jnp.concatenate([norm_ref[base + i] for i in range(step_rows)], axis=1)
        wide_bias = matmul(bias_w_ref[...], wide_norm)
        for i in range(step_rows):
            for head in range(heads):
                held[piece, head, i : i + 1, :] = wide_bias[
                    head : head + 1, i * cols : (i + 1) * cols
                ]
        bias_ref[:, pl.ds(firsts[piece], step_rows), :] = held[piece].astype(jnp.bfloat16)


def weight_kernel(
    heads, idx_ref, project_ref, tri_out_ref, kv_ref, gain_ref, cover_ref, mask_ref, pack_ref, wide_ref, table_ref
):
    for line, shift in enumerate(all_shifts(idx_ref, cover_ref, mask_ref)):
        table_ref[line : line + 1, :] = jnp.full((1, table_ref.shape[1]), shift, jnp.float32)
    wide_ref[...] = widened(gain_ref, wide_ref.shape[1])
    channels = project_ref.shape[0]
    hidden = tri_out_ref.shape[0]
    dim = hidden // heads
    scale = dim ** (-0.5) * LOG2E
    project = project_ref[...]
    for head in range(heads):
        query = project[:, head * dim : (head + 1) * dim]
        key = project[:, hidden + head * dim : hidden + (head + 1) * dim]
        pack_ref[head * channels : (head + 1) * channels, :] = (
            matmul(key, query, 1, 1) * scale
        ).astype(jnp.bfloat16)
    row = heads * channels
    rest = (
        project[:, 3 * hidden :],
        project[:, 2 * hidden : 3 * hidden],
        tri_out_ref[...],
        kv_ref[...],
    )
    for part in rest:
        flipped = part.astype(jnp.float32).T.astype(jnp.bfloat16)
        pack_ref[row : row + flipped.shape[0], :] = flipped
        row += flipped.shape[0]


def when_held(idx_ref, column, part, tile_refs, tiles_per_col, act):
    wanted = idx_ref[2] ^ (tiles_per_col * column + part)
    for turn, tile_ref in enumerate(tile_refs):

        @pl.when(wanted == turn)
        def _():
            act(tile_ref)


def pick_kernel(*refs):
    *tile_refs, _, _, out_ref = refs
    idx_ref = places(tile_refs[0].shape[1])
    for part in range(out_ref.shape[0]):

        def act(tile_ref, part=part):
            out_ref[part] = tile_ref[...]

        when_held(idx_ref, 1 - idx_ref[3], part, tile_refs, out_ref.shape[0], act)


def relative_shift(idx_ref, cover_ref, mask_ref, block):
    shifts = [mask_shift(cover_ref, mask_ref, idx_ref[1], idx_ref[4], b) for b in (block, 1 - block)]
    return shifts[0] - jnp.maximum(*shifts)


def all_shifts(idx_ref, cover_ref, mask_ref):
    own, other, best, far_best = pair_shifts(idx_ref, cover_ref, mask_ref)
    top = jnp.maximum(best, far_best)
    blocks = (idx_ref[3], 1 - idx_ref[3])
    return [relative_shift(idx_ref, cover_ref, mask_ref, block) for block in blocks] + [
        own,
        other,
        best - top,
        far_best - top,
    ]


def place_bias(out_ref, part, tile, shift):
    heads, tile_rows, _ = tile.shape
    for head in range(heads):
        flipped = tile[head].astype(jnp.float32).T
        out_ref[head, :, part * tile_rows : (part + 1) * tile_rows] = (flipped + shift) * LOG2E


def own_bias_kernel(table_ref, *refs):
    *tile_refs, _, out_ref = refs
    idx_ref = places(tile_refs[0].shape[1])
    tiles_per_col = out_ref.shape[2] // tile_refs[0].shape[1]
    shift = table_ref[0:1, : tile_refs[0].shape[1]]
    for part in range(tiles_per_col):

        def act(tile_ref, part=part):
            place_bias(out_ref, part, tile_ref[...], shift)

        when_held(idx_ref, idx_ref[3], part, tile_refs, tiles_per_col, act)


def far_bias_kernel(table_ref, tiles_ref, _, out_ref):
    shift = table_ref[1:2, : tiles_ref.shape[2]]
    for part in range(tiles_ref.shape[0]):
        place_bias(out_ref, part, tiles_ref[part], shift)


def query_kernel(scale, idx_ref, main_ref, w_ref, out_ref):
    step_rows, cols, pair_ch = main_ref.shape
    base = pl.program_id(0) * step_rows
    wide = matmul(w_ref[...], main_ref[...].reshape(step_rows * cols, pair_ch), 1, 1) * scale
    for i in range(step_rows):
        out_ref[base + i] = wide[:, i * cols : (i + 1) * cols]


def split_pack(pack_ref, heads, hidden):
    channels = pack_ref.shape[1]
    ends = [heads * channels]
    for size in (hidden, hidden, channels):
        ends.append(ends[-1] + size)
    return ends


def near_kernel(
    heads, skip, own_ref, own_bias_ref, pack_ref, after_ref, probes, gates, own_mix, near, near_tops, turned
):
    step_rows, _, channels, _ = probes.shape
    ends = split_pack(pack_ref, heads, gates.shape[1])
    for i in range(step_rows):
        own = own_ref[skip + i]
        first = matmul(pack_ref[: ends[2], :], own)
        for h in range(heads):
            probes[i, h] = first[h * channels : (h + 1) * channels, :].astype(jnp.bfloat16)
        gates[i] = jax.nn.sigmoid(first[ends[0] : ends[1], :])
        own_mix[i] = first[ends[1] :, :].astype(jnp.bfloat16)
        turned[i] = own.T
    for i in range(step_rows):
        for h in range(heads):
            scores = matmul(turned[i], probes[i, h]) + own_bias_ref[h]
            near[i, h] = scores
            near_tops[i, h] = jnp.broadcast_to(
                jnp.max(scores, axis=0, keepdims=True), near_tops.shape[2:]
            )


def late_kernel(
    heads,
    skip,
    query_skip,
    x_ref,
    far_ref,
    main_query,
    far_bias_ref,
    pack_ref,
    gain_ref,
    probes,
    gates,
    own_mix,
    near,
    near_tops,
    after_ref,
    out_ref,
    state_ref,
    turned,
    mixers,
    held,
    tops,
    gated,
):
    step_rows, _, cols = out_ref.shape
    hidden = main_query.shape[1]
    dim = hidden // heads
    ends = split_pack(pack_ref, heads, hidden)
    value_w = pack_ref[ends[1] : ends[2], :]
    for i in range(step_rows):
        far = far_ref[skip + i]
        values = matmul(value_w, far).astype(jnp.bfloat16)
        for h in range(heads):
            span = slice(h * dim, (h + 1) * dim)
            mixers[i, h, :dim, :cols] = own_mix[i, span, :]
            mixers[i, h, :dim, cols:] = values[span, :]
            mixers[i, h, dim:, :] = jnp.ones((mixers.shape[2] - dim, 2 * cols), jnp.bfloat16)
        turned[i] = far.T

    slots = held.shape[0]

    def score_row(i, h):
        scores = matmul(turned[i], probes[i, h]) + far_bias_ref[h]
        held[i % slots, h] = scores
        highest = jnp.max(scores, axis=0, keepdims=True)
        tops[i % slots, h] = jnp.maximum(near_tops[i, h], highest)

    def mix_row(i, h):
        top = tops[i % slots, h][:1]
        weights = jnp.concatenate(
            [
                jnp.exp2(part - top).astype(jnp.bfloat16)
                for part in (near[i, h], held[i % slots, h])
            ],
            axis=0,
        )
        mixed = matmul(mixers[i, h], weights)
        span = slice(h * dim, (h + 1) * dim)
        gated[i, span, :] = (
            mixed[:dim] * (1.0 / mixed[dim : dim + 1]) * gates[i, span, :]
        ).astype(jnp.bfloat16)

    for unit in range(heads * step_rows + LEAD):
        if unit < heads * step_rows:
            score_row(*divmod(unit, heads))
        if unit >= LEAD:
            mix_row(*divmod(unit - LEAD, heads))
    write_rows(
        heads, skip, query_skip, x_ref, main_query, pack_ref, gain_ref, gated, out_ref, state_ref
    )


def write_rows(
    heads, skip, query_skip, x_ref, main_query, pack_ref, gain_ref, gated, out_ref, state_ref
):
    step_rows = out_ref.shape[0]
    hidden = gated.shape[1]
    dim = hidden // heads
    ends = split_pack(pack_ref, heads, hidden)
    tri_w = pack_ref[ends[2] : ends[3], :]
    kv_w = pack_ref[ends[3] :, :]
    for i in range(step_rows):
        fresh = x_ref[skip + i].astype(jnp.float32) + matmul(tri_w, gated[i])
        out_ref[i] = fresh.astype(jnp.bfloat16)
    for i in range(step_rows):
        merge_norm = normed_rows(out_ref[i].astype(jnp.float32), gain_ref[...])
        merge_kv = matmul(kv_w, merge_norm).astype(jnp.bfloat16)
        product = main_query[query_skip + i] * merge_kv[:hidden, :].astype(jnp.float32)
        score = jnp.concatenate(
            [
                jnp.sum(product[h * dim : (h + 1) * dim, :], axis=0, keepdims=True)
                for h in range(heads)
            ],
            axis=0,
        )
        store_state(state_ref, i, merge_kv[hidden:, :], score)


def store_state(state_ref, i, values, score):
    hidden = values.shape[0]
    high = score.astype(jnp.bfloat16)
    low = (score - high.astype(jnp.float32)).astype(jnp.bfloat16)
    state_ref[i, :hidden, :] = values
    state_ref[i, hidden:, :] = jnp.concatenate([high, low], axis=0)


def spread_heads(per_head, dim):
    heads, cols = per_head.shape
    return jnp.concatenate(
        [jnp.broadcast_to(per_head[h : h + 1, :], (dim, cols)) for h in range(heads)], axis=0
    )


def joined(heads, first_ref, second_ref, i, first_shift, second_shift):
    hidden = first_ref.shape[1] - 2 * heads

    def parts(ref, shift):
        extra = ref[i, hidden:, :].astype(jnp.float32)
        return ref[i, :hidden, :].astype(jnp.float32), extra[:heads] + extra[heads:] + shift

    first_values, first_score = parts(first_ref, first_shift)
    second_values, second_score = parts(second_ref, second_shift)
    highest = jnp.maximum(first_score, second_score)
    first_weight = jnp.exp(first_score - highest)
    second_weight = jnp.exp(second_score - highest)
    total = first_weight + second_weight
    inverse = 1.0 / total
    dim = hidden // heads
    values = first_values * spread_heads(first_weight * inverse, dim)
    values = values + second_values * spread_heads(second_weight * inverse, dim)
    return values, highest + jnp.log(total)


def pair_shifts(idx_ref, cover_ref, mask_ref):
    templ, col_dev, row_block = idx_ref[1], idx_ref[3], idx_ref[4]
    even = templ - lax.rem(templ, 2)
    own = mask_shift(cover_ref, mask_ref, templ, row_block, col_dev)
    other = mask_shift(cover_ref, mask_ref, 2 * even + 1 - templ, row_block, col_dev)
    far = 2 - even
    far_best = jnp.maximum(
        mask_shift(cover_ref, mask_ref, far, row_block, col_dev),
        mask_shift(cover_ref, mask_ref, far + 1, row_block, col_dev),
    )
    best = jnp.maximum(own, other)
    return own - best, other - best, best, far_best


def core_join_kernel(heads, table_ref, own_ref, other_ref, state_ref):
    own_shift, other_shift = table_ref[2:3, :], table_ref[3:4, :]
    for i in range(own_ref.shape[0]):
        values, score = joined(heads, own_ref, other_ref, i, own_shift, other_shift)
        store_state(state_ref, i, values.astype(jnp.bfloat16), score)


def chip_join_kernel(heads, table_ref, own_ref, other_ref, _, merged_ref):
    own_shift, other_shift = table_ref[4:5, :], table_ref[5:6, :]
    for i in range(own_ref.shape[0]):
        values, _ = joined(heads, own_ref, other_ref, i, own_shift, other_shift)
        merged_ref[i] = values.astype(jnp.bfloat16)


def embed_rows(merged_ref, w_ref, out_ref):
    for i in range(merged_ref.shape[0]):
        out_ref[i] = matmul(merged_ref[i], w_ref[...], 0, 0).astype(jnp.bfloat16)


def embed_kernel(idx_ref, merged_ref, w_ref, prior_ref, out_ref):
    embed_rows(merged_ref, w_ref, out_ref)


def finish_kernel(idx_ref, *refs):
    *row_refs, other_ref, own_ref, w_ref, fresh_ref, out_ref, token_ref = refs
    token_ref[...] = jnp.zeros_like(token_ref)
    for piece, row_ref in enumerate(row_refs):

        @pl.when(pl.program_id(0) == piece)
        def _():
            fresh_ref[...] = row_ref[...]
            if piece < 2:
                embed_rows((other_ref, own_ref)[piece], w_ref, out_ref)


def fused_on_device(
    templ_pair, main_pair, coverage, pair_mask, tri_gain, w_project, w_bias, w_tri_out,
    merge_gain, w_merge_q, w_merge_kv, w_merge_out,
):
    rows, cols, channels = templ_pair.shape[1:]
    hidden = w_tri_out.shape[0]
    heads = w_bias.shape[1]
    dim = hidden // heads
    pair_ch = main_pair.shape[-1]
    row_devs, col_devs = lax.axis_size("row"), lax.axis_size("col")
    tiles_per_col = row_devs // col_devs
    templ, row_dev, col_dev = (lax.axis_index(a) for a in ("tmpl", "row", "col"))
    idx = jnp.stack([templ % 2, templ, row_dev, col_dev, (row_dev * rows) // BLOCK]).astype(jnp.int32)
    pieces = PIECES
    piece_rows = rows // pieces
    stored = jnp.swapaxes(templ_pair[0], 1, 2)
    bf16, f32 = jnp.bfloat16, jnp.float32

    def in_hbm(array):
        return pltpu.with_memory_space_constraint(array, pltpu.HBM)

    gain_row = in_hbm(tri_gain[None, :])
    cover = coverage.T
    stored, main_pair = in_hbm(stored), in_hbm(main_pair)

    def whole(array):
        return pl.BlockSpec(array.shape, lambda *_: (0,) * array.ndim)

    smem = pl.BlockSpec(memory_space=pltpu.SMEM)
    vmem = pl.BlockSpec(memory_space=pltpu.VMEM)
    anywhere = pl.BlockSpec(memory_space=pl.ANY)

    def call(kernel, grid, in_specs, out_specs, out_shape, scratch=(), aliases=None, cost=1e6):
        return pl.pallas_call(
            kernel,
            grid_spec=pltpu.PrefetchScalarGridSpec(
                num_scalar_prefetch=1, grid=grid, in_specs=in_specs, out_specs=out_specs,
                scratch_shapes=list(scratch),
            ),
            out_shape=out_shape,
            input_output_aliases=aliases or {},
            cost_estimate=pl.CostEstimate(
                flops=int(cost), bytes_accessed=1 << 20, transcendentals=0
            ),
            compiler_params=pltpu.CompilerParams(vmem_limit_bytes=VMEM_GRANT),
        )

    chunks = pieces // 2

    def plain_call(kernel, in_specs, out_shape, scratch=(), cost=1e6):
        return pl.pallas_call(
            kernel,
            in_specs=in_specs,
            out_specs=jax.tree.map(lambda _: vmem, out_shape),
            out_shape=out_shape,
            scratch_shapes=list(scratch),
            cost_estimate=pl.CostEstimate(
                flops=int(cost), bytes_accessed=1 << 20, transcendentals=0
            ),
            compiler_params=pltpu.CompilerParams(vmem_limit_bytes=VMEM_GRANT),
        )

    hbm = pl.BlockSpec(memory_space=pltpu.HBM)
    flat_bias_w = in_hbm(w_bias.T)
    *kept_rows, bias_tile = plain_call(
        functools.partial(norm_kernel, heads),
        [hbm, hbm, hbm],
        [jax.ShapeDtypeStruct((2 * piece_rows, channels, cols), bf16)] * (2 * chunks)
        + [jax.ShapeDtypeStruct((heads, rows, cols), bf16)],
        [
            pltpu.VMEM((pieces, heads, piece_rows, cols), f32),
            pltpu.VMEM((channels, cols), f32),
            pltpu.VMEM((pieces, piece_rows, channels, cols), bf16),
            pltpu.VMEM((1, channels), f32),
            pltpu.VMEM(flat_bias_w.shape, bf16),
            pltpu.SemaphoreType.DMA((pieces + 2,)),
        ],
    )(stored, gain_row, flat_bias_w)
    norms, raws = kept_rows[::2], kept_rows[1::2]


    tiles = [bias_tile]
    for turn in range(1, row_devs):
        perm = [(z, z ^ turn) for z in range(row_devs)]
        tiles.append(lax.ppermute(bias_tile, "row", perm))
    swap = [(c, col_devs - 1 - c) for c in range(col_devs)]
    fars = [lax.ppermute(norms[0], "col", swap)]
    pack_shape = (heads * channels + 2 * hidden + channels + 2 * hidden, channels)
    raw_weights = [in_hbm(w) for w in (w_project, w_tri_out, w_merge_kv, merge_gain[None, :])]
    packed_shapes = [
        jax.ShapeDtypeStruct(pack_shape, bf16),
        jax.ShapeDtypeStruct((channels, cols), f32),
        jax.ShapeDtypeStruct((8, cols), f32),
    ]
    pack, merge_gain_wide, table = call(
        functools.partial(weight_kernel, heads),
        (1,),
        [whole(w) for w in raw_weights] + [smem] * 2,
        [vmem] * len(packed_shapes),
        packed_shapes,
    )(idx, *raw_weights, cover, pair_mask)
    query_w = in_hbm(w_merge_q.T)
    query_w = in_hbm(w_merge_q.T)
    main_query = call(
        functools.partial(query_kernel, dim ** (-0.5)),
        (pieces,),
        [
            pl.BlockSpec((piece_rows, cols, pair_ch), lambda g, s: (piece_of(g, s, pieces), 0, 0)),
            whole(query_w),
        ],
        vmem,
        jax.ShapeDtypeStruct((rows, hidden, cols), f32),
    )(idx, main_pair, query_w)
    picked = plain_call(
        pick_kernel,
        [vmem] * row_devs + [anywhere] * 2,
        jax.ShapeDtypeStruct((tiles_per_col,) + bias_tile.shape, bf16),
    )(*tiles, pack, main_query)
    far_tiles = lax.ppermute(picked, "col", swap)
    half_shape = jax.ShapeDtypeStruct((heads, cols, cols), f32)
    own_bias = plain_call(own_bias_kernel, [vmem] * (row_devs + 1) + [anywhere], half_shape)(
        table, *tiles, picked
    )
    after = own_bias
    nears = []
    near_shapes = [
        jax.ShapeDtypeStruct((piece_rows,) + shape, dtype)
        for shape, dtype in (
            ((heads, channels, cols), bf16),
            ((hidden, cols), f32),
            ((hidden, cols), bf16),
            ((heads, cols, cols), f32),
            ((heads, 8, cols), f32),
        )
    ]

    def near_part(after):
        piece = len(nears)
        nears.append(
            plain_call(
                functools.partial(near_kernel, heads, piece % 2 * piece_rows),
                [vmem] * 3 + [anywhere],
                near_shapes,
                [pltpu.VMEM((piece_rows, cols, channels), bf16)],
                2e9,
            )(norms[piece // 2], own_bias, pack, after)
        )
        return nears[-1][-1]

    while len(nears) < EARLY:
        after = near_part(after)
    far_bias = plain_call(far_bias_kernel, [vmem, vmem, anywhere], half_shape)(
        table, far_tiles, after
    )
    held_back = lax.optimization_barrier((norms[1:], picked))[0]
    fars += [lax.ppermute(norm, "col", swap) for norm in held_back]

    fresh, states, pair_states = [], [], []
    after = far_bias
    cores = [(t, t + 1 - 2 * (t % 2)) for t in range(lax.axis_size("tmpl"))]
    chips = [(t, (t + 2) % 4) for t in range(lax.axis_size("tmpl"))]
    state_shape = jax.ShapeDtypeStruct((piece_rows, hidden + 2 * heads, cols), bf16)
    for piece in range(pieces):
        chunk, side = piece // 2, piece % 2
        if len(nears) == piece:
            after = near_part(after)
        rows_out, state = plain_call(
            functools.partial(late_kernel, heads, side * piece_rows, piece * piece_rows),
            [vmem] * 11 + [anywhere],
            [jax.ShapeDtypeStruct((piece_rows, channels, cols), bf16), state_shape],
            [
                pltpu.VMEM((piece_rows, cols, channels), bf16),
                pltpu.VMEM((piece_rows, heads, 2 * dim, col_devs * cols), bf16),
                pltpu.VMEM((2, heads, cols, cols), f32),
                pltpu.VMEM((2, heads, 8, cols), f32),
                pltpu.VMEM((piece_rows, hidden, cols), bf16),
            ],
            6e9,
        )(
            raws[chunk], fars[chunk], main_query, far_bias, pack, merge_gain_wide,
            *nears[piece], after,
        )
        fresh.append(rows_out)
        states.append(state)
        after = state
        if side:
            after = plain_call(
                functools.partial(core_join_kernel, heads),
                [vmem] * 3,
                state_shape,
            )(table, state, swapped)
            pair_states.append(after)
            if len(nears) < pieces:
                after = near_part(after)
        else:
            swapped = lax.ppermute(state, "tmpl", cores)

    emb_shape = jax.ShapeDtypeStruct(main_pair.shape, bf16)
    token = pair_states[-1]
    token_shape = jax.ShapeDtypeStruct((8, cols), f32)
    merged_shape = jax.ShapeDtypeStruct((piece_rows, hidden, cols), bf16)
    for chunk in range(chunks):
        pair_state = pair_states[chunk]
        far_state = lax.ppermute(pair_state, "tmpl", chips)
        merged = plain_call(
            functools.partial(chip_join_kernel, heads),
            [vmem] * 3 + [anywhere],
            merged_shape,
        )(table, pair_state, far_state, token)
        merged_other = lax.ppermute(merged, "tmpl", cores)

        def at_piece(piece):
            return lambda g, s: (piece_of(piece, s, pieces), 0, 0)

        if chunk == 0:
            out, emb, token = call(
                finish_kernel,
                (pieces,),
                [vmem] * (pieces + 3),
                [
                    pl.BlockSpec(
                        (piece_rows, channels, cols),
                        lambda g, s: (piece_of(g, s, pieces), 0, 0),
                    ),
                    pl.BlockSpec(
                        (piece_rows, cols, pair_ch),
                        lambda g, s: (piece_of(jnp.minimum(g, 1), s, pieces), 0, 0),
                    ),
                    vmem,
                ],
                [jax.ShapeDtypeStruct(stored.shape, bf16), emb_shape, token_shape],
            )(idx, *fresh, merged_other, merged, w_merge_out)
        else:
            for piece, part in ((2 * chunk + 1, merged), (2 * chunk, merged_other)):
                emb = call(
                    embed_kernel,
                    (1,),
                    [vmem, vmem, anywhere],
                    pl.BlockSpec((piece_rows, cols, pair_ch), at_piece(piece)),
                    emb_shape,
                    aliases={3: 0},
                )(idx, part, w_merge_out, emb)
    return (jnp.swapaxes(out, 1, 2)[None], emb)


PIECES = 4
EARLY = 3
LEAD = 1
VMEM_GRANT = 16 << 20
STEP_ROWS = 8


def takes_fused(templ_pair, main_pair):
    rows, cols = templ_pair.shape[1:3]
    row_devs, col_devs = lax.axis_size("row"), lax.axis_size("col")
    return (
        lax.axis_size("tmpl") == 4
        and col_devs == 2
        and cols == BLOCK
        and BLOCK % rows == 0
        and row_devs & (row_devs - 1) == 0
        and row_devs % col_devs == 0
        and rows * (row_devs // col_devs) == cols
        and rows % (PIECES * STEP_ROWS) == 0
    )


def on_device(*operands):
    if takes_fused(*operands[:2]):
        return fused_on_device(*operands)
    return plain_on_device(*operands)


def solution(mesh):
    in_specs = (
        P("tmpl", "row", "col", None),
        P("row", "col", None),
        P(),
        P(),
        P(),
        P(),
        P(),
        P(),
        P(),
        P(),
        P(),
        P(),
    )
    out_specs = (P("tmpl", "row", "col", None), P("row", "col", None))
    return jax.shard_map(
        on_device, mesh=mesh, in_specs=in_specs, out_specs=out_specs, check_vma=False
    )
```

```python
import functools

import jax
import jax.numpy as jnp
from jax import lax
from jax.experimental import pallas as pl
from jax.experimental.pallas import tpu as pltpu
from jax.sharding import PartitionSpec as P

BLOCK = 128


MASK_SHIFT = 10000.0
EPSILON = 1e-05
NEG_START = -1e30


def combined_all(part, axis, combine):
    gathered = jax.tree.map(lambda a: lax.all_gather(a, axis), part)

    def take(source):
        return jax.tree.map(lambda a: lax.dynamic_index_in_dim(a, source, 0, False), gathered)

    return lax.fori_loop(
        1, lax.axis_size(axis), lambda source, state: combine(state, take(source)), take(0)
    )


def layer_norm(values, scale_gain):
    values = values.astype(jnp.float32)
    center = values - jnp.mean(values, axis=-1, keepdims=True)
    spread = jnp.mean(center * center, axis=-1, keepdims=True)
    return center * lax.rsqrt(spread + EPSILON) * scale_gain


def row_group(rows_dev, cols_dev):
    chosen = 1
    for candidate in range(1, rows_dev + 1):
        if rows_dev % candidate == 0 and candidate * cols_dev <= 2048:
            chosen = candidate
    return chosen


def plain_on_device(
    templ_pair,
    main_pair,
    coverage,
    pair_mask,
    tri_gain,
    w_project,
    w_bias,
    w_tri_out,
    merge_gain,
    w_merge_q,
    w_merge_kv,
    w_merge_out,
):
    pair_tile = templ_pair[0]
    rows_dev, cols_dev, channels = pair_tile.shape
    hidden = w_tri_out.shape[0]
    head_count = w_bias.shape[1]
    head_dim = hidden // head_count
    score_scale = head_dim ** (-0.5)
    row_start = lax.axis_index("row") * rows_dev
    col_start = lax.axis_index("col") * cols_dev
    templ_index = lax.axis_index("tmpl")
    cover_tok = jnp.repeat(coverage, BLOCK, axis=1)
    own_cover = lax.dynamic_index_in_dim(cover_tok, templ_index, 0, keepdims=False)
    mask_full = jnp.repeat(jnp.repeat(pair_mask, BLOCK, axis=0), BLOCK, axis=1)
    mask_rows = lax.dynamic_slice_in_dim(mask_full, row_start, rows_dev, 0)
    cover_rows = lax.dynamic_slice_in_dim(own_cover, row_start, rows_dev, 0)
    normed = layer_norm(pair_tile, tri_gain).astype(jnp.bfloat16)
    flat_norm = normed.reshape(-1, channels)
    w_query_gate = jnp.concatenate([w_project[:, :hidden], w_project[:, 3 * hidden :]], axis=1)
    query_gate = jnp.dot(flat_norm, w_query_gate, preferred_element_type=jnp.float32).reshape(
        rows_dev, cols_dev, 2 * hidden
    )
    queries = (
        (query_gate[..., :hidden] * score_scale)
        .astype(jnp.bfloat16)
        .reshape(rows_dev, cols_dev, head_count, head_dim)
    )
    gate_values = jax.nn.sigmoid(query_gate[..., hidden:])
    bias_tile = jnp.dot(flat_norm, w_bias, preferred_element_type=jnp.float32).astype(jnp.bfloat16)
    bias_tile = jnp.transpose(bias_tile.reshape(rows_dev, cols_dev, head_count), (2, 0, 1))
    bias_column = lax.all_gather(bias_tile, "row", axis=1, tiled=True)
    bias_slab = lax.all_to_all(bias_column, "col", split_axis=1, concat_axis=2, tiled=True)
    bias_rows = jnp.transpose(bias_slab, (1, 0, 2)).astype(jnp.float32)
    key_shift = MASK_SHIFT * (
        (cover_rows[:, None] * own_cover[None, :] * mask_rows).astype(jnp.float32) - 1.0
    )
    w_key_value = w_project[:, hidden : 3 * hidden]
    group = row_group(rows_dev, cols_dev)
    splits = rows_dev // group

    def grouped(array):
        return array.reshape((splits, group) + array.shape[1:])

    start_state = (
        jnp.full((rows_dev, cols_dev, head_count), NEG_START, jnp.float32),
        jnp.zeros((rows_dev, cols_dev, head_count), jnp.float32),
        jnp.zeros((rows_dev, cols_dev, head_count, head_dim), jnp.float32),
    )
    norm_piece = lax.all_gather(normed, "col", axis=1, tiled=True)
    piece_width = norm_piece.shape[1]

    def one_group(group_args):
        query_part, norm_part, shift_part, maxima, totals, weighted = group_args
        key_value = jnp.dot(
            norm_part.reshape(-1, channels), w_key_value, preferred_element_type=jnp.float32
        ).astype(jnp.bfloat16)
        key_value = key_value.reshape(group, piece_width, 2 * hidden)
        key_part = key_value[..., :hidden].reshape(group, piece_width, head_count, head_dim)
        value_part = key_value[..., hidden:].reshape(group, piece_width, head_count, head_dim)
        scores = jnp.einsum(
            "ijhd,ikhd->ijhk", query_part, key_part, preferred_element_type=jnp.float32
        )
        scores = scores + bias_rows[None] + shift_part[:, None, None, :]
        highest = jnp.maximum(maxima, jnp.max(scores, axis=-1))
        rescale = jnp.exp(maxima - highest)
        weights = jnp.exp(scores - highest[..., None])
        totals = totals * rescale + jnp.sum(weights, axis=-1)
        summed = jnp.einsum(
            "ijhk,ikhd->ijhd",
            weights.astype(jnp.bfloat16),
            value_part,
            preferred_element_type=jnp.float32,
        )
        weighted = weighted * rescale[..., None] + summed
        return (highest, totals, weighted)

    outcome = lax.map(
        one_group,
        (
            grouped(queries),
            grouped(norm_piece),
            grouped(key_shift),
            grouped(start_state[0]),
            grouped(start_state[1]),
            grouped(start_state[2]),
        ),
    )
    result = tuple((member.reshape((rows_dev,) + member.shape[2:]) for member in outcome))
    attended = result[2] / result[1][..., None]
    gated = (attended.reshape(rows_dev, cols_dev, hidden) * gate_values).astype(jnp.bfloat16)
    projected = jnp.dot(
        gated.reshape(-1, hidden), w_tri_out, preferred_element_type=jnp.float32
    ).reshape(rows_dev, cols_dev, channels)
    new_pair = (pair_tile.astype(jnp.float32) + projected).astype(jnp.bfloat16)
    merge_norm = layer_norm(new_pair, merge_gain).astype(jnp.bfloat16)
    merge_kv = jnp.dot(
        merge_norm.reshape(-1, channels), w_merge_kv, preferred_element_type=jnp.float32
    ).astype(jnp.bfloat16)
    merge_kv = merge_kv.reshape(rows_dev, cols_dev, 2 * hidden)
    pair_ch = main_pair.shape[-1]
    main_query = (
        jnp.dot(main_pair.reshape(-1, pair_ch), w_merge_q, preferred_element_type=jnp.float32)
        * score_scale
    )
    main_query = main_query.reshape(rows_dev, cols_dev, head_count, head_dim)
    mask_tile = lax.dynamic_slice_in_dim(mask_rows, col_start, cols_dev, 1)
    own_cols = lax.dynamic_slice_in_dim(own_cover, col_start, cols_dev, 0)
    own_valid = cover_rows[:, None] * own_cols[None, :] * mask_tile
    shift_bias = MASK_SHIFT * (own_valid.astype(jnp.float32) - 1.0)
    keys_own = (
        merge_kv[..., :hidden].astype(jnp.float32).reshape(rows_dev, cols_dev, head_count, head_dim)
    )
    values_own = (
        merge_kv[..., hidden:].astype(jnp.float32).reshape(rows_dev, cols_dev, head_count, head_dim)
    )
    scores = jnp.sum(main_query * keys_own, axis=-1) + shift_bias[..., None]

    def combine(earlier, later):
        highest = jnp.maximum(earlier[0], later[0])
        early_scale = jnp.exp(earlier[0] - highest)
        late_scale = jnp.exp(later[0] - highest)
        return (
            highest,
            earlier[1] * early_scale + later[1] * late_scale,
            earlier[2] * early_scale[..., None] + later[2] * late_scale[..., None],
        )

    merged_state = combined_all((scores, jnp.ones_like(scores), values_own), "tmpl", combine)
    merged = merged_state[2] / merged_state[1][..., None]
    merged = merged.reshape(-1, hidden).astype(jnp.bfloat16)
    embedding = jnp.dot(merged, w_merge_out, preferred_element_type=jnp.float32).astype(
        jnp.bfloat16
    )
    return (new_pair[None], embedding.reshape(rows_dev, cols_dev, pair_ch))


LOG2E = 1.4426950408889634


def normed_rows(values, gain):
    center = values - jnp.mean(values, axis=0, keepdims=True)
    spread = jnp.mean(center * center, axis=0, keepdims=True)
    return (center * lax.rsqrt(spread + EPSILON) * gain).astype(jnp.bfloat16)


def places(rows):
    templ, row_dev, col_dev = (lax.axis_index(axis) for axis in ("tmpl", "row", "col"))
    return lax.rem(templ, 2), templ, row_dev, col_dev, row_dev * rows // BLOCK


def piece_of(piece, idx_ref, pieces):
    half = idx_ref[0]
    odd = lax.rem(piece, 2)
    side = odd * half + (1 - odd) * (1 - half)
    return side * (pieces // 2) + piece // 2


def mask_shift(cover_ref, mask_ref, templ, row_block, col_block):
    valid = (
        cover_ref[row_block, templ] * cover_ref[col_block, templ] * mask_ref[row_block, col_block]
    )
    return MASK_SHIFT * (valid.astype(jnp.float32) - 1.0)


def matmul(lhs, rhs, lhs_dim=1, rhs_dim=0):
    return lax.dot_general(
        lhs, rhs, (((lhs_dim,), (rhs_dim,)), ((), ())), preferred_element_type=jnp.float32
    )


def widened(row_ref, cols):
    return jnp.broadcast_to(row_ref[...], (cols, row_ref.shape[1])).T


def norm_kernel(heads, x_hbm, gain_hbm, bias_w_hbm, *refs):
    *kept_refs, bias_ref, held, wide, x_ref, gain_ref, bias_w_ref, done = refs
    norm_refs, raw_refs = kept_refs[::2], kept_refs[1::2]
    pieces, step_rows, _, cols = x_ref.shape
    idx_ref = places(pieces * step_rows)
    small = [
        pltpu.make_async_copy(gain_hbm, gain_ref, done.at[pieces]),
        pltpu.make_async_copy(bias_w_hbm, bias_w_ref, done.at[pieces + 1]),
    ]
    firsts = [
        pl.multiple_of(piece_of(piece, idx_ref, pieces) * step_rows, step_rows)
        for piece in range(pieces)
    ]
    copies = [
        pltpu.make_async_copy(x_hbm.at[pl.ds(first, step_rows)], x_ref.at[piece], done.at[piece])
        for piece, first in enumerate(firsts)
    ]
    for copy in small + copies:
        copy.start()
    for copy in small:
        copy.wait()
    wide[...] = widened(gain_ref, cols)
    for piece in range(pieces):
        copies[piece].wait()
        base = piece % 2 * step_rows
        norm_ref, raw_ref = norm_refs[piece // 2], raw_refs[piece // 2]
        for i in range(step_rows):
            raw_ref[base + i] = x_ref[piece, i]
            norm_ref[base + i] = normed_rows(x_ref[piece, i].astype(jnp.float32), wide[...])
        wide_norm = jnp.concatenate([norm_ref[base + i] for i in range(step_rows)], axis=1)
        wide_bias = matmul(bias_w_ref[...], wide_norm)
        for i in range(step_rows):
            for head in range(heads):
                held[piece, head, i : i + 1, :] = wide_bias[
                    head : head + 1, i * cols : (i + 1) * cols
                ]
        bias_ref[:, pl.ds(firsts[piece], step_rows), :] = held[piece].astype(jnp.bfloat16)


def weight_kernel(
    heads, idx_ref, project_ref, tri_out_ref, kv_ref, gain_ref, cover_ref, mask_ref, pack_ref, wide_ref, table_ref
):
    for line, shift in enumerate(all_shifts(idx_ref, cover_ref, mask_ref)):
        table_ref[line : line + 1, :] = jnp.full((1, table_ref.shape[1]), shift, jnp.float32)
    wide_ref[...] = widened(gain_ref, wide_ref.shape[1])
    channels = project_ref.shape[0]
    hidden = tri_out_ref.shape[0]
    dim = hidden // heads
    scale = dim ** (-0.5) * LOG2E
    project = project_ref[...]
    for head in range(heads):
        query = project[:, head * dim : (head + 1) * dim]
        key = project[:, hidden + head * dim : hidden + (head + 1) * dim]
        pack_ref[head * channels : (head + 1) * channels, :] = (
            matmul(key, query, 1, 1) * scale
        ).astype(jnp.bfloat16)
    row = heads * channels
    rest = (
        project[:, 3 * hidden :],
        project[:, 2 * hidden : 3 * hidden],
        tri_out_ref[...],
        kv_ref[...],
    )
    for part in rest:
        flipped = part.astype(jnp.float32).T.astype(jnp.bfloat16)
        pack_ref[row : row + flipped.shape[0], :] = flipped
        row += flipped.shape[0]


def when_held(idx_ref, column, part, tile_refs, tiles_per_col, act):
    wanted = idx_ref[2] ^ (tiles_per_col * column + part)
    for turn, tile_ref in enumerate(tile_refs):

        @pl.when(wanted == turn)
        def _():
            act(tile_ref)


def pick_kernel(*refs):
    *tile_refs, _, _, out_ref = refs
    idx_ref = places(tile_refs[0].shape[1])
    for part in range(out_ref.shape[0]):

        def act(tile_ref, part=part):
            out_ref[part] = tile_ref[...]

        when_held(idx_ref, 1 - idx_ref[3], part, tile_refs, out_ref.shape[0], act)


def relative_shift(idx_ref, cover_ref, mask_ref, block):
    shifts = [mask_shift(cover_ref, mask_ref, idx_ref[1], idx_ref[4], b) for b in (block, 1 - block)]
    return shifts[0] - jnp.maximum(*shifts)


def all_shifts(idx_ref, cover_ref, mask_ref):
    own, other, best, far_best = pair_shifts(idx_ref, cover_ref, mask_ref)
    top = jnp.maximum(best, far_best)
    blocks = (idx_ref[3], 1 - idx_ref[3])
    return [relative_shift(idx_ref, cover_ref, mask_ref, block) for block in blocks] + [
        own,
        other,
        best - top,
        far_best - top,
    ]


def place_bias(out_ref, part, tile, shift):
    heads, tile_rows, _ = tile.shape
    for head in range(heads):
        flipped = tile[head].astype(jnp.float32).T
        out_ref[head, :, part * tile_rows : (part + 1) * tile_rows] = (flipped + shift) * LOG2E


def own_bias_kernel(table_ref, *refs):
    *tile_refs, _, out_ref = refs
    idx_ref = places(tile_refs[0].shape[1])
    tiles_per_col = out_ref.shape[2] // tile_refs[0].shape[1]
    shift = table_ref[0:1, : tile_refs[0].shape[1]]
    for part in range(tiles_per_col):

        def act(tile_ref, part=part):
            place_bias(out_ref, part, tile_ref[...], shift)

        when_held(idx_ref, idx_ref[3], part, tile_refs, tiles_per_col, act)


def far_bias_kernel(table_ref, tiles_ref, _, out_ref):
    shift = table_ref[1:2, : tiles_ref.shape[2]]
    for part in range(tiles_ref.shape[0]):
        place_bias(out_ref, part, tiles_ref[part], shift)


def query_kernel(scale, idx_ref, main_ref, w_ref, out_ref):
    step_rows, cols, pair_ch = main_ref.shape
    base = pl.program_id(0) * step_rows
    wide = matmul(w_ref[...], main_ref[...].reshape(step_rows * cols, pair_ch), 1, 1) * scale
    for i in range(step_rows):
        out_ref[base + i] = wide[:, i * cols : (i + 1) * cols]


def split_pack(pack_ref, heads, hidden):
    channels = pack_ref.shape[1]
    ends = [heads * channels]
    for size in (hidden, hidden, channels):
        ends.append(ends[-1] + size)
    return ends


def near_kernel(
    heads, skip, own_ref, own_bias_ref, pack_ref, after_ref, probes, gates, own_mix, near, near_tops, turned
):
    step_rows, _, channels, _ = probes.shape
    ends = split_pack(pack_ref, heads, gates.shape[1])
    for i in range(step_rows):
        own = own_ref[skip + i]
        first = matmul(pack_ref[: ends[2], :], own)
        for h in range(heads):
            probes[i, h] = first[h * channels : (h + 1) * channels, :].astype(jnp.bfloat16)
        gates[i] = jax.nn.sigmoid(first[ends[0] : ends[1], :])
        own_mix[i] = first[ends[1] :, :].astype(jnp.bfloat16)
        turned[i] = own.T
    for i in range(step_rows):
        for h in range(heads):
            scores = matmul(turned[i], probes[i, h]) + own_bias_ref[h]
            near[i, h] = scores
            near_tops[i, h] = jnp.broadcast_to(
                jnp.max(scores, axis=0, keepdims=True), near_tops.shape[2:]
            )


def late_kernel(
    heads,
    skip,
    query_skip,
    x_ref,
    far_ref,
    main_query,
    far_bias_ref,
    pack_ref,
    gain_ref,
    probes,
    gates,
    own_mix,
    near,
    near_tops,
    after_ref,
    out_ref,
    state_ref,
    turned,
    mixers,
    held,
    tops,
    gated,
):
    step_rows, _, cols = out_ref.shape
    hidden = main_query.shape[1]
    dim = hidden // heads
    ends = split_pack(pack_ref, heads, hidden)
    value_w = pack_ref[ends[1] : ends[2], :]
    for i in range(step_rows):
        far = far_ref[skip + i]
        values = matmul(value_w, far).astype(jnp.bfloat16)
        for h in range(heads):
            span = slice(h * dim, (h + 1) * dim)
            mixers[i, h, :dim, :cols] = own_mix[i, span, :]
            mixers[i, h, :dim, cols:] = values[span, :]
            mixers[i, h, dim:, :] = jnp.ones((mixers.shape[2] - dim, 2 * cols), jnp.bfloat16)
        turned[i] = far.T

    slots = held.shape[0]

    def score_row(i, h):
        scores = matmul(turned[i], probes[i, h]) + far_bias_ref[h]
        held[i % slots, h] = scores
        highest = jnp.max(scores, axis=0, keepdims=True)
        tops[i % slots, h] = jnp.maximum(near_tops[i, h], highest)

    def mix_row(i, h):
        top = tops[i % slots, h][:1]
        weights = jnp.concatenate(
            [
                jnp.exp2(part - top).astype(jnp.bfloat16)
                for part in (near[i, h], held[i % slots, h])
            ],
            axis=0,
        )
        mixed = matmul(mixers[i, h], weights)
        span = slice(h * dim, (h + 1) * dim)
        gated[i, span, :] = (
            mixed[:dim] * (1.0 / mixed[dim : dim + 1]) * gates[i, span, :]
        ).astype(jnp.bfloat16)

    for unit in range(heads * step_rows + LEAD):
        if unit < heads * step_rows:
            score_row(*divmod(unit, heads))
        if unit >= LEAD:
            mix_row(*divmod(unit - LEAD, heads))
    write_rows(
        heads, skip, query_skip, x_ref, main_query, pack_ref, gain_ref, gated, out_ref, state_ref
    )


def write_rows(
    heads, skip, query_skip, x_ref, main_query, pack_ref, gain_ref, gated, out_ref, state_ref
):
    step_rows = out_ref.shape[0]
    hidden = gated.shape[1]
    dim = hidden // heads
    ends = split_pack(pack_ref, heads, hidden)
    tri_w = pack_ref[ends[2] : ends[3], :]
    kv_w = pack_ref[ends[3] :, :]
    for i in range(step_rows):
        fresh = x_ref[skip + i].astype(jnp.float32) + matmul(tri_w, gated[i])
        out_ref[i] = fresh.astype(jnp.bfloat16)
    for i in range(step_rows):
        merge_norm = normed_rows(out_ref[i].astype(jnp.float32), gain_ref[...])
        merge_kv = matmul(kv_w, merge_norm).astype(jnp.bfloat16)
        product = main_query[query_skip + i] * merge_kv[:hidden, :].astype(jnp.float32)
        score = jnp.concatenate(
            [
                jnp.sum(product[h * dim : (h + 1) * dim, :], axis=0, keepdims=True)
                for h in range(heads)
            ],
            axis=0,
        )
        store_state(state_ref, i, merge_kv[hidden:, :], score)


def store_state(state_ref, i, values, score):
    hidden = values.shape[0]
    high = score.astype(jnp.bfloat16)
    low = (score - high.astype(jnp.float32)).astype(jnp.bfloat16)
    state_ref[i, :hidden, :] = values
    state_ref[i, hidden:, :] = jnp.concatenate([high, low], axis=0)


def spread_heads(per_head, dim):
    heads, cols = per_head.shape
    return jnp.concatenate(
        [jnp.broadcast_to(per_head[h : h + 1, :], (dim, cols)) for h in range(heads)], axis=0
    )


def joined(heads, first_ref, second_ref, i, first_shift, second_shift):
    hidden = first_ref.shape[1] - 2 * heads

    def parts(ref, shift):
        extra = ref[i, hidden:, :].astype(jnp.float32)
        return ref[i, :hidden, :].astype(jnp.float32), extra[:heads] + extra[heads:] + shift

    first_values, first_score = parts(first_ref, first_shift)
    second_values, second_score = parts(second_ref, second_shift)
    highest = jnp.maximum(first_score, second_score)
    first_weight = jnp.exp(first_score - highest)
    second_weight = jnp.exp(second_score - highest)
    total = first_weight + second_weight
    inverse = 1.0 / total
    dim = hidden // heads
    values = first_values * spread_heads(first_weight * inverse, dim)
    values = values + second_values * spread_heads(second_weight * inverse, dim)
    return values, highest + jnp.log(total)


def pair_shifts(idx_ref, cover_ref, mask_ref):
    templ, col_dev, row_block = idx_ref[1], idx_ref[3], idx_ref[4]
    even = templ - lax.rem(templ, 2)
    own = mask_shift(cover_ref, mask_ref, templ, row_block, col_dev)
    other = mask_shift(cover_ref, mask_ref, 2 * even + 1 - templ, row_block, col_dev)
    far = 2 - even
    far_best = jnp.maximum(
        mask_shift(cover_ref, mask_ref, far, row_block, col_dev),
        mask_shift(cover_ref, mask_ref, far + 1, row_block, col_dev),
    )
    best = jnp.maximum(own, other)
    return own - best, other - best, best, far_best


def core_join_kernel(heads, table_ref, own_ref, other_ref, state_ref):
    own_shift, other_shift = table_ref[2:3, :], table_ref[3:4, :]
    for i in range(own_ref.shape[0]):
        values, score = joined(heads, own_ref, other_ref, i, own_shift, other_shift)
        store_state(state_ref, i, values.astype(jnp.bfloat16), score)


def chip_join_kernel(heads, table_ref, own_ref, other_ref, _, merged_ref):
    own_shift, other_shift = table_ref[4:5, :], table_ref[5:6, :]
    for i in range(own_ref.shape[0]):
        values, _ = joined(heads, own_ref, other_ref, i, own_shift, other_shift)
        merged_ref[i] = values.astype(jnp.bfloat16)


def embed_rows(merged_ref, w_ref, out_ref):
    for i in range(merged_ref.shape[0]):
        out_ref[i] = matmul(merged_ref[i], w_ref[...], 0, 0).astype(jnp.bfloat16)


def embed_kernel(piece, pieces, merged_ref, w_ref, prior_ref, out_hbm, rows_ref, done):
    step_rows = merged_ref.shape[0]
    groups = done.shape[0]
    size = step_rows // groups
    first = piece_of(piece, places(step_rows * pieces), pieces) * step_rows
    copies = []
    for group in range(groups):
        span = pl.ds(group * size, size)
        embed_rows(merged_ref.at[span], w_ref, rows_ref.at[span])
        target = out_hbm.at[pl.ds(pl.multiple_of(first + group * size, size), size)]
        copies.append(pltpu.make_async_copy(rows_ref.at[span], target, done.at[group]))
        copies[-1].start()
    for copy in copies:
        copy.wait()


def finish_kernel(idx_ref, *refs):
    *row_refs, other_ref, own_ref, w_ref, fresh_ref, out_ref, token_ref = refs
    token_ref[...] = jnp.zeros_like(token_ref)
    for piece, row_ref in enumerate(row_refs):

        @pl.when(pl.program_id(0) == piece)
        def _():
            fresh_ref[...] = row_ref[...]
            if piece < 2:
                embed_rows((other_ref, own_ref)[piece], w_ref, out_ref)


def fused_on_device(
    templ_pair, main_pair, coverage, pair_mask, tri_gain, w_project, w_bias, w_tri_out,
    merge_gain, w_merge_q, w_merge_kv, w_merge_out,
):
    rows, cols, channels = templ_pair.shape[1:]
    hidden = w_tri_out.shape[0]
    heads = w_bias.shape[1]
    dim = hidden // heads
    pair_ch = main_pair.shape[-1]
    row_devs, col_devs = lax.axis_size("row"), lax.axis_size("col")
    tiles_per_col = row_devs // col_devs
    templ, row_dev, col_dev = (lax.axis_index(a) for a in ("tmpl", "row", "col"))
    idx = jnp.stack([templ % 2, templ, row_dev, col_dev, (row_dev * rows) // BLOCK]).astype(jnp.int32)
    pieces = PIECES
    piece_rows = rows // pieces
    stored = jnp.swapaxes(templ_pair[0], 1, 2)
    bf16, f32 = jnp.bfloat16, jnp.float32

    def in_hbm(array):
        return pltpu.with_memory_space_constraint(array, pltpu.HBM)

    gain_row = in_hbm(tri_gain[None, :])
    cover = coverage.T
    stored, main_pair = in_hbm(stored), in_hbm(main_pair)

    def whole(array):
        return pl.BlockSpec(array.shape, lambda *_: (0,) * array.ndim)

    smem = pl.BlockSpec(memory_space=pltpu.SMEM)
    vmem = pl.BlockSpec(memory_space=pltpu.VMEM)
    anywhere = pl.BlockSpec(memory_space=pl.ANY)

    def call(kernel, grid, in_specs, out_specs, out_shape, scratch=(), aliases=None, cost=1e6):
        return pl.pallas_call(
            kernel,
            grid_spec=pltpu.PrefetchScalarGridSpec(
                num_scalar_prefetch=1, grid=grid, in_specs=in_specs, out_specs=out_specs,
                scratch_shapes=list(scratch),
            ),
            out_shape=out_shape,
            input_output_aliases=aliases or {},
            cost_estimate=pl.CostEstimate(
                flops=int(cost), bytes_accessed=1 << 20, transcendentals=0
            ),
            compiler_params=pltpu.CompilerParams(vmem_limit_bytes=VMEM_GRANT),
        )

    chunks = pieces // 2

    def plain_call(kernel, in_specs, out_shape, scratch=(), cost=1e6):
        return pl.pallas_call(
            kernel,
            in_specs=in_specs,
            out_specs=jax.tree.map(lambda _: vmem, out_shape),
            out_shape=out_shape,
            scratch_shapes=list(scratch),
            cost_estimate=pl.CostEstimate(
                flops=int(cost), bytes_accessed=1 << 20, transcendentals=0
            ),
            compiler_params=pltpu.CompilerParams(vmem_limit_bytes=VMEM_GRANT),
        )

    hbm = pl.BlockSpec(memory_space=pltpu.HBM)
    flat_bias_w = in_hbm(w_bias.T)
    *kept_rows, bias_tile = plain_call(
        functools.partial(norm_kernel, heads),
        [hbm, hbm, hbm],
        [jax.ShapeDtypeStruct((2 * piece_rows, channels, cols), bf16)] * (2 * chunks)
        + [jax.ShapeDtypeStruct((heads, rows, cols), bf16)],
        [
            pltpu.VMEM((pieces, heads, piece_rows, cols), f32),
            pltpu.VMEM((channels, cols), f32),
            pltpu.VMEM((pieces, piece_rows, channels, cols), bf16),
            pltpu.VMEM((1, channels), f32),
            pltpu.VMEM(flat_bias_w.shape, bf16),
            pltpu.SemaphoreType.DMA((pieces + 2,)),
        ],
    )(stored, gain_row, flat_bias_w)
    norms, raws = kept_rows[::2], kept_rows[1::2]


    tiles = [bias_tile]
    for turn in range(1, row_devs):
        perm = [(z, z ^ turn) for z in range(row_devs)]
        tiles.append(lax.ppermute(bias_tile, "row", perm))
    swap = [(c, col_devs - 1 - c) for c in range(col_devs)]
    fars = [lax.ppermute(norms[0], "col", swap)]
    pack_shape = (heads * channels + 2 * hidden + channels + 2 * hidden, channels)
    raw_weights = [in_hbm(w) for w in (w_project, w_tri_out, w_merge_kv, merge_gain[None, :])]
    packed_shapes = [
        jax.ShapeDtypeStruct(pack_shape, bf16),
        jax.ShapeDtypeStruct((channels, cols), f32),
        jax.ShapeDtypeStruct((8, cols), f32),
    ]
    pack, merge_gain_wide, table = call(
        functools.partial(weight_kernel, heads),
        (1,),
        [whole(w) for w in raw_weights] + [smem] * 2,
        [vmem] * len(packed_shapes),
        packed_shapes,
    )(idx, *raw_weights, cover, pair_mask)
    query_w = in_hbm(w_merge_q.T)
    query_w = in_hbm(w_merge_q.T)
    main_query = call(
        functools.partial(query_kernel, dim ** (-0.5)),
        (pieces,),
        [
            pl.BlockSpec((piece_rows, cols, pair_ch), lambda g, s: (piece_of(g, s, pieces), 0, 0)),
            whole(query_w),
        ],
        vmem,
        jax.ShapeDtypeStruct((rows, hidden, cols), f32),
    )(idx, main_pair, query_w)
    picked = plain_call(
        pick_kernel,
        [vmem] * row_devs + [anywhere] * 2,
        jax.ShapeDtypeStruct((tiles_per_col,) + bias_tile.shape, bf16),
    )(*tiles, pack, main_query)
    far_tiles = lax.ppermute(picked, "col", swap)
    half_shape = jax.ShapeDtypeStruct((heads, cols, cols), f32)
    own_bias = plain_call(own_bias_kernel, [vmem] * (row_devs + 1) + [anywhere], half_shape)(
        table, *tiles, picked
    )
    after = own_bias
    nears = []
    near_shapes = [
        jax.ShapeDtypeStruct((piece_rows,) + shape, dtype)
        for shape, dtype in (
            ((heads, channels, cols), bf16),
            ((hidden, cols), f32),
            ((hidden, cols), bf16),
            ((heads, cols, cols), f32),
            ((heads, 8, cols), f32),
        )
    ]

    def near_part(after):
        piece = len(nears)
        nears.append(
            plain_call(
                functools.partial(near_kernel, heads, piece % 2 * piece_rows),
                [vmem] * 3 + [anywhere],
                near_shapes,
                [pltpu.VMEM((piece_rows, cols, channels), bf16)],
                2e9,
            )(norms[piece // 2], own_bias, pack, after)
        )
        return nears[-1][-1]

    while len(nears) < EARLY:
        after = near_part(after)
    far_bias = plain_call(far_bias_kernel, [vmem, vmem, anywhere], half_shape)(
        table, far_tiles, after
    )
    held_back = lax.optimization_barrier((norms[1:], picked))[0]
    fars += [lax.ppermute(norm, "col", swap) for norm in held_back]

    fresh, states, pair_states = [], [], []
    after = far_bias
    cores = [(t, t + 1 - 2 * (t % 2)) for t in range(lax.axis_size("tmpl"))]
    chips = [(t, (t + 2) % 4) for t in range(lax.axis_size("tmpl"))]
    state_shape = jax.ShapeDtypeStruct((piece_rows, hidden + 2 * heads, cols), bf16)
    for piece in range(pieces):
        chunk, side = piece // 2, piece % 2
        if len(nears) == piece:
            after = near_part(after)
        rows_out, state = plain_call(
            functools.partial(late_kernel, heads, side * piece_rows, piece * piece_rows),
            [vmem] * 11 + [anywhere],
            [jax.ShapeDtypeStruct((piece_rows, channels, cols), bf16), state_shape],
            [
                pltpu.VMEM((piece_rows, cols, channels), bf16),
                pltpu.VMEM((piece_rows, heads, 2 * dim, col_devs * cols), bf16),
                pltpu.VMEM((2, heads, cols, cols), f32),
                pltpu.VMEM((2, heads, 8, cols), f32),
                pltpu.VMEM((piece_rows, hidden, cols), bf16),
            ],
            6e9,
        )(
            raws[chunk], fars[chunk], main_query, far_bias, pack, merge_gain_wide,
            *nears[piece], after,
        )
        fresh.append(rows_out)
        states.append(state)
        after = state
        if side:
            after = plain_call(
                functools.partial(core_join_kernel, heads),
                [vmem] * 3,
                state_shape,
            )(table, state, swapped)
            pair_states.append(after)
            if len(nears) < pieces:
                after = near_part(after)
        else:
            swapped = lax.ppermute(state, "tmpl", cores)

    emb_shape = jax.ShapeDtypeStruct(main_pair.shape, bf16)
    token = pair_states[-1]
    token_shape = jax.ShapeDtypeStruct((8, cols), f32)
    merged_shape = jax.ShapeDtypeStruct((piece_rows, hidden, cols), bf16)
    for chunk in range(chunks):
        pair_state = pair_states[chunk]
        far_state = lax.ppermute(pair_state, "tmpl", chips)
        merged = plain_call(
            functools.partial(chip_join_kernel, heads),
            [vmem] * 3 + [anywhere],
            merged_shape,
        )(table, pair_state, far_state, token)
        merged_other = lax.ppermute(merged, "tmpl", cores)

        if chunk == 0:
            out, emb, token = call(
                finish_kernel,
                (pieces,),
                [vmem] * (pieces + 3),
                [
                    pl.BlockSpec(
                        (piece_rows, channels, cols),
                        lambda g, s: (piece_of(g, s, pieces), 0, 0),
                    ),
                    pl.BlockSpec(
                        (piece_rows, cols, pair_ch),
                        lambda g, s: (piece_of(jnp.minimum(g, 1), s, pieces), 0, 0),
                    ),
                    vmem,
                ],
                [jax.ShapeDtypeStruct(stored.shape, bf16), emb_shape, token_shape],
            )(idx, *fresh, merged_other, merged, w_merge_out)
        else:
            for piece, part in ((2 * chunk + 1, merged), (2 * chunk, merged_other)):
                emb = pl.pallas_call(
                    functools.partial(embed_kernel, piece, pieces),
                    in_specs=[vmem, vmem, hbm],
                    out_specs=hbm,
                    out_shape=emb_shape,
                    scratch_shapes=[
                        pltpu.VMEM((piece_rows, cols, pair_ch), bf16),
                        pltpu.SemaphoreType.DMA((2,)),
                    ],
                    input_output_aliases={2: 0},
                    compiler_params=pltpu.CompilerParams(vmem_limit_bytes=VMEM_GRANT),
                )(part, w_merge_out, emb)
    return (jnp.swapaxes(out, 1, 2)[None], emb)


PIECES = 4
EARLY = 3
LEAD = 1
VMEM_GRANT = 16 << 20
STEP_ROWS = 8


def takes_fused(templ_pair, main_pair):
    rows, cols = templ_pair.shape[1:3]
    row_devs, col_devs = lax.axis_size("row"), lax.axis_size("col")
    return (
        lax.axis_size("tmpl") == 4
        and col_devs == 2
        and cols == BLOCK
        and BLOCK % rows == 0
        and row_devs & (row_devs - 1) == 0
        and row_devs % col_devs == 0
        and rows * (row_devs // col_devs) == cols
        and rows % (PIECES * STEP_ROWS) == 0
    )


def on_device(*operands):
    if takes_fused(*operands[:2]):
        return fused_on_device(*operands)
    return plain_on_device(*operands)


def solution(mesh):
    in_specs = (
        P("tmpl", "row", "col", None),
        P("row", "col", None),
        P(),
        P(),
        P(),
        P(),
        P(),
        P(),
        P(),
        P(),
        P(),
        P(),
    )
    out_specs = (P("tmpl", "row", "col", None), P("row", "col", None))
    return jax.shard_map(
        on_device, mesh=mesh, in_specs=in_specs, out_specs=out_specs, check_vma=False
    )
```
